32 devices in a mesh: cell: 8 (over z, core), energy: 4 (over y, x).
Axes of the slice: x: 2, y: 2, z: 4, core: 2. Of those that a mesh axis runs over, the one named last changes fastest.
Arguments:
- modes: bfloat16 [8, 256, 256], P('cell'), may hold values from -0.375 to 0.375
- levels: float32 [8, 256], P('cell'), may hold values from -0.25 to 0.25
- level_shift: float32 [8, 8, 256], P('cell', 'energy'), may hold values from -0.25 to 0.25
- broadening: float32 [8, 8, 256], P('cell', 'energy'), may hold values from 0.02 to 0.3
- injection: float32 [8, 8, 256], P('cell', 'energy'), may hold values from 0.1 to 1
- coupling: bfloat16 [8, 256, 64], P('cell'), may hold values from -0.625 to 0.625
- row_mask: int32 [8, 4], P('cell'), may hold values 0 or 1
- interface: int32 [8], P('cell'), may hold values from 0 to 3
- screened: bfloat16 [8, 2, 8, 256, 256], P('cell', None, None, 'energy'), may hold values from -18 to 18
- offsets: int32 [8], replicated, may hold values from -2 to 2, as said below
Outputs:
- density: float32 [8, 8, 256], P('cell', 'energy')
- sigma_lesser: bfloat16 [8, 2, 8, 256, 256], P('cell', None, None, 'energy')
The draws below stay inside these ranges and needn't reach their ends.
Inputs may be any that keep to these rules, and one draw needn't show every extreme that they name: interface[i] names one of the 4 blocks of 64 orbitals of cell i - 1. `offsets`: both ends of the range are taken.
All inputs are finite; a program needn't handle non-finite values. No bound on the sum of `row_mask` on one device may be relied on, other than what follows from the above.
Results may differ from the reference program's by a relative error of at most 0.014.
Values may be sent and summed in bfloat16 or wider, within the bound.
No kernel may reach another device: no remote copies, remote signals or barrier semaphores. Data moves between devices by JAX's collectives and lax.ppermute only.
A program may use at most 128 MiB of HBM per device.

```python
import math
from functools import partial
import jax
import jax.numpy as jnp
from jax import lax

B = 256
BLK = 64
K = 8
NB = 4
NC = 8
NE = 8
SHIFT_MAX = 2


def draw_offsets(key, part):
    first_key = jax.random.fold_in(key, 11)
    second_key = jax.random.fold_in(key, 12)
    middle = jax.random.randint(first_key, (K - 2,), -SHIFT_MAX, SHIFT_MAX + 1)
    ends = jnp.array([SHIFT_MAX, -SHIFT_MAX], dtype=jnp.int32)
    joined = jnp.concatenate([ends, middle.astype(jnp.int32)])
    shuffle_order = jax.random.permutation(second_key, K)
    return joined[shuffle_order]


def with_ends(values, rng, smallest, high):
    index_at = [jax.random.randint(jax.random.fold_in(rng, axis), (), 0, length) for axis, length in enumerate(values.shape)]
    widest = values.shape.index(max(values.shape))
    next_to = index_at[:widest] + [(index_at[widest] + 1) % values.shape[widest]] + index_at[widest + 1:]
    return values.at[tuple(index_at)].set(smallest).at[tuple(next_to)].set(high)


def steps_of(rng, shape, cuts, least, high):
    level, own = 1.0, jax.random.fold_in(rng, 6)
    for dim, shards_of in cuts:
        steps = jnp.exp(jax.random.uniform(jax.random.fold_in(own, dim), (shards_of,), jnp.float32, least / len(cuts), high / len(cuts)))
        level = level * jnp.repeat(steps, shape[dim] // shards_of).reshape([-1 if axis == dim else 1 for axis in range(len(shape))])
    return level


def noise(key, shape, width, reach, pieces=(), kind=jnp.bfloat16):
    values = width * jax.random.normal(key, shape, jnp.float32)
    if pieces:
        values = values * steps_of(key, shape, pieces, -0.22, 0.18)
    return jnp.clip(values, -reach, reach).astype(kind)


def setup_inputs(seed: int = 0) -> dict:
    key_of = jax.random.split(jax.random.key(seed), 11)
    return {
        "modes": noise(key_of[0], (NC, B, B), B ** -0.5, 0.375, ((0, 8),)),
        "levels": jnp.clip(jax.random.uniform(key_of[1], (NC, B), jnp.float32, -0.25, 0.25) * steps_of(key_of[1], (NC, B), ((0, 8),), -0.4, 0.0), -0.25, 0.25),
        "level_shift": jnp.clip(jax.random.uniform(key_of[2], (NC, NE, B), jnp.float32, -0.25, 0.25) * steps_of(key_of[2], (NC, NE, B), ((0, 8), (1, 4)), -0.4, 0.0), -0.25, 0.25),
        "broadening": jnp.clip(jnp.exp(math.log(0.3) - 2.7080503 * jax.random.uniform(key_of[3], (NC, NE, B), jnp.float32) ** steps_of(key_of[3], (NC, NE, B), ((0, 8), (1, 4)), -0.2, 0.2)), 0.02, 0.3),
        "injection": jnp.clip(jnp.exp(math.log(1.0) - 2.3025851 * jax.random.uniform(key_of[4], (NC, NE, B), jnp.float32) ** steps_of(key_of[4], (NC, NE, B), ((0, 8), (1, 4)), -0.2, 0.2)), 0.1, 1.0),
        "coupling": noise(key_of[5], (NC, B, BLK), (5 * BLK // 4) ** -0.5, 0.625, ((0, 8),)),
        "row_mask": with_ends((jax.random.randint(key_of[6], (NC, NB), 0, 4) < 3).astype(jnp.int32), jax.random.fold_in(key_of[6], 1), 0, 1),
        "interface": with_ends(jax.random.randint(key_of[7], (NC,), 0, NB), jax.random.fold_in(key_of[7], 1), 0, NB - 1).astype(jnp.int32),
        "screened": noise(key_of[8], (NC, 2, K, B, B), 3.0, 18.0, ((0, 8), (3, 4))),
        "offsets": draw_offsets(jax.random.fold_in(key_of[10], 71), 0),
    }


broaden_base = 1.0
energy_low = -0.25
energy_span = 0.5
highest = lax.Precision.HIGHEST

def complex_product(left_re, left_im, right_re, right_im):
    einsum_high = partial(jnp.einsum, 'eij,ejk->eik', precision=highest)
    return (einsum_high(left_re, right_re) - einsum_high(left_im, right_im), einsum_high(left_re, right_im) + einsum_high(left_im, right_re))

def complex_adjoint(left_re, left_im, right_re, right_im):
    einsum_high = partial(jnp.einsum, 'eik,ejk->eij', precision=highest)
    return (einsum_high(left_re, right_re) + einsum_high(left_im, right_im), einsum_high(left_im, right_re) - einsum_high(left_re, right_im))

def block_of(values, chosen, extent, axis_dim):
    return lax.dynamic_slice_in_dim(values, (chosen * extent).astype(jnp.int32), extent, axis_dim)

def convolve(lesser, screen, offsets):
    overall = lesser.shape[-3]
    ndims = lesser.ndim
    widths = [(0, 0)] * (ndims - 3) + [(overall, overall), (0, 0), (0, 0)]
    padded = jnp.pad(lesser, widths)
    accum_re = jnp.zeros(lesser[..., 0, :, :, :].shape, jnp.float32)
    accum_im = jnp.zeros(lesser[..., 0, :, :, :].shape, jnp.float32)
    for position in range(screen.shape[-3]):
        start_row = (overall - offsets[position]).astype(jnp.int32)
        shifted = lax.dynamic_slice_in_dim(padded, start_row, overall, ndims - 3)
        shifted_re = shifted[..., 0, :, :, :].astype(jnp.float32)
        shifted_im = shifted[..., 1, :, :, :].astype(jnp.float32)
        screen_re = screen[..., 0, position, :, :][..., None, :, :].astype(jnp.float32)
        screen_im = screen[..., 1, position, :, :][..., None, :, :].astype(jnp.float32)
        accum_re = accum_re - (screen_re * shifted_im + screen_im * shifted_re)
        accum_im = accum_im + (screen_re * shifted_re - screen_im * shifted_im)
    return jnp.stack([accum_re, accum_im], axis=ndims - 4).astype(jnp.bfloat16)

def reference(modes, levels, level_shift, broadening, injection, coupling, row_mask, interface, screened, offsets):
    energy_grid = energy_low + energy_span * (jnp.arange(NE).astype(jnp.float32) + 0.5) / NE
    following = jnp.concatenate([interface[1:], jnp.zeros((1,), jnp.int32)])
    zero_block = jnp.zeros((NE, BLK, BLK), jnp.float32)

    def as_float(values):
        return values.astype(jnp.float32)

    def halved(values):
        return as_float(values.astype(jnp.bfloat16))

    def advance(carried, items):
        zr_re, zr_im, zl_re, zl_im = carried
        mode_mat, level_row, shift_rows, broad_rows, inject_rows, link_cols, mask_row, chosen, screen = items
        detune = energy_grid[:, None] - level_row[None, :] - shift_rows
        damping = broaden_base + broad_rows
        denominator = detune * detune + damping * damping
        flipped = as_float(mode_mat.T)[None]
        scaled_re = ((detune / denominator)[:, :, None] * flipped).astype(jnp.bfloat16)
        scaled_im = ((-damping / denominator)[:, :, None] * flipped).astype(jnp.bfloat16)
        free_re = jnp.einsum('mn,enk->emk', as_float(mode_mat), as_float(scaled_re), precision=highest)
        free_im = jnp.einsum('mn,enk->emk', as_float(mode_mat), as_float(scaled_im), precision=highest)
        half_re = free_re.astype(jnp.bfloat16)
        half_im = free_im.astype(jnp.bfloat16)
        spread = jnp.repeat(mask_row, BLK).astype(jnp.bfloat16)
        link_mat = link_cols * spread[:, None]
        left_re = jnp.einsum('emn,nk->emk', as_float(half_re), as_float(link_mat), precision=highest)
        left_im = jnp.einsum('emn,nk->emk', as_float(half_im), as_float(link_mat), precision=highest)
        right_re = jnp.einsum('nk,enm->ekm', as_float(link_mat), as_float(half_re), precision=highest)
        right_im = jnp.einsum('nk,enm->ekm', as_float(link_mat), as_float(half_im), precision=highest)
        weight_root = jnp.sqrt(inject_rows)[:, None, :]
        root_re = as_float((free_re * weight_root).astype(jnp.bfloat16))
        root_im = as_float((free_im * weight_root).astype(jnp.bfloat16))
        inner_dot = partial(jnp.einsum, 'eik,ejk->eij', precision=highest)
        local_re = inner_dot(root_re, root_re) + inner_dot(root_im, root_im)
        local_im = inner_dot(root_im, root_re) - inner_dot(root_re, root_im)
        pz_re, pz_im = complex_product(left_re, left_im, zr_re, zr_im)
        pz_re, pz_im = (halved(pz_re), halved(pz_im))
        diag_im = jnp.einsum('enk,ekn->en', pz_re, halved(right_im), precision=highest) + jnp.einsum('enk,ekn->en', pz_im, halved(right_re), precision=highest)
        density = -(jnp.diagonal(free_im, axis1=1, axis2=2) + diag_im) / math.pi
        pl_re, pl_im = complex_product(left_re, left_im, zl_re, zl_im)
        chain_re, chain_im = complex_adjoint(halved(pl_re), halved(pl_im), halved(left_re), halved(left_im))
        lesser = jnp.stack([chain_re + local_re, chain_im + local_im]).astype(jnp.bfloat16)
        sigma_cell = convolve(lesser, screen, offsets)
        prop_re = block_of(left_re, chosen, BLK, 1)
        prop_im = block_of(left_im, chosen, BLK, 1)
        back_re = block_of(right_re, chosen, BLK, 2)
        back_im = block_of(right_im, chosen, BLK, 2)
        diag_re = block_of(block_of(free_re, chosen, BLK, 1), chosen, BLK, 2)
        diag_imag = block_of(block_of(free_im, chosen, BLK, 1), chosen, BLK, 2)
        quad_re = block_of(block_of(local_re, chosen, BLK, 1), chosen, BLK, 2)
        quad_im = block_of(block_of(local_im, chosen, BLK, 1), chosen, BLK, 2)
        middle_re, middle_im = complex_product(prop_re, prop_im, zr_re, zr_im)
        retard_re, retard_im = complex_product(middle_re, middle_im, back_re, back_im)
        leading_re, leading_im = complex_product(prop_re, prop_im, zl_re, zl_im)
        lesser_re, lesser_im = complex_adjoint(leading_re, leading_im, prop_re, prop_im)
        new_state = (diag_re + retard_re, diag_imag + retard_im, quad_re + lesser_re, quad_im + lesser_im)
        return (new_state, (density, sigma_cell))
    final_state, outputs = lax.scan(advance, (zero_block, zero_block, zero_block, zero_block), (modes, levels, level_shift, broadening, injection, coupling, row_mask, following, screened))
    return (outputs[0], outputs[1])
```

```python
from functools import partial
import math

import jax
import jax.numpy as jnp
from jax import lax
from jax.experimental import pallas as pl
from jax.experimental.pallas import tpu as pltpu
from jax.sharding import PartitionSpec as P

broaden_base = 1.0
energy_low = -0.25
energy_span = 0.5
f32 = jnp.float32
bf16 = jnp.bfloat16

VMEM = pl.BlockSpec(memory_space=pltpu.VMEM)
SMEM = pl.BlockSpec(memory_space=pltpu.SMEM)


def dot_last(a, b, precision=None):
    return lax.dot_general(
        a, b, (((1,), (1,)), ((), ())), precision=precision, preferred_element_type=f32
    )


def dot_mat(a, b):
    return lax.dot_general(a, b, (((1,), (0,)), ((), ())), preferred_element_type=f32)


def signs(width, left_sign):
    lane = lax.broadcasted_iota(jnp.int32, (1, width), 1)
    return jnp.where(lane < width // 2, left_sign, -left_sign).astype(f32)


def swap_halves(x):
    return pltpu.roll(x, x.shape[1] // 2, 1)


def full(x):
    x = x.astype(f32)
    return jnp.concatenate([x, swap_halves(x) * signs(x.shape[1], -1.0)], axis=0).astype(bf16)


def full_conj(x):
    x = x.astype(f32)
    return jnp.concatenate([x * signs(x.shape[1], 1.0), swap_halves(x)], axis=0).astype(bf16)


def resolvent(levels, shift, broad, index, overall):
    eps = energy_low + energy_span * (index.astype(f32) + 0.5) / overall
    detune = eps - levels - shift
    damping = broaden_base + broad
    inverse = 1.0 / (detune * detune + damping * damping)
    return detune * inverse, -damping * inverse


def masked_link(coupling_ref, mask_ref, link2_ref):
    rows, extent = coupling_ref.shape[1:]
    count = mask_ref.shape[1]
    size = rows // count
    link2_ref[...] = jnp.zeros_like(link2_ref)
    for block in range(count):
        keep = mask_ref[0, block].astype(f32)
        piece = (coupling_ref[0, block * size : (block + 1) * size, :].astype(f32) * keep).astype(bf16)
        link2_ref[block * size : (block + 1) * size, 0:extent] = piece
        link2_ref[rows + block * size : rows + (block + 1) * size, extent : 2 * extent] = piece


def maps_kernel(overall, ahead_ref, mask_ref, modes_ref, levels_ref, params_ref, coupling_ref, out_ref, link2_ref):
    energies = params_ref.shape[1]
    extent = coupling_ref.shape[2]
    first = lax.axis_index("energy") * energies
    masked_link(coupling_ref, mask_ref, link2_ref)
    link2 = link2_ref[...]
    chosen = pl.multiple_of(ahead_ref[0] * extent, extent)
    modes = modes_ref[0]
    rows = modes_ref[0, pl.ds(chosen, extent), :]
    rows_f = rows.astype(f32)
    none = jnp.zeros_like(rows)
    rows2 = jnp.concatenate(
        [jnp.concatenate([rows, none], axis=1), jnp.concatenate([none, rows], axis=1)], axis=0
    )
    for e in range(energies):
        dr, di = resolvent(
            levels_ref[...], params_ref[0, e : e + 1, :], params_ref[1, e : e + 1, :], first + e, overall
        )
        scaled_re = (rows_f * dr).astype(bf16)
        scaled_im = (rows_f * di).astype(bf16)
        both = dot_last(jnp.concatenate([scaled_re, scaled_im], axis=0), modes)
        free_re, free_im = both[:extent], both[extent:]
        halves = jnp.concatenate([free_re.astype(bf16), free_im.astype(bf16)], axis=1)
        out_ref[e, 0] = dot_mat(halves, link2).astype(bf16)
        out_ref[e, 1] = dot_last(jnp.concatenate([scaled_re, scaled_im], axis=1), rows2).astype(bf16)
        weight = jnp.sqrt(params_ref[2, e : e + 1, :])
        root_re, root_im = free_re * weight, free_im * weight
        straight = jnp.concatenate([root_re, root_im], axis=1).astype(bf16)
        turned = jnp.concatenate([-root_im, root_re], axis=1).astype(bf16)
        out_ref[e, 2] = dot_last(straight, jnp.concatenate([straight, turned], axis=0)).astype(bf16)


def rows_kernel(
    overall, hop, share, mask_ref, modes_ref, levels_ref, params_ref, coupling_ref, left_ref, local_ref, link2_ref
):
    energies = params_ref.shape[1]
    group = lax.axis_index("energy")
    first = jnp.bitwise_xor(group, hop) * energies
    masked_link(coupling_ref, mask_ref, link2_ref)
    link2 = link2_ref[...]
    modes = modes_ref[0]
    modes_f = modes.astype(f32)
    mine = pl.multiple_of(group * share, share)
    rows_f = modes_ref[0, pl.ds(mine, share), :].astype(f32)
    for e in range(energies):
        dr, di = resolvent(
            levels_ref[...], params_ref[0, e : e + 1, :], params_ref[1, e : e + 1, :], first + e, overall
        )
        free_re = dot_last((modes_f * dr).astype(bf16), modes)
        free_im = dot_last((modes_f * di).astype(bf16), modes)
        halves = jnp.concatenate([free_re.astype(bf16), free_im.astype(bf16)], axis=1)
        left_ref[e] = dot_mat(halves, link2).astype(bf16)
        weight = jnp.sqrt(params_ref[2, e : e + 1, :])
        straight = jnp.concatenate([free_re * weight, free_im * weight], axis=1).astype(bf16)
        turned = jnp.concatenate([-(free_im * weight), free_re * weight], axis=1).astype(bf16)
        own_re = dot_last((rows_f * dr).astype(bf16), modes) * weight
        own_im = dot_last((rows_f * di).astype(bf16), modes) * weight
        own = jnp.concatenate([own_re, own_im], axis=1).astype(bf16)
        local_ref[e, 0] = dot_last(own, straight).astype(bf16)
        local_ref[e, 1] = dot_last(own, turned).astype(bf16)


def pushed(step, state):
    first = dot_mat(step[0], jnp.concatenate([full(state[0]), full(state[1])], axis=1)).astype(bf16)
    width = step[0].shape[1]
    return (
        dot_last(first[:, :width], full_conj(step[0])),
        dot_last(first[:, width:], full(step[0])),
    )


def compose(earlier, latter):
    retarded, lesser = pushed(latter, earlier[1:])
    return (
        dot_mat(latter[0], full(earlier[0])),
        latter[1].astype(f32) + retarded,
        latter[2].astype(f32) + lesser,
    )


def pick(flag, yes, no):
    return tuple(jnp.where(flag, a, b) for a, b in zip(yes, no))


def neutral(extent, width):
    row = lax.broadcasted_iota(jnp.int32, (extent, width), 0)
    lane = lax.broadcasted_iota(jnp.int32, (extent, width), 1)
    zero = jnp.zeros((extent, width), f32)
    return (jnp.where(row == lane, 1.0, 0.0).astype(bf16), zero.astype(bf16), zero.astype(bf16))


def read(ref, e):
    return tuple(ref[e, part] for part in range(ref.shape[1]))


def join_kernel(level, *refs):
    total_ref, other_ref = refs[:2]
    enter_ref = refs[2] if level else None
    new_total_ref, new_enter_ref = refs[-2:]
    energies, _, extent, width = total_ref.shape
    place = lax.axis_index("cell")
    upper = jnp.bitwise_and(jnp.right_shift(place, level), 1) == 1
    parts = new_total_ref.shape[1]
    for e in range(energies):
        total, other = read(total_ref, e), read(other_ref, e)
        joined = compose(pick(upper, other, total), pick(upper, total, other))
        for part in range(parts):
            new_total_ref[e, part] = joined[part + 3 - parts].astype(bf16)
        if level:
            enter = read(enter_ref, e)
            longer = compose(other, enter)
            longer = tuple(x.astype(bf16) for x in longer)
            enter = pick(upper, longer, enter)
        else:
            enter = pick(upper, other, neutral(extent, width))
        for part in range(3):
            new_enter_ref[e, part] = enter[part]


def arrive_kernel(enter_ref, state_ref, retarded_ref, lesser_ref):
    for e in range(enter_ref.shape[0]):
        enter = read(enter_ref, e)
        retarded, lesser = pushed(enter, read(state_ref, e))
        retarded_ref[e] = (enter[1].astype(f32) + retarded).astype(bf16)
        lesser_ref[e] = (enter[2].astype(f32) + lesser).astype(bf16)


def density_kernel(overall, modes_ref, levels_ref, params_ref, left_ref, retarded_ref, out_ref):
    energies = params_ref.shape[1]
    first = lax.axis_index("energy") * energies
    modes = modes_ref[0].astype(f32)
    for e in range(energies):
        _, di = resolvent(
            levels_ref[...], params_ref[0, e : e + 1, :], params_ref[1, e : e + 1, :], first + e, overall
        )
        plain = modes * (modes * di).astype(bf16).astype(f32)
        left = left_ref[e]
        pz = dot_mat(left, full(retarded_ref[e])).astype(bf16).astype(f32)
        turned = pz * swap_halves(left.astype(f32))
        highest = lax.Precision.HIGHEST
        total = dot_last(jnp.ones((8, plain.shape[1]), f32), plain, highest) + dot_last(
            jnp.ones((8, turned.shape[1]), f32), turned, highest
        )
        out_ref[0, e : e + 1, :] = -total[0:1] / math.pi


def convolve_kernel(groups, reach, offsets_ref, screen_ref, *refs):
    lefts, locals_, lessers = refs[:groups], refs[groups : 2 * groups], refs[2 * groups : 3 * groups]
    out_ref, g_re, g_im = refs[3 * groups :]
    energies = lefts[0].shape[0]
    overall = energies * groups
    share, width = out_ref.shape[3:]
    group = lax.axis_index("energy")
    mine = pl.multiple_of(group * share, share)
    blank = jnp.zeros((share, width), f32)
    for e in range(reach):
        g_re[e] = blank
        g_im[e] = blank
        g_re[overall + reach + e] = blank
        g_im[overall + reach + e] = blank
    for hop in range(groups):
        base = jnp.bitwise_xor(group, hop) * energies + reach
        for e in range(energies):
            left = lefts[hop][e]
            own = lefts[hop][e, pl.ds(mine, share), :]
            pl_hat = dot_mat(own, full(lessers[hop][e]))
            turned = swap_halves(pl_hat) * signs(pl_hat.shape[1], 1.0)
            chain = dot_last(jnp.concatenate([pl_hat, turned], axis=0).astype(bf16), left)
            g_re[base + e] = chain[:share] + locals_[hop][e, 0].astype(f32)
            g_im[base + e] = chain[share:] + locals_[hop][e, 1].astype(f32)
    points = screen_ref.shape[2]
    lanes, height, batch = 128, 16, min(8, overall)

    def rows_of(step, _):
        top = pl.multiple_of(step * height, height)
        for lane in range(0, width, lanes):
            for e0 in range(0, overall, batch):
                sums = [None] * batch
                for k in range(points):
                    start = e0 + reach - offsets_ref[k]
                    w_re = screen_ref[0, 0, k, pl.ds(top, height), lane : lane + lanes].astype(f32)
                    w_im = screen_ref[0, 1, k, pl.ds(top, height), lane : lane + lanes].astype(f32)
                    for e in range(batch):
                        x_re = g_re[start + e, pl.ds(top, height), lane : lane + lanes]
                        x_im = g_im[start + e, pl.ds(top, height), lane : lane + lanes]
                        re = w_re * x_im + w_im * x_re
                        im = w_re * x_re - w_im * x_im
                        sums[e] = (re, im) if k == 0 else (sums[e][0] + re, sums[e][1] + im)
                for e in range(batch):
                    out_ref[0, 0, e0 + e, pl.ds(top, height), lane : lane + lanes] = (-sums[e][0]).astype(bf16)
                    out_ref[0, 1, e0 + e, pl.ds(top, height), lane : lane + lanes] = sums[e][1].astype(bf16)
        return 0

    lax.fori_loop(0, share // height, rows_of, 0)


def call(kernel, out_shape, in_specs, scratch=(), flops=1_000_000, size=1_000_000):
    outs = jax.tree.map(lambda _: VMEM, out_shape)
    return pl.pallas_call(
        kernel,
        out_shape=out_shape,
        in_specs=in_specs,
        out_specs=outs,
        scratch_shapes=list(scratch),
        cost_estimate=pl.CostEstimate(flops=flops, bytes_accessed=size, transcendentals=0),
    )


def body(
    modes,
    levels,
    level_shift,
    broadening,
    injection,
    coupling,
    row_mask,
    interface,
    screened,
    offsets,
):
    cells = lax.axis_size("cell")
    groups = lax.axis_size("energy")
    rounds = cells.bit_length() - 1
    assert cells == 1 << rounds and groups & (groups - 1) == 0
    energies = level_shift.shape[1]
    overall = energies * groups
    orbitals, extent = coupling.shape[1:]
    width = 2 * extent
    share = orbitals // groups
    sds = jax.ShapeDtypeStruct

    ahead = lax.ppermute(interface, "cell", [(i + 1, i) for i in range(cells - 1)])
    params = jnp.concatenate([level_shift, broadening, injection], axis=0)
    all_params = [params] + [
        lax.ppermute(params, "energy", [(i, i ^ hop) for i in range(groups)]) for hop in range(1, groups)
    ]
    link2 = pltpu.VMEM((2 * orbitals, width), bf16)

    total = call(
        partial(maps_kernel, overall),
        sds((energies, 3, extent, width), bf16),
        [SMEM, SMEM, VMEM, VMEM, VMEM, VMEM],
        [link2],
    )(ahead, row_mask, modes, levels, params, coupling)

    lefts, locals_ = [], []
    for hop in range(groups):
        left, local = call(
            partial(rows_kernel, overall, hop, share),
            (sds((energies, orbitals, width), bf16), sds((energies, 2, share, orbitals), bf16)),
            [SMEM, VMEM, VMEM, VMEM, VMEM],
            [link2],
        )(row_mask, modes, levels, all_params[hop], coupling)
        lefts.append(left)
        locals_.append(local)

    enter = None
    for level in range(rounds - 1):
        other = lax.ppermute(total, "cell", [(i, i ^ (1 << level)) for i in range(cells)])
        parts = 3 if level < rounds - 2 else 2
        given = [total, other] + ([enter] if level else [])
        total, enter = call(
            partial(join_kernel, level),
            (sds((energies, parts, extent, width), bf16), sds((energies, 3, extent, width), bf16)),
            [VMEM] * len(given),
        )(*given)
    half = cells // 2
    state = lax.ppermute(total, "cell", [(i, i + half) for i in range(half)])
    retarded, lesser = call(
        arrive_kernel,
        (sds((energies, extent, width), bf16), sds((energies, extent, width), bf16)),
        [VMEM, VMEM],
    )(enter, state)

    lessers = [lesser] + [
        lax.ppermute(lesser, "energy", [(i, i ^ hop) for i in range(groups)]) for hop in range(1, groups)
    ]
    density = call(
        partial(density_kernel, overall),
        sds((1, energies, orbitals), f32),
        [VMEM] * 5,
    )(modes, levels, params, lefts[0], retarded)

    reach = overall // 4
    spread = pltpu.VMEM((overall + 2 * reach, share, orbitals), f32)
    sigma = call(
        partial(convolve_kernel, groups, reach),
        sds((1, 2, overall, share, orbitals), bf16),
        [SMEM, VMEM] + [VMEM] * (3 * groups),
        [spread, spread],
    )(offsets, screened, *lefts, *locals_, *lessers)
    return (density, sigma)


def solution(mesh):
    placed = (
        P("cell", None, None),
        P("cell", None),
        P("cell", "energy", None),
        P("cell", "energy", None),
        P("cell", "energy", None),
        P("cell", None, None),
        P("cell", None),
        P("cell"),
        P("cell", None, None, "energy", None),
        P(),
    )
    return jax.shard_map(
        body,
        mesh=mesh,
        in_specs=placed,
        out_specs=(P("cell", "energy", None), P("cell", None, None, "energy", None)),
        check_vma=False,
    )
```

```python
from functools import partial
import math

import jax
import jax.numpy as jnp
from jax import lax
from jax.experimental import pallas as pl
from jax.experimental.pallas import tpu as pltpu
from jax.sharding import PartitionSpec as P


broaden_base = 1.0
energy_low = -0.25
energy_span = 0.5
f32 = jnp.float32
bf16 = jnp.bfloat16

VMEM = pl.BlockSpec(memory_space=pltpu.VMEM)
SMEM = pl.BlockSpec(memory_space=pltpu.SMEM)


def dot_last(a, b, precision=None):
    return lax.dot_general(
        a, b, (((1,), (1,)), ((), ())), precision=precision, preferred_element_type=f32
    )


def dot_mat(a, b):
    return lax.dot_general(a, b, (((1,), (0,)), ((), ())), preferred_element_type=f32)


def signs(width, left_sign):
    lane = lax.broadcasted_iota(jnp.int32, (1, width), 1)
    return jnp.where(lane < width // 2, left_sign, -left_sign).astype(f32)


def swap_halves(x):
    return pltpu.roll(x, x.shape[1] // 2, 1)


def full(x):
    x = x.astype(f32)
    return jnp.concatenate([x, swap_halves(x) * signs(x.shape[1], -1.0)], axis=0).astype(bf16)


def full_conj(x):
    x = x.astype(f32)
    return jnp.concatenate([x * signs(x.shape[1], 1.0), swap_halves(x)], axis=0).astype(bf16)


def resolvent(levels, shift, broad, index, overall):
    eps = energy_low + energy_span * (index.astype(f32) + 0.5) / overall
    detune = eps - levels - shift
    damping = broaden_base + broad
    inverse = 1.0 / (detune * detune + damping * damping)
    return detune * inverse, -damping * inverse


def masked_link(coupling_ref, mask_ref, link2_ref):
    extent, rows = coupling_ref.shape[1:]
    count = mask_ref.shape[1]
    block = lax.broadcasted_iota(jnp.int32, (1, rows), 1) // (rows // count)
    keep = jnp.zeros((1, rows), f32)
    for index in range(count):
        keep = jnp.where(block == index, mask_ref[0, index].astype(f32), keep)
    link = (coupling_ref[0].astype(f32) * keep).astype(bf16)
    none = jnp.zeros_like(link)
    link2_ref[0:extent, 0:rows] = link
    link2_ref[0:extent, rows:] = none
    link2_ref[extent:, 0:rows] = none
    link2_ref[extent:, rows:] = link


def resolvents(overall, first, e, levels_ref, shift_ref, broad_ref):
    return resolvent(levels_ref[...], shift_ref[0, e : e + 1, :], broad_ref[0, e : e + 1, :], first + e, overall)


def three_parts(refs):
    return refs if len(refs) == 3 else tuple(refs[0].at[i : i + 1] for i in range(3))


def maps_kernel(
    overall,
    ahead_ref,
    modes_ref,
    levels_ref,
    shift_ref,
    broad_ref,
    inject_ref,
    left_ref,
    free_ref,
    out_ref,
):
    energies = shift_ref.shape[1]
    extent = out_ref.shape[2]
    first = lax.axis_index("energy") * energies
    chosen = pl.multiple_of(ahead_ref[0] * extent, extent)
    rows = modes_ref[0, pl.ds(chosen, extent), :]
    width = rows.shape[1]
    rows_f = rows.astype(f32)
    none = jnp.zeros_like(rows)
    rows2 = jnp.concatenate(
        [jnp.concatenate([rows, none], axis=1), jnp.concatenate([none, rows], axis=1)], axis=0
    )
    for e in range(energies):
        dr, di = resolvents(overall, first, e, levels_ref, shift_ref, broad_ref)
        scaled = jnp.concatenate([(rows_f * dr).astype(bf16), (rows_f * di).astype(bf16)], axis=1)
        out_ref[e, 0] = left_ref[e, pl.ds(chosen, extent), :]
        out_ref[e, 1] = dot_last(scaled, rows2).astype(bf16)
        free = free_ref[e, pl.ds(chosen, extent), :]
        free_f = free.astype(f32)
        weight = inject_ref[0, e : e + 1, :]
        weighted = jnp.concatenate([free_f[:, :width] * weight, free_f[:, width:] * weight], axis=1)
        turned = jnp.concatenate([-free_f[:, width:], free_f[:, :width]], axis=1)
        out_ref[e, 2] = dot_last(
            weighted.astype(bf16), jnp.concatenate([free, turned.astype(bf16)], axis=0)
        ).astype(bf16)


def rows_kernel(
    overall,
    hop,
    share,
    mask_ref,
    modes_ref,
    levels_ref,
    coupling_ref,
    *rest,
):
    given = 3 if hop == 0 else 1
    shift_ref, broad_ref, inject_ref = three_parts(rest[:given])
    left_ref, local_ref, *rest = rest[given:]
    link2_ref = rest[-1]
    energies = shift_ref.shape[1]
    group = lax.axis_index("energy")
    first = jnp.bitwise_xor(group, hop) * energies
    masked_link(coupling_ref, mask_ref, link2_ref)
    link2 = link2_ref[...]
    modes = modes_ref[0]
    modes_f = modes.astype(f32)
    mine = pl.multiple_of(group * share, share)
    rows_f = modes_ref[0, pl.ds(mine, share), :].astype(f32)
    for e in range(energies):
        dr, di = resolvents(overall, first, e, levels_ref, shift_ref, broad_ref)
        free_re = dot_last((modes_f * dr).astype(bf16), modes)
        free_im = dot_last((modes_f * di).astype(bf16), modes)
        free = jnp.concatenate([free_re.astype(bf16), free_im.astype(bf16)], axis=1)
        if hop == 0:
            rest[0][e] = free
        left_ref[e] = dot_last(free, link2).astype(bf16)
        weight = inject_ref[0, e : e + 1, :]
        own = dot_last(jnp.concatenate([rows_f * dr, rows_f * di], axis=0).astype(bf16), modes) * weight
        own_re, own_im = own[:share], own[share:]
        own = jnp.concatenate(
            [jnp.concatenate([own_re, own_im], axis=1), jnp.concatenate([own_im, -own_re], axis=1)], axis=0
        )
        local = dot_last(own.astype(bf16), free)
        local_ref[e, 0] = local[:share].astype(bf16)
        local_ref[e, 1] = local[share:].astype(bf16)


def pushed(step, state):
    first = dot_mat(step[0], jnp.concatenate([full(state[0]), full(state[1])], axis=1)).astype(bf16)
    width = step[0].shape[1]
    return (
        dot_last(first[:, :width], full_conj(step[0])),
        dot_last(first[:, width:], full(step[0])),
    )


def compose(earlier, latter):
    retarded, lesser = pushed(latter, earlier[1:])
    return (
        dot_mat(latter[0], full(earlier[0])),
        latter[1].astype(f32) + retarded,
        latter[2].astype(f32) + lesser,
    )


def pick(flag, yes, no):
    return tuple(jnp.where(flag, a, b) for a, b in zip(yes, no))


def neutral(extent, width):
    row = lax.broadcasted_iota(jnp.int32, (extent, width), 0)
    lane = lax.broadcasted_iota(jnp.int32, (extent, width), 1)
    zero = jnp.zeros((extent, width), f32)
    return (jnp.where(row == lane, 1.0, 0.0).astype(bf16), zero.astype(bf16), zero.astype(bf16))


def read(ref, e):
    return tuple(ref[e, part] for part in range(ref.shape[1]))


def join_kernel(level, *refs):
    total_ref, other_ref = refs[:2]
    enter_ref = refs[2] if level else None
    new_total_ref, new_enter_ref = refs[-2:]
    energies, _, extent, width = total_ref.shape
    place = lax.axis_index("cell")
    upper = jnp.bitwise_and(jnp.right_shift(place, level), 1) == 1
    parts = new_total_ref.shape[1]
    for e in range(energies):
        total, other = read(total_ref, e), read(other_ref, e)
        joined = compose(pick(upper, other, total), pick(upper, total, other))
        for part in range(parts):
            new_total_ref[e, part] = joined[part + 3 - parts].astype(bf16)
        if level:
            enter = read(enter_ref, e)
            longer = compose(other, enter)
            longer = tuple(x.astype(bf16) for x in longer)
            enter = pick(upper, longer, enter)
        else:
            enter = pick(upper, other, neutral(extent, width))
        for part in range(3):
            new_enter_ref[e, part] = enter[part]


def arrive_kernel(level, enter_ref, state_ref, retarded_ref, lesser_ref):
    upper = jnp.right_shift(lax.axis_index("cell"), level) == 1
    for e in range(enter_ref.shape[0]):
        enter = read(enter_ref, e)
        state = pick(upper, read(state_ref, e), (jnp.zeros_like(enter[1]), jnp.zeros_like(enter[2])))
        retarded, lesser = pushed(enter, state)
        retarded_ref[e] = (enter[1].astype(f32) + retarded).astype(bf16)
        lesser_ref[e] = (enter[2].astype(f32) + lesser).astype(bf16)


def density_kernel(overall, modes_ref, levels_ref, shift_ref, broad_ref, left_ref, retarded_ref, out_ref):
    energies = shift_ref.shape[1]
    first = lax.axis_index("energy") * energies
    modes = modes_ref[0].astype(f32)
    for e in range(energies):
        _, di = resolvents(overall, first, e, levels_ref, shift_ref, broad_ref)
        plain = modes * (modes * di).astype(bf16).astype(f32)
        left = left_ref[e]
        pz = dot_mat(left, full(retarded_ref[e])).astype(bf16).astype(f32)
        turned = pz * swap_halves(left.astype(f32))
        highest = lax.Precision.HIGHEST
        total = dot_last(jnp.ones((8, plain.shape[1]), f32), plain, highest) + dot_last(
            jnp.ones((8, turned.shape[1]), f32), turned, highest
        )
        out_ref[0, e : e + 1, :] = -total[0:1] / math.pi


def convolve_kernel(groups, reach, offsets_ref, screen_ref, *refs):
    lefts, locals_, lessers = refs[:groups], refs[groups : 2 * groups], refs[2 * groups : 3 * groups]
    out_ref, g_re, g_im = refs[3 * groups :]
    energies = lefts[0].shape[0]
    overall = energies * groups
    share, width = out_ref.shape[3:]
    group = lax.axis_index("energy")
    mine = pl.multiple_of(group * share, share)
    blank = jnp.zeros((share, width), f32)
    for e in range(reach):
        g_re[e] = blank
        g_im[e] = blank
        g_re[overall + reach + e] = blank
        g_im[overall + reach + e] = blank
    for hop in range(groups):
        base = jnp.bitwise_xor(group, hop) * energies + reach
        for e in range(energies):
            left = lefts[hop][e]
            own = lefts[hop][e, pl.ds(mine, share), :]
            pl_hat = dot_mat(own, full(lessers[hop][e]))
            turned = swap_halves(pl_hat) * signs(pl_hat.shape[1], 1.0)
            chain = dot_last(jnp.concatenate([pl_hat, turned], axis=0).astype(bf16), left)
            g_re[base + e] = chain[:share] + locals_[hop][e, 0].astype(f32)
            g_im[base + e] = chain[share:] + locals_[hop][e, 1].astype(f32)
    points = screen_ref.shape[2]
    lanes, height, batch = 128, 16, min(8, overall)

    def rows_of(step, _):
        top = pl.multiple_of(step * height, height)
        for lane in range(0, width, lanes):
            for e0 in range(0, overall, batch):
                sums = [None] * batch
                for k in range(points):
                    start = e0 + reach - offsets_ref[k]
                    w_re = screen_ref[0, 0, k, pl.ds(top, height), lane : lane + lanes].astype(f32)
                    w_im = screen_ref[0, 1, k, pl.ds(top, height), lane : lane + lanes].astype(f32)
                    for e in range(batch):
                        x_re = g_re[start + e, pl.ds(top, height), lane : lane + lanes]
                        x_im = g_im[start + e, pl.ds(top, height), lane : lane + lanes]
                        re = w_re * x_im + w_im * x_re
                        im = w_re * x_re - w_im * x_im
                        sums[e] = (re, im) if k == 0 else (sums[e][0] + re, sums[e][1] + im)
                for e in range(batch):
                    out_ref[0, 0, e0 + e, pl.ds(top, height), lane : lane + lanes] = (-sums[e][0]).astype(bf16)
                    out_ref[0, 1, e0 + e, pl.ds(top, height), lane : lane + lanes] = sums[e][1].astype(bf16)
        return 0

    lax.fori_loop(0, share // height, rows_of, 0)


def call(kernel, out_shape, in_specs, scratch=(), flops=1_000_000, size=1_000_000):
    outs = jax.tree.map(lambda _: VMEM, out_shape)
    return pl.pallas_call(
        kernel,
        out_shape=out_shape,
        in_specs=in_specs,
        out_specs=outs,
        scratch_shapes=list(scratch),
        compiler_params=pltpu.CompilerParams(vmem_limit_bytes=16 << 20),
        cost_estimate=pl.CostEstimate(flops=flops, bytes_accessed=size, transcendentals=0),
    )


def body(
    modes,
    levels,
    level_shift,
    broadening,
    injection,
    coupling,
    row_mask,
    interface,
    screened,
    offsets,
):
    cells = lax.axis_size("cell")
    groups = lax.axis_size("energy")
    rounds = cells.bit_length() - 1
    assert cells == 1 << rounds and groups & (groups - 1) == 0
    energies = level_shift.shape[1]
    overall = energies * groups
    orbitals, extent = coupling.shape[1:]
    width = 2 * extent
    share = orbitals // groups
    sds = jax.ShapeDtypeStruct

    def swapped(x, axis, distance):
        return lax.ppermute(x, axis, [(i, i ^ distance) for i in range(lax.axis_size(axis))])

    def others(x):
        got = [x]
        for hop in range(1, groups):
            got.append(swapped(x, "energy", hop))
        return got

    coupling = jnp.swapaxes(coupling, 1, 2)
    ahead = lax.ppermute(interface, "cell", [(i + 1, i) for i in range(cells - 1)])
    params = others(jnp.concatenate([level_shift, broadening, injection], axis=0))

    lefts, locals_ = [], []
    for hop in range(groups):
        outs = (sds((energies, orbitals, width), bf16), sds((energies, 2, share, orbitals), bf16))
        given = (level_shift, broadening, injection)
        if hop == 0:
            outs += (sds((energies, orbitals, 2 * orbitals), bf16),)
        else:
            given = (params[hop],)
        left, local, *rest = call(
            partial(rows_kernel, overall, hop, share),
            outs,
            [SMEM] + [VMEM] * (3 + len(given)),
            [pltpu.VMEM((width, 2 * orbitals), bf16)],
        )(row_mask, modes, levels, coupling, *given)
        if hop == 0:
            free = rest[0]
        lefts.append(left)
        locals_.append(local)

    total = call(
        partial(maps_kernel, overall),
        sds((energies, 3, extent, width), bf16),
        [SMEM] + [VMEM] * 7,
    )(ahead, modes, levels, level_shift, broadening, injection, lefts[0], free)

    enter = None
    for level in range(rounds - 1):
        other = swapped(total, "cell", 1 << level)
        parts = 3 if level < rounds - 2 else 2
        given = [total, other] + ([enter] if level else [])
        total, enter = call(
            partial(join_kernel, level),
            (sds((energies, parts, extent, width), bf16), sds((energies, 3, extent, width), bf16)),
            [VMEM] * len(given),
        )(*given)
    state = swapped(total, "cell", cells // 2)
    retarded, lesser = call(
        partial(arrive_kernel, rounds - 1),
        (sds((energies, extent, width), bf16), sds((energies, extent, width), bf16)),
        [VMEM, VMEM],
    )(enter, state)

    lessers = others(lesser)
    density = call(
        partial(density_kernel, overall),
        sds((1, energies, orbitals), f32),
        [VMEM] * 6,
    )(modes, levels, level_shift, broadening, lefts[0], retarded)

    reach = overall // 4
    spread = pltpu.VMEM((overall + 2 * reach, share, orbitals), f32)
    sigma = call(
        partial(convolve_kernel, groups, reach),
        sds((1, 2, overall, share, orbitals), bf16),
        [SMEM, VMEM] + [VMEM] * (3 * groups),
        [spread, spread],
    )(offsets, screened, *lefts, *locals_, *lessers)
    return (density, sigma)


def solution(mesh):
    placed = (
        P("cell", None, None),
        P("cell", None),
        P("cell", "energy", None),
        P("cell", "energy", None),
        P("cell", "energy", None),
        P("cell", None, None),
        P("cell", None),
        P("cell"),
        P("cell", None, None, "energy", None),
        P(),
    )
    return jax.shard_map(
        body,
        mesh=mesh,
        in_specs=placed,
        out_specs=(P("cell", "energy", None), P("cell", None, None, "energy", None)),
        check_vma=False,
    )
```

```python
from functools import partial
import math

import jax
import jax.numpy as jnp
from jax import lax
from jax.experimental import pallas as pl
from jax.experimental.pallas import tpu as pltpu
from jax.sharding import PartitionSpec as P


broaden_base = 1.0
energy_low = -0.25
energy_span = 0.5
f32 = jnp.float32
bf16 = jnp.bfloat16

VMEM = pl.BlockSpec(memory_space=pltpu.VMEM)
SMEM = pl.BlockSpec(memory_space=pltpu.SMEM)
HBM = pl.BlockSpec(memory_space=pltpu.HBM)


def dot_last(a, b, precision=None):
    return lax.dot_general(
        a, b, (((1,), (1,)), ((), ())), precision=precision, preferred_element_type=f32
    )


def dot_mat(a, b):
    return lax.dot_general(a, b, (((1,), (0,)), ((), ())), preferred_element_type=f32)


def signs(width, left_sign):
    lane = lax.broadcasted_iota(jnp.int32, (1, width), 1)
    return jnp.where(lane < width // 2, left_sign, -left_sign).astype(f32)


def swap_halves(x):
    return pltpu.roll(x, x.shape[1] // 2, 1)


def full(x):
    x = x.astype(f32)
    return jnp.concatenate([x, swap_halves(x) * signs(x.shape[1], -1.0)], axis=0).astype(bf16)


def full_conj(x):
    x = x.astype(f32)
    return jnp.concatenate([x * signs(x.shape[1], 1.0), swap_halves(x)], axis=0).astype(bf16)


def resolvent(levels, shift, broad, index, overall):
    eps = energy_low + energy_span * (index.astype(f32) + 0.5) / overall
    detune = eps - levels - shift
    damping = broaden_base + broad
    inverse = 1.0 / (detune * detune + damping * damping)
    return detune * inverse, -damping * inverse


def masked_link(link2_ref, coupling_ref, mask_ref):
    extent, rows = coupling_ref.shape[1:]
    count = mask_ref.shape[1]
    block = lax.broadcasted_iota(jnp.int32, (1, rows), 1) // (rows // count)
    keep = jnp.zeros((1, rows), f32)
    for index in range(count):
        keep = jnp.where(block == index, mask_ref[0, index].astype(f32), keep)
    link = (coupling_ref[0].astype(f32) * keep).astype(bf16)
    none = jnp.zeros_like(link)
    link2_ref[0:extent, 0:rows] = link
    link2_ref[0:extent, rows:] = none
    link2_ref[extent:, 0:rows] = none
    link2_ref[extent:, rows:] = link


def resolvents(overall, first, e, levels_ref, params_ref):
    return resolvent(levels_ref[...], params_ref[0, e : e + 1, :], params_ref[1, e : e + 1, :], first + e, overall)


def maps_kernel(
    overall,
    one_ref,
    two_ref,
    modes_ref,
    levels_ref,
    params_ref,
    left_ref,
    free_ref,
    out_ref,
    message_ref,
):
    energies = params_ref.shape[2]
    extent = out_ref.shape[2]
    first = lax.axis_index("energy") * energies
    odd = jnp.bitwise_and(lax.axis_index("cell"), 1) == 1
    chosen = pl.multiple_of(jnp.where(odd, two_ref[0], one_ref[0]) * extent, extent)
    rows = modes_ref[0, pl.ds(chosen, extent), :]
    width = rows.shape[1]
    rows_f = rows.astype(f32)
    none = jnp.zeros_like(rows)
    rows2 = jnp.concatenate(
        [jnp.concatenate([rows, none], axis=1), jnp.concatenate([none, rows], axis=1)], axis=0
    )
    maps = []
    for e in range(energies):
        dr, di = resolvents(overall, first, e, levels_ref, params_ref.at[0])
        scaled = jnp.concatenate([(rows_f * dr).astype(bf16), (rows_f * di).astype(bf16)], axis=1)
        free = free_ref[e, pl.ds(chosen, extent), :]
        free_f = free.astype(f32)
        weight = params_ref[0, 2, e : e + 1, :]
        weighted = jnp.concatenate([free_f[:, :width] * weight, free_f[:, width:] * weight], axis=1)
        turned = jnp.concatenate([-free_f[:, width:], free_f[:, :width]], axis=1)
        maps.append(
            (
                left_ref[e, pl.ds(chosen, extent), :],
                dot_last(scaled, rows2),
                dot_last(weighted.astype(bf16), jnp.concatenate([free, turned.astype(bf16)], axis=0)),
            )
        )
        for part in range(3):
            out_ref[e, part] = maps[e][part].astype(bf16)
    write_message(message_ref, maps)


def make_rows(energies, hop, overall, share, modes_ref, levels_ref, params_ref, link2_ref, left_ref, local_ref, free_ref):
    group = lax.axis_index("energy")
    first = jnp.bitwise_xor(group, hop) * energies
    link2 = link2_ref[...]
    modes = modes_ref[0]
    modes_f = modes.astype(f32)
    mine = pl.multiple_of(group * share, share)
    rows_f = modes_ref[0, pl.ds(mine, share), :].astype(f32)
    for e in range(energies):
        dr, di = resolvents(overall, first, e, levels_ref, params_ref)
        free_re = dot_last((modes_f * dr).astype(bf16), modes)
        free_im = dot_last((modes_f * di).astype(bf16), modes)
        free = jnp.concatenate([free_re.astype(bf16), free_im.astype(bf16)], axis=1)
        if free_ref is not None:
            free_ref[e] = free
        left_ref[e] = dot_last(free, link2).astype(bf16)
        weight = params_ref[2, e : e + 1, :]
        own = dot_last(jnp.concatenate([rows_f * dr, rows_f * di], axis=0).astype(bf16), modes) * weight
        own_re, own_im = own[:share], own[share:]
        own = jnp.concatenate(
            [jnp.concatenate([own_re, own_im], axis=1), jnp.concatenate([own_im, -own_re], axis=1)], axis=0
        )
        local = dot_last(own.astype(bf16), free)
        local_ref[e, 0] = local[:share].astype(bf16)
        local_ref[e, 1] = local[share:].astype(bf16)


def own_rows_kernel(
    overall,
    share,
    mask_hbm,
    modes_hbm,
    levels_hbm,
    coupling_hbm,
    shift_hbm,
    broad_hbm,
    inject_hbm,
    left_ref,
    local_ref,
    free_ref,
    link2_ref,
    modes_ref,
    levels_ref,
    params_ref,
    mask_ref,
    coupling_ref,
    sems,
):
    energies = shift_hbm.shape[1]
    copies = [
        pltpu.make_async_copy(source, target, sems.at[index])
        for index, (source, target) in enumerate(
            (
                (mask_hbm, mask_ref),
                (coupling_hbm, coupling_ref),
                (shift_hbm, params_ref.at[0, 0:1]),
                (broad_hbm, params_ref.at[0, 1:2]),
                (inject_hbm, params_ref.at[0, 2:3]),
                (levels_hbm, levels_ref),
                (modes_hbm, modes_ref),
            )
        )
    ]
    for copy in copies:
        copy.start()
    for copy in copies:
        copy.wait()
    masked_link(link2_ref, coupling_ref, mask_ref)
    make_rows(
        energies,
        0,
        overall,
        share,
        modes_ref,
        levels_ref,
        params_ref.at[0],
        link2_ref,
        left_ref,
        local_ref,
        free_ref,
    )


def rows_kernel(overall, share, hop, slot, modes_ref, levels_ref, link2_ref, got_ref, *rest):
    if len(rest) > 2:
        had_ref, left_ref, local_ref, both_ref = rest
        count = had_ref.shape[0]
        both_ref[0:count] = had_ref[...]
        both_ref[count:] = got_ref[...]
    else:
        left_ref, local_ref = rest
    make_rows(
        got_ref.shape[2],
        hop,
        overall,
        share,
        modes_ref,
        levels_ref,
        got_ref.at[slot],
        link2_ref,
        left_ref,
        local_ref,
        None,
    )


spare = 16


def places(extent, width):
    row = lax.broadcasted_iota(jnp.int32, (extent, width), 0)
    lane = lax.broadcasted_iota(jnp.int32, (extent, width), 1)
    return row, jnp.where(lane < extent, lane, lane - extent), lane < extent


def pack_lesser(first, second):
    _, _, low = places(*first.shape)
    return jnp.where(low, first + swap_halves(first), second + swap_halves(second))


def with_turned(x):
    square = jnp.concatenate([x, swap_halves(x)], axis=0)
    return square, square.T


def unpack_lesser(packed):
    packed = packed.astype(f32)
    extent, width = packed.shape
    _, _, low = places(extent, width)
    square, turned = with_turned(packed)
    total, change = 0.5 * (square + turned), 0.5 * (square - turned)
    return (
        jnp.where(low, total[:extent], change[extent:]),
        jnp.where(low, total[extent:], change[:extent]),
    )


def pack_retarded(first, second):
    row, column, _ = places(*first.shape)
    diagonal = jnp.sum(jnp.where(row == column, second, 0.0), axis=0, keepdims=True)
    return jnp.where(row <= column, first, second), jnp.broadcast_to(diagonal, (spare, first.shape[1]))


def unpack_retarded(packed, diagonal):
    packed, diagonal = packed.astype(f32), diagonal.astype(f32)
    extent, width = packed.shape
    row, column, _ = places(extent, width)
    turned = with_turned(packed)[1][:extent]
    return (
        jnp.where(row <= column, packed, turned),
        jnp.where(row > column, packed, jnp.where(row == column, diagonal, turned)),
    )


def write_message(ref, maps):
    extent = maps[0][-1].shape[0]
    for pair in range(ref.shape[0]):
        first, second = maps[2 * pair], maps[2 * pair + 1]
        shared, diagonal = pack_retarded(first[-2], second[-2])
        ref[pair, 0:extent] = shared.astype(bf16)
        ref[pair, extent : 2 * extent] = pack_lesser(first[-1], second[-1]).astype(bf16)
        ref[pair, 2 * extent : 2 * extent + spare] = diagonal.astype(bf16)
        if ref.shape[1] > 2 * extent + spare:
            ref[pair, 2 * extent + spare : 3 * extent + spare] = first[0].astype(bf16)
            ref[pair, 3 * extent + spare :] = second[0].astype(bf16)


def read_message(ref):
    extent = ref.shape[2] // 2
    maps = []
    for pair in range(ref.shape[0]):
        retarded = unpack_retarded(ref[pair, 0:extent], ref[pair, 2 * extent : 2 * extent + 1])
        lesser = unpack_lesser(ref[pair, extent : 2 * extent])
        for which in range(2):
            start = (2 + which) * extent + spare
            front = (ref[pair, start : start + extent],) if ref.shape[1] > 2 * extent + spare else ()
            maps.append(front + (retarded[which].astype(bf16), lesser[which].astype(bf16)))
    return maps


def pushed(step, state):
    first = dot_mat(step[0], jnp.concatenate([full(state[0]), full(state[1])], axis=1)).astype(bf16)
    width = step[0].shape[1]
    return (
        dot_last(first[:, :width], full_conj(step[0])),
        dot_last(first[:, width:], full(step[0])),
    )


def compose(earlier, latter):
    retarded, lesser = pushed(latter, earlier[1:])
    return (
        dot_mat(latter[0], full(earlier[0])),
        latter[1].astype(f32) + retarded,
        latter[2].astype(f32) + lesser,
    )


def pick(flag, yes, no):
    return tuple(jnp.where(flag, a, b) for a, b in zip(yes, no))


def neutral(extent, width):
    row = lax.broadcasted_iota(jnp.int32, (extent, width), 0)
    lane = lax.broadcasted_iota(jnp.int32, (extent, width), 1)
    zero = jnp.zeros((extent, width), f32)
    return (jnp.where(row == lane, 1.0, 0.0).astype(bf16), zero.astype(bf16), zero.astype(bf16))


def read(ref, e):
    return tuple(ref[e, part] for part in range(ref.shape[1]))


def join_kernel(level, *refs):
    total_ref, other_ref = refs[:2]
    enter_ref = refs[2] if level else None
    outs = refs[3 if level else 2 :]
    new_enter_ref, message_ref = outs[:2]
    energies, _, extent, width = total_ref.shape
    place = lax.axis_index("cell")
    upper = jnp.bitwise_and(jnp.right_shift(place, level), 1) == 1
    others = read_message(other_ref)
    joined = []
    for e in range(energies):
        total, other = read(total_ref, e), others[e]
        joined.append(compose(pick(upper, other, total), pick(upper, total, other)))
        if level:
            enter = read(enter_ref, e)
            longer = compose(other, enter)
            longer = tuple(x.astype(bf16) for x in longer)
            enter = pick(upper, longer, enter)
        else:
            enter = pick(upper, other, neutral(extent, width))
        for part in range(3):
            new_enter_ref[e, part] = enter[part]
            if len(outs) > 2:
                outs[2][e, part] = joined[e][part].astype(bf16)
    write_message(message_ref, joined)


def arrive_kernel(level, enter_ref, state_ref, retarded_ref, lesser_ref):
    upper = jnp.right_shift(lax.axis_index("cell"), level) == 1
    states = read_message(state_ref)
    lessers = []
    for e in range(enter_ref.shape[0]):
        enter = read(enter_ref, e)
        state = pick(upper, states[e], (jnp.zeros_like(enter[1]), jnp.zeros_like(enter[2])))
        retarded, lesser = pushed(enter, state)
        retarded_ref[e] = (enter[1].astype(f32) + retarded).astype(bf16)
        lessers.append(enter[2].astype(f32) + lesser)
    for pair in range(lesser_ref.shape[0]):
        lesser_ref[pair] = pack_lesser(lessers[2 * pair], lessers[2 * pair + 1]).astype(bf16)


def density_kernel(overall, modes_ref, levels_ref, params_ref, left_ref, retarded_ref, out_ref):
    energies = params_ref.shape[2]
    first = lax.axis_index("energy") * energies
    modes = modes_ref[0].astype(f32)
    for e in range(energies):
        _, di = resolvents(overall, first, e, levels_ref, params_ref.at[0])
        plain = modes * (modes * di).astype(bf16).astype(f32)
        left = left_ref[e]
        pz = dot_mat(left, full(retarded_ref[e])).astype(bf16).astype(f32)
        turned = pz * swap_halves(left.astype(f32))
        highest = lax.Precision.HIGHEST
        total = dot_last(jnp.ones((8, plain.shape[1]), f32), plain, highest) + dot_last(
            jnp.ones((8, turned.shape[1]), f32), turned, highest
        )
        out_ref[0, e : e + 1, :] = -total[0:1] / math.pi


def convolve_kernel(groups, reach, offsets_hbm, screen_ref, *refs):
    lefts, locals_, lessers = refs[:groups], refs[groups : 2 * groups], refs[2 * groups : 3 * groups]
    out_ref, g_re, g_im, offsets_ref, sem = refs[3 * groups :]
    copy = pltpu.make_async_copy(offsets_hbm, offsets_ref, sem)
    copy.start()
    energies = lefts[0].shape[0]
    overall = energies * groups
    share, width = out_ref.shape[3:]
    group = lax.axis_index("energy")
    mine = pl.multiple_of(group * share, share)
    blank = jnp.zeros((share, width), f32)
    for e in range(reach):
        g_re[e] = blank
        g_im[e] = blank
        g_re[overall + reach + e] = blank
        g_im[overall + reach + e] = blank
    for hop in range(groups):
        base = jnp.bitwise_xor(group, hop) * energies + reach
        for pair in range(energies // 2):
            states = unpack_lesser(lessers[hop][pair])
            for e in (2 * pair, 2 * pair + 1):
                left = lefts[hop][e]
                own = lefts[hop][e, pl.ds(mine, share), :]
                pl_hat = dot_mat(own, full(states[e - 2 * pair]))
                turned = swap_halves(pl_hat) * signs(pl_hat.shape[1], 1.0)
                chain = dot_last(jnp.concatenate([pl_hat, turned], axis=0).astype(bf16), left)
                g_re[base + e] = chain[:share] + locals_[hop][e, 0].astype(f32)
                g_im[base + e] = chain[share:] + locals_[hop][e, 1].astype(f32)
    copy.wait()
    points = screen_ref.shape[2]
    lanes, height, batch = 128, 16, min(8, overall)

    def rows_of(step, _):
        top = pl.multiple_of(step * height, height)
        for lane in range(0, width, lanes):
            for e0 in range(0, overall, batch):
                sums = [None] * batch
                for k in range(points):
                    start = e0 + reach - offsets_ref[k]
                    w_re = screen_ref[0, 0, k, pl.ds(top, height), lane : lane + lanes].astype(f32)
                    w_im = screen_ref[0, 1, k, pl.ds(top, height), lane : lane + lanes].astype(f32)
                    for e in range(batch):
                        x_re = g_re[start + e, pl.ds(top, height), lane : lane + lanes]
                        x_im = g_im[start + e, pl.ds(top, height), lane : lane + lanes]
                        re = w_re * x_im + w_im * x_re
                        im = w_re * x_re - w_im * x_im
                        sums[e] = (re, im) if k == 0 else (sums[e][0] + re, sums[e][1] + im)
                for e in range(batch):
                    out_ref[0, 0, e0 + e, pl.ds(top, height), lane : lane + lanes] = (-sums[e][0]).astype(bf16)
                    out_ref[0, 1, e0 + e, pl.ds(top, height), lane : lane + lanes] = sums[e][1].astype(bf16)
        return 0

    lax.fori_loop(0, share // height, rows_of, 0)


def in_hbm(x):
    return pltpu.with_memory_space_constraint(x, pltpu.HBM)


def call(kernel, out_shape, in_specs, scratch=(), flops=1_000_000, size=1_000_000):
    outs = jax.tree.map(lambda _: VMEM, out_shape)
    return pl.pallas_call(
        kernel,
        out_shape=out_shape,
        in_specs=in_specs,
        out_specs=outs,
        scratch_shapes=list(scratch),
        compiler_params=pltpu.CompilerParams(vmem_limit_bytes=16 << 20),
        cost_estimate=pl.CostEstimate(flops=flops, bytes_accessed=size, transcendentals=0),
    )


def body(
    modes,
    levels,
    level_shift,
    broadening,
    injection,
    coupling,
    row_mask,
    interface,
    screened,
    offsets,
):
    cells = lax.axis_size("cell")
    groups = lax.axis_size("energy")
    rounds = cells.bit_length() - 1
    assert cells == 1 << rounds and groups & (groups - 1) == 0
    energies = level_shift.shape[1]
    overall = energies * groups
    orbitals, extent = coupling.shape[1:]
    width = 2 * extent
    share = orbitals // groups
    sds = jax.ShapeDtypeStruct

    def swapped(x, axis, distance):
        return lax.ppermute(x, axis, [(i, i ^ distance) for i in range(lax.axis_size(axis))])

    assert energies % 2 == 0
    pairs = energies // 2
    maps_shape = sds((energies, 3, extent, width), bf16)
    message = sds((pairs, 4 * extent + spare, width), bf16)
    state_message = sds((pairs, 2 * extent + spare, width), bf16)
    coupling = jnp.swapaxes(coupling, 1, 2)
    one = swapped(interface, "cell", 1)
    near = [(i, i + 1) for i in range(1, cells - 1, 2)]
    two = lax.ppermute(interface, "cell", near + [(j, i) for i, j in near])

    left_shape = sds((energies, orbitals, width), bf16)
    local_shape = sds((energies, 2, share, orbitals), bf16)
    params_shape = (3, energies, orbitals)
    left, local, free, link2, modes, levels, params = call(
        partial(own_rows_kernel, overall, share),
        (
            left_shape,
            local_shape,
            sds((energies, orbitals, 2 * orbitals), bf16),
            sds((width, 2 * orbitals), bf16),
            sds(modes.shape, bf16),
            sds(levels.shape, f32),
            sds((1,) + params_shape, f32),
        ),
        [HBM] * 7,
        [
            pltpu.SMEM(row_mask.shape, jnp.int32),
            pltpu.VMEM(coupling.shape, bf16),
            pltpu.SemaphoreType.DMA((7,)),
        ],
    )(*map(in_hbm, (row_mask, modes, levels, coupling, level_shift, broadening, injection)))
    lefts, locals_ = [left], [local]

    total, sent = call(
        partial(maps_kernel, overall),
        (maps_shape, message),
        [SMEM] * 2 + [VMEM] * 5,
    )(one, two, modes, levels, params, left, free)

    known = params
    while known.shape[0] < groups:
        count = known.shape[0]
        got = swapped(known, "energy", count)
        more = 2 * count < groups
        for slot in range(count):
            outs, given = (left_shape, local_shape), (modes, levels, link2, got)
            if slot == 0 and more:
                outs, given = outs + (sds((2 * count,) + params_shape, f32),), given + (known,)
            left, local, *rest = call(
                partial(rows_kernel, overall, share, count + slot, slot), outs, [VMEM] * len(given)
            )(*given)
            lefts.append(left)
            locals_.append(local)
            if rest:
                both = rest[0]
        if not more:
            break
        known = both

    enter = None
    for level in range(rounds - 1):
        other = swapped(sent, "cell", 1 << level)
        outs = (maps_shape, message, maps_shape) if level < rounds - 2 else (maps_shape, state_message)
        given = [total, other] + ([enter] if level else [])
        enter, sent, *rest = call(partial(join_kernel, level), outs, [VMEM] * len(given))(*given)
        total = rest[0] if rest else None
    state = swapped(sent, "cell", cells // 2)
    retarded, lesser = call(
        partial(arrive_kernel, rounds - 1),
        (sds((energies, extent, width), bf16), sds((pairs, extent, width), bf16)),
        [VMEM, VMEM],
    )(enter, state)

    lessers = [lesser]
    for hop in range(1, groups):
        lessers.append(swapped(lesser, "energy", hop))
    density = call(
        partial(density_kernel, overall),
        sds((1, energies, orbitals), f32),
        [VMEM] * 5,
    )(modes, levels, params, lefts[0], retarded)

    reach = overall // 4
    spread = pltpu.VMEM((overall + 2 * reach, share, orbitals), f32)
    sigma = call(
        partial(convolve_kernel, groups, reach),
        sds((1, 2, overall, share, orbitals), bf16),
        [HBM, VMEM] + [VMEM] * (3 * groups),
        [spread, spread, pltpu.SMEM(offsets.shape, jnp.int32), pltpu.SemaphoreType.DMA],
    )(in_hbm(offsets), screened, *lefts, *locals_, *lessers)
    return (density, sigma)


def solution(mesh):
    placed = (
        P("cell", None, None),
        P("cell", None),
        P("cell", "energy", None),
        P("cell", "energy", None),
        P("cell", "energy", None),
        P("cell", None, None),
        P("cell", None),
        P("cell"),
        P("cell", None, None, "energy", None),
        P(),
    )
    return jax.shard_map(
        body,
        mesh=mesh,
        in_specs=placed,
        out_specs=(P("cell", "energy", None), P("cell", None, None, "energy", None)),
        check_vma=False,
    )
```

```python
from functools import partial
import math

import jax
import jax.numpy as jnp
from jax import lax
from jax.experimental import pallas as pl
from jax.experimental.pallas import tpu as pltpu
from jax.sharding import PartitionSpec as P


broaden_base = 1.0
energy_low = -0.25
energy_span = 0.5
f32 = jnp.float32
bf16 = jnp.bfloat16

VMEM = pl.BlockSpec(memory_space=pltpu.VMEM)
SMEM = pl.BlockSpec(memory_space=pltpu.SMEM)
HBM = pl.BlockSpec(memory_space=pltpu.HBM)


def dot_last(a, b, precision=None):
    return lax.dot_general(
        a, b, (((1,), (1,)), ((), ())), precision=precision, preferred_element_type=f32
    )


def dot_mat(a, b):
    return lax.dot_general(a, b, (((1,), (0,)), ((), ())), preferred_element_type=f32)


def signs(width, left_sign):
    lane = lax.broadcasted_iota(jnp.int32, (1, width), 1)
    return jnp.where(lane < width // 2, left_sign, -left_sign).astype(f32)


def swap_halves(x):
    return pltpu.roll(x, x.shape[1] // 2, 1)


def full(x):
    x = x.astype(f32)
    return jnp.concatenate([x, swap_halves(x) * signs(x.shape[1], -1.0)], axis=0).astype(bf16)


def full_conj(x):
    x = x.astype(f32)
    return jnp.concatenate([x * signs(x.shape[1], 1.0), swap_halves(x)], axis=0).astype(bf16)


def resolvent(levels, shift, broad, index, overall):
    eps = energy_low + energy_span * (index.astype(f32) + 0.5) / overall
    detune = eps - levels - shift
    damping = broaden_base + broad
    inverse = 1.0 / (detune * detune + damping * damping)
    return detune * inverse, -damping * inverse


def masked_link(link2_ref, coupling_ref, mask_ref):
    extent, rows = coupling_ref.shape[1:]
    count = mask_ref.shape[1]
    block = lax.broadcasted_iota(jnp.int32, (1, rows), 1) // (rows // count)
    keep = jnp.zeros((1, rows), f32)
    for index in range(count):
        keep = jnp.where(block == index, mask_ref[0, index].astype(f32), keep)
    link = (coupling_ref[0].astype(f32) * keep).astype(bf16)
    none = jnp.zeros_like(link)
    link2_ref[0:extent, 0:rows] = link
    link2_ref[0:extent, rows:] = none
    link2_ref[extent:, 0:rows] = none
    link2_ref[extent:, rows:] = link


def resolvents(overall, first, e, levels_ref, params_ref):
    return resolvent(levels_ref[...], params_ref[0, e : e + 1, :], params_ref[1, e : e + 1, :], first + e, overall)


def maps_kernel(
    overall,
    one_ref,
    two_ref,
    modes_ref,
    levels_ref,
    params_ref,
    left_ref,
    free_ref,
    out_ref,
    message_ref,
):
    energies = params_ref.shape[2]
    extent = out_ref.shape[2]
    first = lax.axis_index("energy") * energies
    odd = jnp.bitwise_and(lax.axis_index("cell"), 1) == 1
    block = jnp.max(jnp.where(odd, two_ref[...], one_ref[...])).astype(jnp.int32)
    chosen = pl.multiple_of(block * extent, extent)
    rows = modes_ref[0, pl.ds(chosen, extent), :]
    width = rows.shape[1]
    rows_f = rows.astype(f32)
    none = jnp.zeros_like(rows)
    rows2 = jnp.concatenate(
        [jnp.concatenate([rows, none], axis=1), jnp.concatenate([none, rows], axis=1)], axis=0
    )
    maps = []
    for e in range(energies):
        dr, di = resolvents(overall, first, e, levels_ref, params_ref.at[0])
        scaled = jnp.concatenate([(rows_f * dr).astype(bf16), (rows_f * di).astype(bf16)], axis=1)
        free = free_ref[e, pl.ds(chosen, extent), :]
        free_f = free.astype(f32)
        weight = params_ref[0, 2, e : e + 1, :]
        weighted = jnp.concatenate([free_f[:, :width] * weight, free_f[:, width:] * weight], axis=1)
        turned = jnp.concatenate([-free_f[:, width:], free_f[:, :width]], axis=1)
        maps.append(
            (
                left_ref[e, pl.ds(chosen, extent), :],
                dot_last(scaled, rows2),
                dot_last(weighted.astype(bf16), jnp.concatenate([free, turned.astype(bf16)], axis=0)),
            )
        )
        for part in range(3):
            out_ref[e, part] = maps[e][part].astype(bf16)
    write_message(message_ref, maps)


def make_rows(energies, hop, overall, share, modes_ref, levels_ref, params_ref, link2_ref, left_ref, local_ref, free_ref):
    group = lax.axis_index("energy")
    first = jnp.bitwise_xor(group, hop) * energies
    link2 = link2_ref[...]
    modes = modes_ref[0]
    modes_f = modes.astype(f32)
    mine = pl.multiple_of(group * share, share)
    rows_f = modes_ref[0, pl.ds(mine, share), :].astype(f32)
    for e in range(energies):
        dr, di = resolvents(overall, first, e, levels_ref, params_ref)
        free_re = dot_last((modes_f * dr).astype(bf16), modes)
        free_im = dot_last((modes_f * di).astype(bf16), modes)
        free = jnp.concatenate([free_re.astype(bf16), free_im.astype(bf16)], axis=1)
        if free_ref is not None:
            free_ref[e] = free
        left_ref[e] = dot_last(free, link2).astype(bf16)
        weight = params_ref[2, e : e + 1, :]
        own = dot_last(jnp.concatenate([rows_f * dr, rows_f * di], axis=0).astype(bf16), modes) * weight
        own_re, own_im = own[:share], own[share:]
        own = jnp.concatenate(
            [jnp.concatenate([own_re, own_im], axis=1), jnp.concatenate([own_im, -own_re], axis=1)], axis=0
        )
        local = dot_last(own.astype(bf16), free)
        local_ref[e, 0] = local[:share].astype(bf16)
        local_ref[e, 1] = local[share:].astype(bf16)


def front_kernel(
    interface_ref,
    mask_hbm,
    modes_hbm,
    levels_hbm,
    coupling_hbm,
    shift_hbm,
    broad_hbm,
    inject_hbm,
    block_ref,
    link2_ref,
    modes_ref,
    levels_ref,
    params_ref,
    mask_ref,
    coupling_ref,
    sems,
):
    copies = [
        pltpu.make_async_copy(source, target, sems.at[index])
        for index, (source, target) in enumerate(
            (
                (mask_hbm, mask_ref),
                (coupling_hbm, coupling_ref),
                (shift_hbm, params_ref.at[0, 0:1]),
                (broad_hbm, params_ref.at[0, 1:2]),
                (inject_hbm, params_ref.at[0, 2:3]),
                (levels_hbm, levels_ref),
                (modes_hbm, modes_ref),
            )
        )
    ]
    for copy in copies:
        copy.start()
    for copy in copies:
        copy.wait()
    block_ref[...] = jnp.full(block_ref.shape, interface_ref[0].astype(f32))
    masked_link(link2_ref, coupling_ref, mask_ref)


def own_rows_kernel(overall, share, modes_ref, levels_ref, link2_ref, params_ref, left_ref, local_ref, free_ref):
    make_rows(
        params_ref.shape[2],
        0,
        overall,
        share,
        modes_ref,
        levels_ref,
        params_ref.at[0],
        link2_ref,
        left_ref,
        local_ref,
        free_ref,
    )


def rows_kernel(overall, share, hop, slot, modes_ref, levels_ref, link2_ref, got_ref, *rest):
    if len(rest) > 2:
        had_ref, left_ref, local_ref, both_ref = rest
        count = had_ref.shape[0]
        both_ref[0:count] = had_ref[...]
        both_ref[count:] = got_ref[...]
    else:
        left_ref, local_ref = rest
    make_rows(
        got_ref.shape[2],
        hop,
        overall,
        share,
        modes_ref,
        levels_ref,
        got_ref.at[slot],
        link2_ref,
        left_ref,
        local_ref,
        None,
    )


spare = 16


def places(extent, width):
    row = lax.broadcasted_iota(jnp.int32, (extent, width), 0)
    lane = lax.broadcasted_iota(jnp.int32, (extent, width), 1)
    return row, jnp.where(lane < extent, lane, lane - extent), lane < extent


def pack_lesser(first, second):
    _, _, low = places(*first.shape)
    return jnp.where(low, first + swap_halves(first), second + swap_halves(second))


def with_turned(x):
    square = jnp.concatenate([x, swap_halves(x)], axis=0)
    return square, square.T


def unpack_lesser(packed):
    packed = packed.astype(f32)
    extent, width = packed.shape
    _, _, low = places(extent, width)
    square, turned = with_turned(packed)
    total, change = 0.5 * (square + turned), 0.5 * (square - turned)
    return (
        jnp.where(low, total[:extent], change[extent:]),
        jnp.where(low, total[extent:], change[:extent]),
    )


def pack_retarded(first, second):
    row, column, _ = places(*first.shape)
    diagonal = jnp.sum(jnp.where(row == column, second, 0.0), axis=0, keepdims=True)
    return jnp.where(row <= column, first, second), jnp.broadcast_to(diagonal, (spare, first.shape[1]))


def unpack_retarded(packed, diagonal):
    packed, diagonal = packed.astype(f32), diagonal.astype(f32)
    extent, width = packed.shape
    row, column, _ = places(extent, width)
    turned = with_turned(packed)[1][:extent]
    return (
        jnp.where(row <= column, packed, turned),
        jnp.where(row > column, packed, jnp.where(row == column, diagonal, turned)),
    )


def write_message(ref, maps):
    extent = maps[0][-1].shape[0]
    for pair in range(ref.shape[0]):
        first, second = maps[2 * pair], maps[2 * pair + 1]
        shared, diagonal = pack_retarded(first[-2], second[-2])
        ref[pair, 0:extent] = shared.astype(bf16)
        ref[pair, extent : 2 * extent] = pack_lesser(first[-1], second[-1]).astype(bf16)
        ref[pair, 2 * extent : 2 * extent + spare] = diagonal.astype(bf16)
        if ref.shape[1] > 2 * extent + spare:
            ref[pair, 2 * extent + spare : 3 * extent + spare] = first[0].astype(bf16)
            ref[pair, 3 * extent + spare :] = second[0].astype(bf16)


def read_message(ref):
    extent = ref.shape[2] // 2
    maps = []
    for pair in range(ref.shape[0]):
        retarded = unpack_retarded(ref[pair, 0:extent], ref[pair, 2 * extent : 2 * extent + 1])
        lesser = unpack_lesser(ref[pair, extent : 2 * extent])
        for which in range(2):
            start = (2 + which) * extent + spare
            front = (ref[pair, start : start + extent],) if ref.shape[1] > 2 * extent + spare else ()
            maps.append(front + (retarded[which].astype(bf16), lesser[which].astype(bf16)))
    return maps


def pushed(step, state):
    first = dot_mat(step[0], jnp.concatenate([full(state[0]), full(state[1])], axis=1)).astype(bf16)
    width = step[0].shape[1]
    return (
        dot_last(first[:, :width], full_conj(step[0])),
        dot_last(first[:, width:], full(step[0])),
    )


def compose(earlier, latter):
    retarded, lesser = pushed(latter, earlier[1:])
    return (
        dot_mat(latter[0], full(earlier[0])),
        latter[1].astype(f32) + retarded,
        latter[2].astype(f32) + lesser,
    )


def pick(flag, yes, no):
    return tuple(jnp.where(flag, a, b) for a, b in zip(yes, no))


def neutral(extent, width):
    row = lax.broadcasted_iota(jnp.int32, (extent, width), 0)
    lane = lax.broadcasted_iota(jnp.int32, (extent, width), 1)
    zero = jnp.zeros((extent, width), f32)
    return (jnp.where(row == lane, 1.0, 0.0).astype(bf16), zero.astype(bf16), zero.astype(bf16))


def read(ref, e):
    return tuple(ref[e, part] for part in range(ref.shape[1]))


def join_kernel(level, *refs):
    total_ref, other_ref = refs[:2]
    enter_ref = refs[2] if level else None
    outs = refs[3 if level else 2 :]
    new_enter_ref, message_ref = outs[:2]
    energies, _, extent, width = total_ref.shape
    place = lax.axis_index("cell")
    upper = jnp.bitwise_and(jnp.right_shift(place, level), 1) == 1
    others = read_message(other_ref)
    joined = []
    for e in range(energies):
        total, other = read(total_ref, e), others[e]
        joined.append(compose(pick(upper, other, total), pick(upper, total, other)))
        if level:
            enter = read(enter_ref, e)
            longer = compose(other, enter)
            longer = tuple(x.astype(bf16) for x in longer)
            enter = pick(upper, longer, enter)
        else:
            enter = pick(upper, other, neutral(extent, width))
        for part in range(3):
            new_enter_ref[e, part] = enter[part]
            if len(outs) > 2:
                outs[2][e, part] = joined[e][part].astype(bf16)
    write_message(message_ref, joined)


def arrive_kernel(level, enter_ref, state_ref, retarded_ref, lesser_ref):
    upper = jnp.right_shift(lax.axis_index("cell"), level) == 1
    states = read_message(state_ref)
    lessers = []
    for e in range(enter_ref.shape[0]):
        enter = read(enter_ref, e)
        state = pick(upper, states[e], (jnp.zeros_like(enter[1]), jnp.zeros_like(enter[2])))
        retarded, lesser = pushed(enter, state)
        retarded_ref[e] = (enter[1].astype(f32) + retarded).astype(bf16)
        lessers.append(enter[2].astype(f32) + lesser)
    for pair in range(lesser_ref.shape[0]):
        lesser_ref[pair] = pack_lesser(lessers[2 * pair], lessers[2 * pair + 1]).astype(bf16)


def row_sums(x):
    return dot_last(jnp.ones((8, x.shape[1]), bf16), x.astype(bf16))[0:1]


def diagonal_kernel(overall, modes_ref, levels_ref, params_ref, out_ref):
    energies = params_ref.shape[2]
    first = lax.axis_index("energy") * energies
    modes = modes_ref[0].astype(f32)
    for e in range(energies):
        _, di = resolvents(overall, first, e, levels_ref, params_ref.at[0])
        out_ref[0, e : e + 1, :] = row_sums(modes * (modes * di).astype(bf16).astype(f32))


def density_kernel(diagonal_ref, left_ref, retarded_ref, out_ref):
    for e in range(left_ref.shape[0]):
        left = left_ref[e]
        pz = dot_mat(left, full(retarded_ref[e])).astype(bf16).astype(f32)
        total = diagonal_ref[0, e : e + 1, :] + row_sums(pz * swap_halves(left.astype(f32)))
        out_ref[0, e : e + 1, :] = -total / math.pi


def convolve_kernel(groups, reach, offsets_hbm, screen_ref, *refs):
    lefts, locals_, lessers = refs[:groups], refs[groups : 2 * groups], refs[2 * groups : 3 * groups]
    out_hbm, g_re, g_im, g_sum, out_ref, offsets_ref, sem, out_sems = refs[3 * groups :]
    copy = pltpu.make_async_copy(offsets_hbm, offsets_ref, sem)
    copy.start()
    energies = lefts[0].shape[0]
    overall = energies * groups
    share, width = out_ref.shape[3:]
    group = lax.axis_index("energy")
    mine = pl.multiple_of(group * share, share)
    blank = jnp.zeros((share, width), f32)
    for e in range(reach):
        for g in (g_re, g_im, g_sum):
            g[e] = blank
            g[overall + reach + e] = blank
    for hop in range(groups):
        base = jnp.bitwise_xor(group, hop) * energies + reach
        for pair in range(energies // 2):
            states = unpack_lesser(lessers[hop][pair])
            for e in (2 * pair, 2 * pair + 1):
                left = lefts[hop][e]
                own = lefts[hop][e, pl.ds(mine, share), :]
                pl_hat = dot_mat(own, full(states[e - 2 * pair]))
                turned = swap_halves(pl_hat) * signs(pl_hat.shape[1], 1.0)
                chain = dot_last(jnp.concatenate([pl_hat, turned], axis=0).astype(bf16), left)
                re = chain[:share] + locals_[hop][e, 0].astype(f32)
                im = chain[share:] + locals_[hop][e, 1].astype(f32)
                g_re[base + e] = re
                g_im[base + e] = im
                g_sum[base + e] = re + im
    copy.wait()
    points = screen_ref.shape[2]
    lanes, height, batch = 128, 16, min(8, overall)

    def out_copy(step):
        rows = pl.ds(pl.multiple_of(step * height, height), height)
        return pltpu.make_async_copy(
            out_ref.at[:, :, :, rows, :], out_hbm.at[:, :, :, rows, :], out_sems.at[step]
        )

    def rows_of(step, _):
        top = pl.multiple_of(step * height, height)
        for lane in range(0, width, lanes):
            for e0 in range(0, overall, batch):
                sums = [None] * batch
                for k in range(points):
                    start = e0 + reach - offsets_ref[k]
                    w_re = screen_ref[0, 0, k, pl.ds(top, height), lane : lane + lanes].astype(f32)
                    w_im = screen_ref[0, 1, k, pl.ds(top, height), lane : lane + lanes].astype(f32)
                    w_sum, w_change = w_re + w_im, w_im - w_re
                    for e in range(batch):
                        new = tuple(
                            w * g[start + e, pl.ds(top, height), lane : lane + lanes]
                            for w, g in ((w_re, g_sum), (w_sum, g_im), (w_change, g_re))
                        )
                        sums[e] = new if k == 0 else tuple(a + b for a, b in zip(sums[e], new))
                for e in range(batch):
                    common, first, second = sums[e]
                    where = (e0 + e, pl.ds(top, height), slice(lane, lane + lanes))
                    out_ref[(0, 0) + where] = (-(common + second)).astype(bf16)
                    out_ref[(0, 1) + where] = (common - first).astype(bf16)
        out_copy(step).start()
        return 0

    steps = share // height
    lax.fori_loop(0, steps, rows_of, 0)
    for step in range(steps):
        out_copy(step).wait()


def in_hbm(x):
    return pltpu.with_memory_space_constraint(x, pltpu.HBM)


def call(kernel, out_shape, in_specs, scratch=(), flops=1_000_000, size=1_000_000, out_specs=None):
    outs = out_specs or jax.tree.map(lambda _: VMEM, out_shape)
    return pl.pallas_call(
        kernel,
        out_shape=out_shape,
        in_specs=in_specs,
        out_specs=outs,
        scratch_shapes=list(scratch),
        compiler_params=pltpu.CompilerParams(vmem_limit_bytes=16 << 20),
        cost_estimate=pl.CostEstimate(flops=flops, bytes_accessed=size, transcendentals=0),
    )


def body(
    modes,
    levels,
    level_shift,
    broadening,
    injection,
    coupling,
    row_mask,
    interface,
    screened,
    offsets,
):
    cells = lax.axis_size("cell")
    groups = lax.axis_size("energy")
    rounds = cells.bit_length() - 1
    assert cells == 1 << rounds and groups & (groups - 1) == 0
    energies = level_shift.shape[1]
    overall = energies * groups
    orbitals, extent = coupling.shape[1:]
    width = 2 * extent
    share = orbitals // groups
    sds = jax.ShapeDtypeStruct

    def swapped(x, axis, distance):
        return lax.ppermute(x, axis, [(i, i ^ distance) for i in range(lax.axis_size(axis))])

    assert energies % 2 == 0
    pairs = energies // 2
    maps_shape = sds((energies, 3, extent, width), bf16)
    message = sds((pairs, 4 * extent + spare, width), bf16)
    state_message = sds((pairs, 2 * extent + spare, width), bf16)
    coupling = jnp.swapaxes(coupling, 1, 2)
    block, link2, modes, levels, params = call(
        front_kernel,
        (
            sds((8, width), f32),
            sds((width, 2 * orbitals), bf16),
            sds(modes.shape, bf16),
            sds(levels.shape, f32),
            sds((1, 3, energies, orbitals), f32),
        ),
        [SMEM] + [HBM] * 7,
        [
            pltpu.SMEM(row_mask.shape, jnp.int32),
            pltpu.VMEM(coupling.shape, bf16),
            pltpu.SemaphoreType.DMA((7,)),
        ],
    )(interface, *map(in_hbm, (row_mask, modes, levels, coupling, level_shift, broadening, injection)))
    one = swapped(block, "cell", 1)
    near = [(i, i + 1) for i in range(1, cells - 1, 2)]
    two = lax.ppermute(block, "cell", near + [(j, i) for i, j in near])

    left_shape = sds((energies, orbitals, width), bf16)
    local_shape = sds((energies, 2, share, orbitals), bf16)
    params_shape = (3, energies, orbitals)
    left, local, free = call(
        partial(own_rows_kernel, overall, share),
        (left_shape, local_shape, sds((energies, orbitals, 2 * orbitals), bf16)),
        [VMEM] * 4,
    )(modes, levels, link2, params)
    lefts, locals_ = [left], [local]

    total, sent = call(
        partial(maps_kernel, overall),
        (maps_shape, message),
        [VMEM] * 7,
    )(one, two, modes, levels, params, left, free)
    diagonal = call(
        partial(diagonal_kernel, overall), sds((1, energies, orbitals), f32), [VMEM] * 3
    )(modes, levels, params)

    known = params
    while known.shape[0] < groups:
        count = known.shape[0]
        got = swapped(known, "energy", count)
        more = 2 * count < groups
        for slot in range(count):
            outs, given = (left_shape, local_shape), (modes, levels, link2, got)
            if slot == 0 and more:
                outs, given = outs + (sds((2 * count,) + params_shape, f32),), given + (known,)
            left, local, *rest = call(
                partial(rows_kernel, overall, share, count + slot, slot), outs, [VMEM] * len(given)
            )(*given)
            lefts.append(left)
            locals_.append(local)
            if rest:
                both = rest[0]
        if not more:
            break
        known = both

    enter = None
    for level in range(rounds - 1):
        other = swapped(sent, "cell", 1 << level)
        outs = (maps_shape, message, maps_shape) if level < rounds - 2 else (maps_shape, state_message)
        given = [total, other] + ([enter] if level else [])
        enter, sent, *rest = call(partial(join_kernel, level), outs, [VMEM] * len(given))(*given)
        total = rest[0] if rest else None
    state = swapped(sent, "cell", cells // 2)
    retarded, lesser = call(
        partial(arrive_kernel, rounds - 1),
        (sds((energies, extent, width), bf16), sds((pairs, extent, width), bf16)),
        [VMEM, VMEM],
    )(enter, state)

    lessers = [lesser]
    for hop in range(1, groups):
        lessers.append(swapped(lesser, "energy", hop))
    density = call(density_kernel, sds((1, energies, orbitals), f32), [VMEM] * 3)(
        diagonal, lefts[0], retarded
    )

    reach = overall // 4
    spread = pltpu.VMEM((overall + 2 * reach, share, orbitals), f32)
    out_shape = (1, 2, overall, share, orbitals)
    sigma = call(
        partial(convolve_kernel, groups, reach),
        sds(out_shape, bf16),
        [HBM, VMEM] + [VMEM] * (3 * groups),
        [
            spread,
            spread,
            spread,
            pltpu.VMEM(out_shape, bf16),
            pltpu.SMEM(offsets.shape, jnp.int32),
            pltpu.SemaphoreType.DMA,
            pltpu.SemaphoreType.DMA((share // 16,)),
        ],
        out_specs=HBM,
    )(in_hbm(offsets), screened, *lefts, *locals_, *lessers)
    return (density, sigma)


def solution(mesh):
    placed = (
        P("cell", None, None),
        P("cell", None),
        P("cell", "energy", None),
        P("cell", "energy", None),
        P("cell", "energy", None),
        P("cell", None, None),
        P("cell", None),
        P("cell"),
        P("cell", None, None, "energy", None),
        P(),
    )
    return jax.shard_map(
        body,
        mesh=mesh,
        in_specs=placed,
        out_specs=(P("cell", "energy", None), P("cell", None, None, "energy", None)),
        check_vma=False,
    )
```

```python
from functools import partial
import math

import jax
import jax.numpy as jnp
from jax import lax
from jax.experimental import pallas as pl
from jax.experimental.pallas import tpu as pltpu
from jax.sharding import PartitionSpec as P


broaden_base = 1.0
energy_low = -0.25
energy_span = 0.5
f32 = jnp.float32
bf16 = jnp.bfloat16

VMEM = pl.BlockSpec(memory_space=pltpu.VMEM)
SMEM = pl.BlockSpec(memory_space=pltpu.SMEM)
HBM = pl.BlockSpec(memory_space=pltpu.HBM)


def dot_last(a, b, precision=None):
    return lax.dot_general(
        a, b, (((1,), (1,)), ((), ())), precision=precision, preferred_element_type=f32
    )


def dot_mat(a, b):
    return lax.dot_general(a, b, (((1,), (0,)), ((), ())), preferred_element_type=f32)


def signs(width, left_sign):
    lane = lax.broadcasted_iota(jnp.int32, (1, width), 1)
    return jnp.where(lane < width // 2, left_sign, -left_sign).astype(f32)


def swap_halves(x):
    return pltpu.roll(x, x.shape[1] // 2, 1)


def full(x):
    x = x.astype(f32)
    return jnp.concatenate([x, swap_halves(x) * signs(x.shape[1], -1.0)], axis=0).astype(bf16)


def full_conj(x):
    x = x.astype(f32)
    return jnp.concatenate([x * signs(x.shape[1], 1.0), swap_halves(x)], axis=0).astype(bf16)


def resolvent(levels, shift, broad, index, overall):
    eps = energy_low + energy_span * (index.astype(f32) + 0.5) / overall
    detune = eps - levels - shift
    damping = broaden_base + broad
    inverse = 1.0 / (detune * detune + damping * damping)
    return detune * inverse, -damping * inverse


def masked_link(link2_ref, coupling_ref, mask_ref):
    extent, rows = coupling_ref.shape[1:]
    count = mask_ref.shape[1]
    block = lax.broadcasted_iota(jnp.int32, (1, rows), 1) // (rows // count)
    keep = jnp.zeros((1, rows), f32)
    for index in range(count):
        keep = jnp.where(block == index, mask_ref[0, index].astype(f32), keep)
    link = (coupling_ref[0].astype(f32) * keep).astype(bf16)
    none = jnp.zeros_like(link)
    link2_ref[0:extent, 0:rows] = link
    link2_ref[0:extent, rows:] = none
    link2_ref[extent:, 0:rows] = none
    link2_ref[extent:, rows:] = link


def resolvents(overall, first, e, levels_ref, params_ref):
    return resolvent(levels_ref[...], params_ref[0, e : e + 1, :], params_ref[1, e : e + 1, :], first + e, overall)


def own_maps(overall, block_ref, modes_ref, levels_ref, params_ref, left_ref, free_ref):
    energies, _, width = left_ref.shape
    extent = width // 2
    first = lax.axis_index("energy") * energies
    block = jnp.max(block_ref[...]).astype(jnp.int32)
    chosen = pl.multiple_of(block * extent, extent)
    rows = modes_ref[0, pl.ds(chosen, extent), :]
    width = rows.shape[1]
    rows_f = rows.astype(f32)
    none = jnp.zeros_like(rows)
    rows2 = jnp.concatenate(
        [jnp.concatenate([rows, none], axis=1), jnp.concatenate([none, rows], axis=1)], axis=0
    )
    maps = []
    for e in range(energies):
        dr, di = resolvents(overall, first, e, levels_ref, params_ref.at[0])
        scaled = jnp.concatenate([(rows_f * dr).astype(bf16), (rows_f * di).astype(bf16)], axis=1)
        free = free_ref[e, pl.ds(chosen, extent), :]
        free_f = free.astype(f32)
        weight = params_ref[0, 2, e : e + 1, :]
        weighted = jnp.concatenate([free_f[:, :width] * weight, free_f[:, width:] * weight], axis=1)
        turned = jnp.concatenate([-free_f[:, width:], free_f[:, :width]], axis=1)
        maps.append(
            (
                left_ref[e, pl.ds(chosen, extent), :],
                dot_last(scaled, rows2),
                dot_last(weighted.astype(bf16), jnp.concatenate([free, turned.astype(bf16)], axis=0)),
            )
        )
    return maps


def maps_kernel(overall, block_ref, modes_ref, levels_ref, params_ref, left_ref, free_ref, message_ref):
    write_message(
        message_ref, own_maps(overall, block_ref, modes_ref, levels_ref, params_ref, left_ref, free_ref)
    )


def make_rows(energies, hop, overall, share, modes_ref, levels_ref, params_ref, link2_ref, left_ref, local_ref, free_ref):
    group = lax.axis_index("energy")
    first = jnp.bitwise_xor(group, hop) * energies
    link2 = link2_ref[...]
    modes = modes_ref[0]
    modes_f = modes.astype(f32)
    mine = pl.multiple_of(group * share, share)
    rows_f = modes_ref[0, pl.ds(mine, share), :].astype(f32)
    for e in range(energies):
        dr, di = resolvents(overall, first, e, levels_ref, params_ref)
        free_re = dot_last((modes_f * dr).astype(bf16), modes)
        free_im = dot_last((modes_f * di).astype(bf16), modes)
        free = jnp.concatenate([free_re.astype(bf16), free_im.astype(bf16)], axis=1)
        if free_ref is not None:
            free_ref[e] = free
        left_ref[e] = dot_last(free, link2).astype(bf16)
        weight = params_ref[2, e : e + 1, :]
        own = dot_last(jnp.concatenate([rows_f * dr, rows_f * di], axis=0).astype(bf16), modes) * weight
        own_re, own_im = own[:share], own[share:]
        own = jnp.concatenate(
            [jnp.concatenate([own_re, own_im], axis=1), jnp.concatenate([own_im, -own_re], axis=1)], axis=0
        )
        local = dot_last(own.astype(bf16), free)
        local_ref[e, 0] = local[:share].astype(bf16)
        local_ref[e, 1] = local[share:].astype(bf16)


def front_kernel(
    interface_ref,
    mask_hbm,
    modes_hbm,
    levels_hbm,
    coupling_hbm,
    shift_hbm,
    broad_hbm,
    inject_hbm,
    block_ref,
    link2_ref,
    modes_ref,
    levels_ref,
    params_ref,
    mask_ref,
    coupling_ref,
    sems,
):
    copies = [
        pltpu.make_async_copy(source, target, sems.at[index])
        for index, (source, target) in enumerate(
            (
                (mask_hbm, mask_ref),
                (coupling_hbm, coupling_ref),
                (shift_hbm, params_ref.at[0, 0:1]),
                (broad_hbm, params_ref.at[0, 1:2]),
                (inject_hbm, params_ref.at[0, 2:3]),
                (levels_hbm, levels_ref),
                (modes_hbm, modes_ref),
            )
        )
    ]
    for copy in copies:
        copy.start()
    for copy in copies:
        copy.wait()
    block_ref[...] = jnp.full(block_ref.shape, interface_ref[0].astype(f32))
    masked_link(link2_ref, coupling_ref, mask_ref)


def own_rows_kernel(overall, share, modes_ref, levels_ref, link2_ref, params_ref, left_ref, local_ref, free_ref):
    make_rows(
        params_ref.shape[2],
        0,
        overall,
        share,
        modes_ref,
        levels_ref,
        params_ref.at[0],
        link2_ref,
        left_ref,
        local_ref,
        free_ref,
    )


def rows_kernel(overall, share, hop, slot, modes_ref, levels_ref, link2_ref, got_ref, *rest):
    if len(rest) > 2:
        had_ref, left_ref, local_ref, both_ref = rest
        count = had_ref.shape[0]
        both_ref[0:count] = had_ref[...]
        both_ref[count:] = got_ref[...]
    else:
        left_ref, local_ref = rest
    make_rows(
        got_ref.shape[2],
        hop,
        overall,
        share,
        modes_ref,
        levels_ref,
        got_ref.at[slot],
        link2_ref,
        left_ref,
        local_ref,
        None,
    )


spare = 16


def places(extent, width):
    row = lax.broadcasted_iota(jnp.int32, (extent, width), 0)
    lane = lax.broadcasted_iota(jnp.int32, (extent, width), 1)
    return row, jnp.where(lane < extent, lane, lane - extent), lane < extent


def pack_lesser(first, second):
    _, _, low = places(*first.shape)
    return jnp.where(low, first + swap_halves(first), second + swap_halves(second))


def with_turned(x):
    square = jnp.concatenate([x, swap_halves(x)], axis=0)
    return square, square.T


def unpack_lesser(packed):
    packed = packed.astype(f32)
    extent, width = packed.shape
    _, _, low = places(extent, width)
    square, turned = with_turned(packed)
    total, change = 0.5 * (square + turned), 0.5 * (square - turned)
    return (
        jnp.where(low, total[:extent], change[extent:]),
        jnp.where(low, total[extent:], change[:extent]),
    )


def pack_retarded(first, second):
    row, column, _ = places(*first.shape)
    diagonal = jnp.sum(jnp.where(row == column, second, 0.0), axis=0, keepdims=True)
    return jnp.where(row <= column, first, second), jnp.broadcast_to(diagonal, (spare, first.shape[1]))


def unpack_retarded(packed, diagonal):
    packed, diagonal = packed.astype(f32), diagonal.astype(f32)
    extent, width = packed.shape
    row, column, _ = places(extent, width)
    turned = with_turned(packed)[1][:extent]
    return (
        jnp.where(row <= column, packed, turned),
        jnp.where(row > column, packed, jnp.where(row == column, diagonal, turned)),
    )


def write_message(ref, maps):
    extent = maps[0][-1].shape[0]
    for pair in range(ref.shape[0]):
        first, second = maps[2 * pair], maps[2 * pair + 1]
        shared, diagonal = pack_retarded(first[-2], second[-2])
        ref[pair, 0:extent] = shared.astype(bf16)
        ref[pair, extent : 2 * extent] = pack_lesser(first[-1], second[-1]).astype(bf16)
        ref[pair, 2 * extent : 2 * extent + spare] = diagonal.astype(bf16)
        if ref.shape[1] > 2 * extent + spare:
            ref[pair, 2 * extent + spare : 3 * extent + spare] = first[0].astype(bf16)
            ref[pair, 3 * extent + spare :] = second[0].astype(bf16)


def read_message(ref):
    extent = ref.shape[2] // 2
    maps = []
    for pair in range(ref.shape[0]):
        retarded = unpack_retarded(ref[pair, 0:extent], ref[pair, 2 * extent : 2 * extent + 1])
        lesser = unpack_lesser(ref[pair, extent : 2 * extent])
        for which in range(2):
            start = (2 + which) * extent + spare
            front = (ref[pair, start : start + extent],) if ref.shape[1] > 2 * extent + spare else ()
            maps.append(front + (retarded[which].astype(bf16), lesser[which].astype(bf16)))
    return maps


def pushed(step, state):
    first = dot_mat(step[0], jnp.concatenate([full(state[0]), full(state[1])], axis=1)).astype(bf16)
    width = step[0].shape[1]
    return (
        dot_last(first[:, :width], full_conj(step[0])),
        dot_last(first[:, width:], full(step[0])),
    )


def compose(earlier, latter):
    retarded, lesser = pushed(latter, earlier[1:])
    return (
        dot_mat(latter[0], full(earlier[0])),
        latter[1].astype(f32) + retarded,
        latter[2].astype(f32) + lesser,
    )


def join_kernel(
    overall, block_ref, modes_ref, levels_ref, params_ref, left_ref, free_ref, other_ref, even_ref, *outs
):
    latter = own_maps(overall, block_ref, modes_ref, levels_ref, params_ref, left_ref, free_ref)
    earlier = read_message(other_ref)
    joined = []
    for e in range(len(latter)):
        joined.append(compose(earlier[e], latter[e]))
        for part in range(3):
            even_ref[e, part] = earlier[e][part]
    for out in outs:
        write_message(out, joined)


def arrive_kernel(count, even_ref, *refs):
    hops, (keep_ref, hand_ref, retarded_ref) = refs[:count], refs[count:]
    energies, _, extent, width = even_ref.shape
    if hops:
        states = [x[-2:] for x in read_message(hops[-1])]
        for hop in reversed(hops[:-1]):
            maps = read_message(hop)
            states = [moved(maps[e], states[e]) for e in range(energies)]
    else:
        states = [(jnp.zeros((extent, width), f32),) * 2] * energies
    nexts = [moved(tuple(even_ref[e, part] for part in range(3)), states[e]) for e in range(energies)]
    states = [tuple(x.astype(f32) for x in state) for state in states]
    write_message(hand_ref, states)
    for pair in range(keep_ref.shape[0]):
        e = 2 * pair
        keep_ref[pair, 0:extent] = pack_lesser(states[e][1], states[e + 1][1]).astype(bf16)
        keep_ref[pair, extent:] = pack_lesser(nexts[e][1], nexts[e + 1][1]).astype(bf16)
    for e in range(energies):
        retarded_ref[e] = nexts[e][0].astype(bf16)


def moved(step, state):
    retarded, lesser = pushed(step, state)
    return step[1].astype(f32) + retarded, step[2].astype(f32) + lesser


def is_odd():
    return jnp.bitwise_and(lax.axis_index("cell"), 1) == 1


def row_sums(x):
    return dot_last(jnp.ones((8, x.shape[1]), bf16), x.astype(bf16))[0:1]


def diagonal_kernel(overall, modes_ref, levels_ref, params_ref, out_ref):
    energies = params_ref.shape[2]
    first = lax.axis_index("energy") * energies
    modes = modes_ref[0].astype(f32)
    for e in range(energies):
        _, di = resolvents(overall, first, e, levels_ref, params_ref.at[0])
        out_ref[0, e : e + 1, :] = row_sums(modes * (modes * di).astype(bf16).astype(f32))


def density_kernel(diagonal_ref, left_ref, retarded_ref, hand_ref, out_ref):
    odd = is_odd()
    given = read_message(hand_ref)
    for e in range(left_ref.shape[0]):
        left = left_ref[e]
        state = jnp.where(odd, retarded_ref[e], given[e][0])
        pz = dot_mat(left, full(state)).astype(bf16).astype(f32)
        total = diagonal_ref[0, e : e + 1, :] + row_sums(pz * swap_halves(left.astype(f32)))
        out_ref[0, e : e + 1, :] = -total / math.pi


def convolve_kernel(groups, reach, offsets_hbm, screen_ref, *refs):
    lefts, locals_, kept, given = (refs[part * groups : (part + 1) * groups] for part in range(4))
    out_hbm, g_re, g_im, g_sum, out_ref, offsets_ref, sem, out_sems = refs[4 * groups :]
    odd = is_odd()
    extent = lefts[0].shape[2] // 2
    copy = pltpu.make_async_copy(offsets_hbm, offsets_ref, sem)
    copy.start()
    energies = lefts[0].shape[0]
    overall = energies * groups
    share, width = out_ref.shape[3:]
    group = lax.axis_index("energy")
    mine = pl.multiple_of(group * share, share)
    blank = jnp.zeros((share, width), f32)
    for e in range(reach):
        for g in (g_re, g_im, g_sum):
            g[e] = blank
            g[overall + reach + e] = blank
    for hop in range(groups):
        base = jnp.bitwise_xor(group, hop) * energies + reach
        for pair in range(energies // 2):
            start = 0 if hop else extent
            states = unpack_lesser(
                jnp.where(odd, kept[hop][pair, extent : 2 * extent], given[hop][pair, start : start + extent])
            )
            for e in (2 * pair, 2 * pair + 1):
                left = lefts[hop][e]
                own = lefts[hop][e, pl.ds(mine, share), :]
                pl_hat = dot_mat(own, full(states[e - 2 * pair]))
                turned = swap_halves(pl_hat) * signs(pl_hat.shape[1], 1.0)
                chain = dot_last(jnp.concatenate([pl_hat, turned], axis=0).astype(bf16), left)
                re = chain[:share] + locals_[hop][e, 0].astype(f32)
                im = chain[share:] + locals_[hop][e, 1].astype(f32)
                g_re[base + e] = re
                g_im[base + e] = im
                g_sum[base + e] = re + im
    copy.wait()
    points = screen_ref.shape[2]
    lanes, height, batch = 128, 16, min(8, overall)

    def out_copy(step):
        rows = pl.ds(pl.multiple_of(step * height, height), height)
        return pltpu.make_async_copy(
            out_ref.at[:, :, :, rows, :], out_hbm.at[:, :, :, rows, :], out_sems.at[step]
        )

    def rows_of(step, _):
        top = pl.multiple_of(step * height, height)
        for lane in range(0, width, lanes):
            for e0 in range(0, overall, batch):
                sums = [None] * batch
                for k in range(points):
                    start = e0 + reach - offsets_ref[k]
                    w_re = screen_ref[0, 0, k, pl.ds(top, height), lane : lane + lanes].astype(f32)
                    w_im = screen_ref[0, 1, k, pl.ds(top, height), lane : lane + lanes].astype(f32)
                    w_sum, w_change = w_re + w_im, w_im - w_re
                    for e in range(batch):
                        new = tuple(
                            w * g[start + e, pl.ds(top, height), lane : lane + lanes]
                            for w, g in ((w_re, g_sum), (w_sum, g_im), (w_change, g_re))
                        )
                        sums[e] = new if k == 0 else tuple(a + b for a, b in zip(sums[e], new))
                for e in range(batch):
                    common, first, second = sums[e]
                    where = (e0 + e, pl.ds(top, height), slice(lane, lane + lanes))
                    out_ref[(0, 0) + where] = (-(common + second)).astype(bf16)
                    out_ref[(0, 1) + where] = (common - first).astype(bf16)
        out_copy(step).start()
        return 0

    steps = share // height
    lax.fori_loop(0, steps, rows_of, 0)
    for step in range(steps):
        out_copy(step).wait()


def in_hbm(x):
    return pltpu.with_memory_space_constraint(x, pltpu.HBM)


def call(kernel, out_shape, in_specs, scratch=(), flops=1_000_000, size=1_000_000, out_specs=None):
    outs = out_specs or jax.tree.map(lambda _: VMEM, out_shape)
    return pl.pallas_call(
        kernel,
        out_shape=out_shape,
        in_specs=in_specs,
        out_specs=outs,
        scratch_shapes=list(scratch),
        compiler_params=pltpu.CompilerParams(vmem_limit_bytes=16 << 20),
        cost_estimate=pl.CostEstimate(flops=flops, bytes_accessed=size, transcendentals=0),
    )


def body(
    modes,
    levels,
    level_shift,
    broadening,
    injection,
    coupling,
    row_mask,
    interface,
    screened,
    offsets,
):
    cells = lax.axis_size("cell")
    groups = lax.axis_size("energy")
    chips = cells // 2
    assert cells % 2 == 0 and groups & (groups - 1) == 0
    energies = level_shift.shape[1]
    overall = energies * groups
    orbitals, extent = coupling.shape[1:]
    width = 2 * extent
    share = orbitals // groups
    sds = jax.ShapeDtypeStruct

    def swapped(x, axis, distance):
        return lax.ppermute(x, axis, [(i, i ^ distance) for i in range(lax.axis_size(axis))])

    assert energies % 2 == 0
    pairs = energies // 2
    maps_shape = sds((energies, 3, extent, width), bf16)
    message = sds((pairs, 4 * extent + spare, width), bf16)
    state_message = sds((pairs, 2 * extent + spare, width), bf16)
    coupling = jnp.swapaxes(coupling, 1, 2)
    block, link2, modes, levels, params = call(
        front_kernel,
        (
            sds((8, width), f32),
            sds((width, 2 * orbitals), bf16),
            sds(modes.shape, bf16),
            sds(levels.shape, f32),
            sds((1, 3, energies, orbitals), f32),
        ),
        [SMEM] + [HBM] * 7,
        [
            pltpu.SMEM(row_mask.shape, jnp.int32),
            pltpu.VMEM(coupling.shape, bf16),
            pltpu.SemaphoreType.DMA((7,)),
        ],
    )(interface, *map(in_hbm, (row_mask, modes, levels, coupling, level_shift, broadening, injection)))
    odds = range(1, cells, 2)
    one = lax.ppermute(block, "cell", [(i, i - 1) for i in odds])
    two = lax.ppermute(block, "cell", [(i + 1, i) for i in odds if i + 1 < cells])

    left_shape = sds((energies, orbitals, width), bf16)
    local_shape = sds((energies, 2, share, orbitals), bf16)
    params_shape = (3, energies, orbitals)
    left, local, free = call(
        partial(own_rows_kernel, overall, share),
        (left_shape, local_shape, sds((energies, orbitals, 2 * orbitals), bf16)),
        [VMEM] * 4,
    )(modes, levels, link2, params)
    lefts, locals_ = [left], [local]

    sent = call(partial(maps_kernel, overall), message, [VMEM] * 6)(one, modes, levels, params, left, free)
    other = lax.ppermute(sent, "cell", [(i - 1, i) for i in odds])
    diagonal = call(
        partial(diagonal_kernel, overall), sds((1, energies, orbitals), f32), [VMEM] * 3
    )(modes, levels, params)

    known = params
    while known.shape[0] < groups:
        count = known.shape[0]
        got = swapped(known, "energy", count)
        more = 2 * count < groups
        for slot in range(count):
            outs, given = (left_shape, local_shape), (modes, levels, link2, got)
            if slot == 0 and more:
                outs, given = outs + (sds((2 * count,) + params_shape, f32),), given + (known,)
            left, local, *rest = call(
                partial(rows_kernel, overall, share, count + slot, slot), outs, [VMEM] * len(given)
            )(*given)
            lefts.append(left)
            locals_.append(local)
            if rest:
                both = rest[0]
        if not more:
            break
        known = both

    even, total, total_state = call(
        partial(join_kernel, overall), (maps_shape, message, state_message), [VMEM] * 7
    )(two, modes, levels, params, lefts[0], free, other)
    hops = []
    for hop in range(1, chips):
        route = [(i, i + 2 * hop) for i in odds if i + 2 * hop < cells]
        hops.append(lax.ppermute(total if hop < chips - 1 else total_state, "cell", route))
    keep, hand, retarded = call(
        partial(arrive_kernel, len(hops)),
        (
            sds((pairs, 2 * extent, width), bf16),
            state_message,
            sds((energies, extent, width), bf16),
        ),
        [VMEM] * (1 + len(hops)),
    )(even, *hops)

    def handed(x):
        return lax.ppermute(x, "cell", [(i, i - 1) for i in odds])

    kept = [keep]
    for hop in range(1, groups):
        route = [(i * groups + g, i * groups + (g ^ hop)) for i in odds for g in range(groups)]
        kept.append(lax.ppermute(keep, ("cell", "energy"), route))
    given = []
    for hop in range(groups):
        given.append(handed(kept[hop] if hop else hand))
    density = call(density_kernel, sds((1, energies, orbitals), f32), [VMEM] * 4)(
        diagonal, lefts[0], retarded, given[0]
    )

    reach = overall // 4
    spread = pltpu.VMEM((overall + 2 * reach, share, orbitals), f32)
    out_shape = (1, 2, overall, share, orbitals)
    sigma = call(
        partial(convolve_kernel, groups, reach),
        sds(out_shape, bf16),
        [HBM, VMEM] + [VMEM] * (4 * groups),
        [
            spread,
            spread,
            spread,
            pltpu.VMEM(out_shape, bf16),
            pltpu.SMEM(offsets.shape, jnp.int32),
            pltpu.SemaphoreType.DMA,
            pltpu.SemaphoreType.DMA((share // 16,)),
        ],
        out_specs=HBM,
    )(in_hbm(offsets), screened, *lefts, *locals_, *kept, *given)
    return (density, sigma)


def solution(mesh):
    placed = (
        P("cell", None, None),
        P("cell", None),
        P("cell", "energy", None),
        P("cell", "energy", None),
        P("cell", "energy", None),
        P("cell", None, None),
        P("cell", None),
        P("cell"),
        P("cell", None, None, "energy", None),
        P(),
    )
    return jax.shard_map(
        body,
        mesh=mesh,
        in_specs=placed,
        out_specs=(P("cell", "energy", None), P("cell", None, None, "energy", None)),
        check_vma=False,
    )
```

```python
from functools import partial
import math

import jax
import jax.numpy as jnp
from jax import lax
from jax.experimental import pallas as pl
from jax.experimental.pallas import tpu as pltpu
from jax.sharding import PartitionSpec as P


broaden_base = 1.0
energy_low = -0.25
energy_span = 0.5
f32 = jnp.float32
bf16 = jnp.bfloat16

VMEM = pl.BlockSpec(memory_space=pltpu.VMEM)
SMEM = pl.BlockSpec(memory_space=pltpu.SMEM)
HBM = pl.BlockSpec(memory_space=pltpu.HBM)


def dot_last(a, b, precision=None):
    return lax.dot_general(
        a, b, (((1,), (1,)), ((), ())), precision=precision, preferred_element_type=f32
    )


def dot_mat(a, b):
    return lax.dot_general(a, b, (((1,), (0,)), ((), ())), preferred_element_type=f32)


def signs(width, left_sign):
    lane = lax.broadcasted_iota(jnp.int32, (1, width), 1)
    return jnp.where(lane < width // 2, left_sign, -left_sign).astype(f32)


def swap_halves(x):
    return pltpu.roll(x, x.shape[1] // 2, 1)


def full(x):
    x = x.astype(f32)
    return jnp.concatenate([x, swap_halves(x) * signs(x.shape[1], -1.0)], axis=0).astype(bf16)


def full_conj(x):
    x = x.astype(f32)
    return jnp.concatenate([x * signs(x.shape[1], 1.0), swap_halves(x)], axis=0).astype(bf16)


def resolvent(levels, shift, broad, index, overall):
    eps = energy_low + energy_span * (index.astype(f32) + 0.5) / overall
    detune = eps - levels - shift
    damping = broaden_base + broad
    inverse = 1.0 / (detune * detune + damping * damping)
    return detune * inverse, -damping * inverse


def masked_link(link2_ref, coupling_ref, mask_ref):
    extent, rows = coupling_ref.shape[1:]
    count = mask_ref.shape[1]
    block = lax.broadcasted_iota(jnp.int32, (1, rows), 1) // (rows // count)
    keep = jnp.zeros((1, rows), f32)
    for index in range(count):
        keep = jnp.where(block == index, mask_ref[0, index].astype(f32), keep)
    link = (coupling_ref[0].astype(f32) * keep).astype(bf16)
    none = jnp.zeros_like(link)
    link2_ref[0:extent, 0:rows] = link
    link2_ref[0:extent, rows:] = none
    link2_ref[extent:, 0:rows] = none
    link2_ref[extent:, rows:] = link


def resolvents(overall, first, e, levels_ref, params_ref):
    return resolvent(levels_ref[...], params_ref[0, e : e + 1, :], params_ref[1, e : e + 1, :], first + e, overall)


def maps_kernel(
    overall,
    one_ref,
    two_ref,
    modes_ref,
    levels_ref,
    params_ref,
    left_ref,
    free_ref,
    out_ref,
    message_ref,
):
    energies = params_ref.shape[2]
    extent = out_ref.shape[2]
    first = lax.axis_index("energy") * energies
    odd = jnp.bitwise_and(lax.axis_index("cell"), 1) == 1
    block = jnp.max(jnp.where(odd, two_ref[...], one_ref[...])).astype(jnp.int32)
    chosen = pl.multiple_of(block * extent, extent)
    rows = modes_ref[0, pl.ds(chosen, extent), :]
    width = rows.shape[1]
    rows_f = rows.astype(f32)
    none = jnp.zeros_like(rows)
    rows2 = jnp.concatenate(
        [jnp.concatenate([rows, none], axis=1), jnp.concatenate([none, rows], axis=1)], axis=0
    )
    maps = []
    for e in range(energies):
        dr, di = resolvents(overall, first, e, levels_ref, params_ref.at[0])
        scaled = jnp.concatenate([(rows_f * dr).astype(bf16), (rows_f * di).astype(bf16)], axis=1)
        free = free_ref[e, pl.ds(chosen, extent), :]
        free_f = free.astype(f32)
        weight = params_ref[0, 2, e : e + 1, :]
        weighted = jnp.concatenate([free_f[:, :width] * weight, free_f[:, width:] * weight], axis=1)
        turned = jnp.concatenate([-free_f[:, width:], free_f[:, :width]], axis=1)
        maps.append(
            (
                left_ref[e, pl.ds(chosen, extent), :],
                dot_last(scaled, rows2),
                dot_last(weighted.astype(bf16), jnp.concatenate([free, turned.astype(bf16)], axis=0)),
            )
        )
        for part in range(3):
            out_ref[e, part] = maps[e][part].astype(bf16)
    write_message(message_ref, maps)


def make_rows(energies, hop, overall, share, modes_ref, levels_ref, params_ref, link2_ref, left_ref, local_ref, free_ref):
    group = lax.axis_index("energy")
    first = jnp.bitwise_xor(group, hop) * energies
    link2 = link2_ref[...]
    modes = modes_ref[0]
    modes_f = modes.astype(f32)
    mine = pl.multiple_of(group * share, share)
    rows_f = modes_ref[0, pl.ds(mine, share), :].astype(f32)
    for e in range(energies):
        dr, di = resolvents(overall, first, e, levels_ref, params_ref)
        free_re = dot_last((modes_f * dr).astype(bf16), modes)
        free_im = dot_last((modes_f * di).astype(bf16), modes)
        free = jnp.concatenate([free_re.astype(bf16), free_im.astype(bf16)], axis=1)
        if free_ref is not None:
            free_ref[e] = free
        left_ref[e] = dot_last(free, link2).astype(bf16)
        weight = params_ref[2, e : e + 1, :]
        own = dot_last(jnp.concatenate([rows_f * dr, rows_f * di], axis=0).astype(bf16), modes) * weight
        own_re, own_im = own[:share], own[share:]
        own = jnp.concatenate(
            [jnp.concatenate([own_re, own_im], axis=1), jnp.concatenate([own_im, -own_re], axis=1)], axis=0
        )
        local = dot_last(own.astype(bf16), free)
        local_ref[e, 0] = local[:share].astype(bf16)
        local_ref[e, 1] = local[share:].astype(bf16)


def front_kernel(
    interface_ref,
    mask_hbm,
    modes_hbm,
    levels_hbm,
    coupling_hbm,
    shift_hbm,
    broad_hbm,
    inject_hbm,
    offsets_hbm,
    block_ref,
    link2_ref,
    modes_ref,
    levels_ref,
    params_ref,
    offsets_ref,
    mask_ref,
    coupling_ref,
    sems,
):
    copies = [
        pltpu.make_async_copy(source, target, sems.at[index])
        for index, (source, target) in enumerate(
            (
                (mask_hbm, mask_ref),
                (offsets_hbm, offsets_ref),
                (coupling_hbm, coupling_ref),
                (shift_hbm, params_ref.at[0, 0:1]),
                (broad_hbm, params_ref.at[0, 1:2]),
                (inject_hbm, params_ref.at[0, 2:3]),
                (levels_hbm, levels_ref),
                (modes_hbm, modes_ref),
            )
        )
    ]
    for copy in copies:
        copy.start()
    for copy in copies:
        copy.wait()
    block_ref[...] = jnp.full(block_ref.shape, interface_ref[0].astype(f32))
    masked_link(link2_ref, coupling_ref, mask_ref)


def own_rows_kernel(overall, share, modes_ref, levels_ref, link2_ref, params_ref, left_ref, local_ref, free_ref):
    make_rows(
        params_ref.shape[2],
        0,
        overall,
        share,
        modes_ref,
        levels_ref,
        params_ref.at[0],
        link2_ref,
        left_ref,
        local_ref,
        free_ref,
    )


def rows_kernel(overall, share, hop, slot, modes_ref, levels_ref, link2_ref, got_ref, *rest):
    if len(rest) > 2:
        had_ref, left_ref, local_ref, both_ref = rest
        count = had_ref.shape[0]
        both_ref[0:count] = had_ref[...]
        both_ref[count:] = got_ref[...]
    else:
        left_ref, local_ref = rest
    make_rows(
        got_ref.shape[2],
        hop,
        overall,
        share,
        modes_ref,
        levels_ref,
        got_ref.at[slot],
        link2_ref,
        left_ref,
        local_ref,
        None,
    )


spare = 16


def places(extent, width):
    row = lax.broadcasted_iota(jnp.int32, (extent, width), 0)
    lane = lax.broadcasted_iota(jnp.int32, (extent, width), 1)
    return row, jnp.where(lane < extent, lane, lane - extent), lane < extent


def pack_lesser(first, second):
    _, _, low = places(*first.shape)
    return jnp.where(low, first + swap_halves(first), second + swap_halves(second))


def with_turned(x):
    square = jnp.concatenate([x, swap_halves(x)], axis=0)
    return square, square.T


def unpack_lesser(packed):
    packed = packed.astype(f32)
    extent, width = packed.shape
    _, _, low = places(extent, width)
    square, turned = with_turned(packed)
    total, change = 0.5 * (square + turned), 0.5 * (square - turned)
    return (
        jnp.where(low, total[:extent], change[extent:]),
        jnp.where(low, total[extent:], change[:extent]),
    )


def pack_retarded(first, second):
    row, column, _ = places(*first.shape)
    diagonal = jnp.sum(jnp.where(row == column, second, 0.0), axis=0, keepdims=True)
    return jnp.where(row <= column, first, second), jnp.broadcast_to(diagonal, (spare, first.shape[1]))


def unpack_retarded(packed, diagonal):
    packed, diagonal = packed.astype(f32), diagonal.astype(f32)
    extent, width = packed.shape
    row, column, _ = places(extent, width)
    turned = with_turned(packed)[1][:extent]
    return (
        jnp.where(row <= column, packed, turned),
        jnp.where(row > column, packed, jnp.where(row == column, diagonal, turned)),
    )


def write_message(ref, maps):
    extent = maps[0][-1].shape[0]
    for pair in range(ref.shape[0]):
        first, second = maps[2 * pair], maps[2 * pair + 1]
        shared, diagonal = pack_retarded(first[-2], second[-2])
        ref[pair, 0:extent] = shared.astype(bf16)
        ref[pair, extent : 2 * extent] = pack_lesser(first[-1], second[-1]).astype(bf16)
        ref[pair, 2 * extent : 2 * extent + spare] = diagonal.astype(bf16)
        if ref.shape[1] > 2 * extent + spare:
            ref[pair, 2 * extent + spare : 3 * extent + spare] = first[0].astype(bf16)
            ref[pair, 3 * extent + spare :] = second[0].astype(bf16)


def read_message(ref):
    extent = ref.shape[2] // 2
    maps = []
    for pair in range(ref.shape[0]):
        retarded = unpack_retarded(ref[pair, 0:extent], ref[pair, 2 * extent : 2 * extent + 1])
        lesser = unpack_lesser(ref[pair, extent : 2 * extent])
        for which in range(2):
            start = (2 + which) * extent + spare
            front = (ref[pair, start : start + extent],) if ref.shape[1] > 2 * extent + spare else ()
            maps.append(front + (retarded[which].astype(bf16), lesser[which].astype(bf16)))
    return maps


def pushed(step, state):
    first = dot_mat(step[0], jnp.concatenate([full(state[0]), full(state[1])], axis=1)).astype(bf16)
    width = step[0].shape[1]
    return (
        dot_last(first[:, :width], full_conj(step[0])),
        dot_last(first[:, width:], full(step[0])),
    )


def compose(earlier, latter):
    retarded, lesser = pushed(latter, earlier[1:])
    return (
        dot_mat(latter[0], full(earlier[0])),
        latter[1].astype(f32) + retarded,
        latter[2].astype(f32) + lesser,
    )


def pick(flag, yes, no):
    return tuple(jnp.where(flag, a, b) for a, b in zip(yes, no))


def neutral(extent, width):
    row = lax.broadcasted_iota(jnp.int32, (extent, width), 0)
    lane = lax.broadcasted_iota(jnp.int32, (extent, width), 1)
    zero = jnp.zeros((extent, width), f32)
    return (jnp.where(row == lane, 1.0, 0.0).astype(bf16), zero.astype(bf16), zero.astype(bf16))


def read(ref, e):
    return tuple(ref[e, part] for part in range(ref.shape[1]))


def join_kernel(level, *refs):
    total_ref, other_ref = refs[:2]
    enter_ref = refs[2] if level else None
    outs = refs[3 if level else 2 :]
    new_enter_ref, message_ref = outs[:2]
    energies, _, extent, width = total_ref.shape
    place = lax.axis_index("cell")
    upper = jnp.bitwise_and(jnp.right_shift(place, level), 1) == 1
    others = read_message(other_ref)
    joined = []
    for e in range(energies):
        total, other = read(total_ref, e), others[e]
        joined.append(compose(pick(upper, other, total), pick(upper, total, other)))
        if level:
            enter = read(enter_ref, e)
            longer = compose(other, enter)
            longer = tuple(x.astype(bf16) for x in longer)
            enter = pick(upper, longer, enter)
        else:
            enter = pick(upper, other, neutral(extent, width))
        for part in range(3):
            new_enter_ref[e, part] = enter[part]
            if len(outs) > 2:
                outs[2][e, part] = joined[e][part].astype(bf16)
    write_message(message_ref, joined)


def arrive_kernel(level, enter_ref, state_ref, retarded_ref, lesser_ref):
    upper = jnp.right_shift(lax.axis_index("cell"), level) == 1
    states = read_message(state_ref)
    lessers = []
    for e in range(enter_ref.shape[0]):
        enter = read(enter_ref, e)
        state = pick(upper, states[e], (jnp.zeros_like(enter[1]), jnp.zeros_like(enter[2])))
        retarded, lesser = pushed(enter, state)
        retarded_ref[e] = (enter[1].astype(f32) + retarded).astype(bf16)
        lessers.append(enter[2].astype(f32) + lesser)
    for pair in range(lesser_ref.shape[0]):
        lesser_ref[pair] = pack_lesser(lessers[2 * pair], lessers[2 * pair + 1]).astype(bf16)


def row_sums(x):
    return dot_last(jnp.ones((8, x.shape[1]), bf16), x.astype(bf16))[0:1]


def diagonal_kernel(overall, modes_ref, levels_ref, params_ref, out_ref):
    energies = params_ref.shape[2]
    first = lax.axis_index("energy") * energies
    modes = modes_ref[0].astype(f32)
    for e in range(energies):
        _, di = resolvents(overall, first, e, levels_ref, params_ref.at[0])
        out_ref[0, e : e + 1, :] = row_sums(modes * (modes * di).astype(bf16).astype(f32))


def density_kernel(diagonal_ref, left_ref, retarded_ref, out_ref):
    for e in range(left_ref.shape[0]):
        left = left_ref[e]
        pz = dot_mat(left, full(retarded_ref[e])).astype(bf16).astype(f32)
        total = diagonal_ref[0, e : e + 1, :] + row_sums(pz * swap_halves(left.astype(f32)))
        out_ref[0, e : e + 1, :] = -total / math.pi


def convolve_kernel(reach, hop, last, offsets_ref, screen_ref, lesser_ref, left_ref, local_ref, *refs):
    if hop:
        refs = refs[1:]
    sums_ref, *refs = refs
    if last:
        out_hbm, *refs = refs
    g_ref, picked_ref, sem, *refs = refs
    copy = pltpu.make_async_copy(offsets_ref, picked_ref, sem)
    copy.start()
    energies = left_ref.shape[0]
    points, share, width = screen_ref.shape[2:]
    overall = sums_ref.shape[1] - 2 * reach
    group = lax.axis_index("energy")
    mine = pl.multiple_of(group * share, share)
    base = jnp.bitwise_xor(group, hop) * energies + reach
    if hop == 0:
        blank = jnp.zeros((share, width), f32)
        for part in range(3):
            for e in range(sums_ref.shape[1]):
                sums_ref[part, e] = blank
    for pair in range(energies // 2):
        states = unpack_lesser(lesser_ref[pair])
        for e in (2 * pair, 2 * pair + 1):
            own = left_ref[e, pl.ds(mine, share), :]
            pl_hat = dot_mat(own, full(states[e - 2 * pair]))
            turned = swap_halves(pl_hat) * signs(pl_hat.shape[1], 1.0)
            chain = dot_last(jnp.concatenate([pl_hat, turned], axis=0).astype(bf16), left_ref[e])
            re = chain[:share] + local_ref[e, 0].astype(f32)
            im = chain[share:] + local_ref[e, 1].astype(f32)
            g_ref[0, e] = re + im
            g_ref[1, e] = im
            g_ref[2, e] = re
    copy.wait()
    height = 16

    def out_copy(step):
        rows = pl.ds(pl.multiple_of(step * height, height), height)
        return pltpu.make_async_copy(
            refs[0].at[:, :, :, rows, :], out_hbm.at[:, :, :, rows, :], refs[1].at[step]
        )

    def rows_of(step, _):
        rows = pl.ds(pl.multiple_of(step * height, height), height)
        for k in range(points):
            w_re = screen_ref[0, 0, k, rows, :].astype(f32)
            w_im = screen_ref[0, 1, k, rows, :].astype(f32)
            factors = (w_re, w_re + w_im, w_im - w_re)
            for e in range(energies):
                target = base + e + picked_ref[k]
                for part in range(3):
                    sums_ref[part, target, rows, :] += factors[part] * g_ref[part, e, rows, :]
        if last:
            for e in range(overall):
                common = sums_ref[0, reach + e, rows, :]
                refs[0][0, 0, e, rows, :] = (-(common + sums_ref[2, reach + e, rows, :])).astype(bf16)
                refs[0][0, 1, e, rows, :] = (common - sums_ref[1, reach + e, rows, :]).astype(bf16)
            out_copy(step).start()
        return 0

    steps = share // height
    lax.fori_loop(0, steps, rows_of, 0)
    if last:
        for step in range(steps):
            out_copy(step).wait()


def in_hbm(x):
    return pltpu.with_memory_space_constraint(x, pltpu.HBM)


def call(kernel, out_shape, in_specs, scratch=(), flops=1_000_000, size=1_000_000, out_specs=None, aliases={}):
    outs = out_specs or jax.tree.map(lambda _: VMEM, out_shape)
    return pl.pallas_call(
        kernel,
        out_shape=out_shape,
        in_specs=in_specs,
        out_specs=outs,
        scratch_shapes=list(scratch),
        input_output_aliases=aliases,
        compiler_params=pltpu.CompilerParams(vmem_limit_bytes=16 << 20),
        cost_estimate=pl.CostEstimate(flops=flops, bytes_accessed=size, transcendentals=0),
    )


def body(
    modes,
    levels,
    level_shift,
    broadening,
    injection,
    coupling,
    row_mask,
    interface,
    screened,
    offsets,
):
    cells = lax.axis_size("cell")
    groups = lax.axis_size("energy")
    rounds = cells.bit_length() - 1
    assert cells == 1 << rounds and groups & (groups - 1) == 0
    energies = level_shift.shape[1]
    overall = energies * groups
    orbitals, extent = coupling.shape[1:]
    width = 2 * extent
    share = orbitals // groups
    sds = jax.ShapeDtypeStruct

    def swapped(x, axis, distance):
        return lax.ppermute(x, axis, [(i, i ^ distance) for i in range(lax.axis_size(axis))])

    assert energies % 2 == 0
    pairs = energies // 2
    maps_shape = sds((energies, 3, extent, width), bf16)
    message = sds((pairs, 4 * extent + spare, width), bf16)
    state_message = sds((pairs, 2 * extent + spare, width), bf16)
    coupling = jnp.swapaxes(coupling, 1, 2)
    block, link2, modes, levels, params, offsets = call(
        front_kernel,
        (
            sds((8, width), f32),
            sds((width, 2 * orbitals), bf16),
            sds(modes.shape, bf16),
            sds(levels.shape, f32),
            sds((1, 3, energies, orbitals), f32),
            sds(offsets.shape, jnp.int32),
        ),
        [SMEM] + [HBM] * 8,
        [
            pltpu.SMEM(row_mask.shape, jnp.int32),
            pltpu.VMEM(coupling.shape, bf16),
            pltpu.SemaphoreType.DMA((8,)),
        ],
    )(interface, *map(in_hbm, (row_mask, modes, levels, coupling, level_shift, broadening, injection, offsets)))
    one = swapped(block, "cell", 1)
    mate = [i + 1 if i % 2 else i - 1 for i in range(cells)]
    mate[0], mate[-1] = 0, cells - 1
    route = [(i * groups + g, mate[i] * groups + (g ^ int(mate[i] == i))) for i in range(cells) for g in range(groups)]
    two = lax.ppermute(block, ("cell", "energy"), route)

    left_shape = sds((energies, orbitals, width), bf16)
    local_shape = sds((energies, 2, share, orbitals), bf16)
    params_shape = (3, energies, orbitals)
    left, local, free = call(
        partial(own_rows_kernel, overall, share),
        (left_shape, local_shape, sds((energies, orbitals, 2 * orbitals), bf16)),
        [VMEM] * 4,
    )(modes, levels, link2, params)
    lefts, locals_ = [left], [local]

    total, sent = call(
        partial(maps_kernel, overall),
        (maps_shape, message),
        [VMEM] * 7,
    )(one, two, modes, levels, params, left, free)
    diagonal = call(
        partial(diagonal_kernel, overall), sds((1, energies, orbitals), f32), [VMEM] * 3
    )(modes, levels, params)

    known = params
    while known.shape[0] < groups:
        count = known.shape[0]
        got = swapped(known, "energy", count)
        more = 2 * count < groups
        for slot in range(count):
            outs, given = (left_shape, local_shape), (modes, levels, link2, got)
            if slot == 0 and more:
                outs, given = outs + (sds((2 * count,) + params_shape, f32),), given + (known,)
            left, local, *rest = call(
                partial(rows_kernel, overall, share, count + slot, slot), outs, [VMEM] * len(given)
            )(*given)
            lefts.append(left)
            locals_.append(local)
            if rest:
                both = rest[0]
        if not more:
            break
        known = both

    enter = None
    for level in range(rounds - 1):
        other = swapped(sent, "cell", 1 << level)
        outs = (maps_shape, message, maps_shape) if level < rounds - 2 else (maps_shape, state_message)
        given = [total, other] + ([enter] if level else [])
        enter, sent, *rest = call(partial(join_kernel, level), outs, [VMEM] * len(given))(*given)
        total = rest[0] if rest else None
    state = swapped(sent, "cell", cells // 2)
    retarded, lesser = call(
        partial(arrive_kernel, rounds - 1),
        (sds((energies, extent, width), bf16), sds((pairs, extent, width), bf16)),
        [VMEM, VMEM],
    )(enter, state)

    lessers = [lesser]
    for hop in range(1, groups):
        lessers.append(swapped(lesser, "energy", hop))
    density = call(density_kernel, sds((1, energies, orbitals), f32), [VMEM] * 3)(
        diagonal, lefts[0], retarded
    )

    reach = overall // 4
    sums_shape = sds((3, overall + 2 * reach, share, orbitals), f32)
    sigma_shape = sds((1, 2, overall, share, orbitals), bf16)
    scratch = [
        pltpu.VMEM((3, energies, share, orbitals), f32),
        pltpu.SMEM(offsets.shape, jnp.int32),
        pltpu.SemaphoreType.DMA,
    ]
    for hop in (0, *reversed(range(1, groups))):
        last = hop == min(1, groups - 1)
        given = (offsets, screened, lessers[hop], lefts[hop], locals_[hop]) + ((sums,) if hop else ())
        outs, specs, extra = sums_shape, VMEM, []
        if last:
            outs, specs = (sums_shape, sigma_shape), (VMEM, HBM)
            extra = [pltpu.VMEM(sigma_shape.shape, bf16), pltpu.SemaphoreType.DMA((share // 16,))]
        sums = call(
            partial(convolve_kernel, reach, hop, last),
            outs,
            [VMEM] * len(given),
            scratch + extra,
            out_specs=specs,
            aliases={5: 0} if hop else {},
        )(*given)
    sigma = sums[1]
    return (density, sigma)


def solution(mesh):
    placed = (
        P("cell", None, None),
        P("cell", None),
        P("cell", "energy", None),
        P("cell", "energy", None),
        P("cell", "energy", None),
        P("cell", None, None),
        P("cell", None),
        P("cell"),
        P("cell", None, None, "energy", None),
        P(),
    )
    return jax.shard_map(
        body,
        mesh=mesh,
        in_specs=placed,
        out_specs=(P("cell", "energy", None), P("cell", None, None, "energy", None)),
        check_vma=False,
    )
```

```python
from functools import partial
import math

import jax
import jax.numpy as jnp
from jax import lax
from jax.experimental import pallas as pl
from jax.experimental.pallas import tpu as pltpu
from jax.sharding import PartitionSpec as P


broaden_base = 1.0
energy_low = -0.25
energy_span = 0.5
f32 = jnp.float32
bf16 = jnp.bfloat16

VMEM = pl.BlockSpec(memory_space=pltpu.VMEM)
SMEM = pl.BlockSpec(memory_space=pltpu.SMEM)
HBM = pl.BlockSpec(memory_space=pltpu.HBM)


def dot_last(a, b, precision=None):
    return lax.dot_general(
        a, b, (((1,), (1,)), ((), ())), precision=precision, preferred_element_type=f32
    )


def dot_mat(a, b):
    return lax.dot_general(a, b, (((1,), (0,)), ((), ())), preferred_element_type=f32)


def signs(width, left_sign):
    lane = lax.broadcasted_iota(jnp.int32, (1, width), 1)
    return jnp.where(lane < width // 2, left_sign, -left_sign).astype(f32)


def swap_halves(x):
    return pltpu.roll(x, x.shape[1] // 2, 1)


def full(x):
    x = x.astype(f32)
    return jnp.concatenate([x, swap_halves(x) * signs(x.shape[1], -1.0)], axis=0).astype(bf16)


def full_conj(x):
    x = x.astype(f32)
    return jnp.concatenate([x * signs(x.shape[1], 1.0), swap_halves(x)], axis=0).astype(bf16)


def resolvent(levels, shift, broad, index, overall):
    eps = energy_low + energy_span * (index.astype(f32) + 0.5) / overall
    detune = eps - levels - shift
    damping = broaden_base + broad
    inverse = 1.0 / (detune * detune + damping * damping)
    return detune * inverse, -damping * inverse


def masked_link(link2_ref, coupling_ref, mask_ref):
    extent, rows = coupling_ref.shape[1:]
    count = mask_ref.shape[1]
    block = lax.broadcasted_iota(jnp.int32, (1, rows), 1) // (rows // count)
    keep = jnp.zeros((1, rows), f32)
    for index in range(count):
        keep = jnp.where(block == index, mask_ref[0, index].astype(f32), keep)
    link = (coupling_ref[0].astype(f32) * keep).astype(bf16)
    none = jnp.zeros_like(link)
    link2_ref[0:extent, 0:rows] = link
    link2_ref[0:extent, rows:] = none
    link2_ref[extent:, 0:rows] = none
    link2_ref[extent:, rows:] = link


def resolvents(overall, first, e, levels_ref, params_ref):
    return resolvent(levels_ref[...], params_ref[0, e : e + 1, :], params_ref[1, e : e + 1, :], first + e, overall)


def maps_kernel(
    overall,
    one_ref,
    two_ref,
    modes_ref,
    levels_ref,
    params_ref,
    left_ref,
    free_ref,
    out_ref,
    message_ref,
):
    energies = params_ref.shape[2]
    extent = out_ref.shape[2]
    first = lax.axis_index("energy") * energies
    odd = jnp.bitwise_and(lax.axis_index("cell"), 1) == 1
    block = jnp.max(jnp.where(odd, two_ref[...], one_ref[...])).astype(jnp.int32)
    chosen = pl.multiple_of(block * extent, extent)
    rows = modes_ref[0, pl.ds(chosen, extent), :]
    width = rows.shape[1]
    rows_f = rows.astype(f32)
    none = jnp.zeros_like(rows)
    rows2 = jnp.concatenate(
        [jnp.concatenate([rows, none], axis=1), jnp.concatenate([none, rows], axis=1)], axis=0
    )
    maps = []
    for e in range(energies):
        dr, di = resolvents(overall, first, e, levels_ref, params_ref.at[0])
        scaled = jnp.concatenate([(rows_f * dr).astype(bf16), (rows_f * di).astype(bf16)], axis=1)
        free = free_ref[e, pl.ds(chosen, extent), :]
        free_f = free.astype(f32)
        weight = params_ref[0, 2, e : e + 1, :]
        weighted = jnp.concatenate([free_f[:, :width] * weight, free_f[:, width:] * weight], axis=1)
        turned = jnp.concatenate([-free_f[:, width:], free_f[:, :width]], axis=1)
        maps.append(
            (
                left_ref[e, pl.ds(chosen, extent), :],
                dot_last(scaled, rows2),
                dot_last(weighted.astype(bf16), jnp.concatenate([free, turned.astype(bf16)], axis=0)),
            )
        )
        for part in range(3):
            out_ref[e, part] = maps[e][part].astype(bf16)
    write_message(message_ref, maps)


def make_rows(energies, hop, overall, share, modes_ref, levels_ref, params_ref, link2_ref, left_ref, local_ref, free_ref):
    group = lax.axis_index("energy")
    first = jnp.bitwise_xor(group, hop) * energies
    link2 = link2_ref[...]
    modes = modes_ref[0]
    modes_f = modes.astype(f32)
    mine = pl.multiple_of(group * share, share)
    rows_f = modes_ref[0, pl.ds(mine, share), :].astype(f32)
    for e in range(energies):
        dr, di = resolvents(overall, first, e, levels_ref, params_ref)
        free_re = dot_last((modes_f * dr).astype(bf16), modes)
        free_im = dot_last((modes_f * di).astype(bf16), modes)
        free = jnp.concatenate([free_re.astype(bf16), free_im.astype(bf16)], axis=1)
        if free_ref is not None:
            free_ref[e] = free
        left_ref[e] = dot_last(free, link2).astype(bf16)
        weight = params_ref[2, e : e + 1, :]
        own = dot_last(jnp.concatenate([rows_f * dr, rows_f * di], axis=0).astype(bf16), modes) * weight
        own_re, own_im = own[:share], own[share:]
        own = jnp.concatenate(
            [jnp.concatenate([own_re, own_im], axis=1), jnp.concatenate([own_im, -own_re], axis=1)], axis=0
        )
        local = dot_last(own.astype(bf16), free)
        local_ref[e, 0] = local[:share].astype(bf16)
        local_ref[e, 1] = local[share:].astype(bf16)


def tile_kernel(interface_ref, block_ref):
    block_ref[...] = jnp.full(block_ref.shape, interface_ref[0].astype(f32))


def front_kernel(
    mask_hbm,
    modes_hbm,
    levels_hbm,
    coupling_hbm,
    shift_hbm,
    broad_hbm,
    inject_hbm,
    offsets_hbm,
    link2_ref,
    modes_ref,
    levels_ref,
    params_ref,
    offsets_ref,
    mask_ref,
    coupling_ref,
    sems,
):
    copies = [
        pltpu.make_async_copy(source, target, sems.at[index])
        for index, (source, target) in enumerate(
            (
                (mask_hbm, mask_ref),
                (offsets_hbm, offsets_ref),
                (coupling_hbm, coupling_ref),
                (shift_hbm, params_ref.at[0, 0:1]),
                (broad_hbm, params_ref.at[0, 1:2]),
                (inject_hbm, params_ref.at[0, 2:3]),
                (levels_hbm, levels_ref),
                (modes_hbm, modes_ref),
            )
        )
    ]
    for copy in copies:
        copy.start()
    for copy in copies:
        copy.wait()
    masked_link(link2_ref, coupling_ref, mask_ref)


def own_rows_kernel(overall, share, modes_ref, levels_ref, link2_ref, params_ref, left_ref, local_ref, free_ref):
    make_rows(
        params_ref.shape[2],
        0,
        overall,
        share,
        modes_ref,
        levels_ref,
        params_ref.at[0],
        link2_ref,
        left_ref,
        local_ref,
        free_ref,
    )


def rows_kernel(overall, share, hop, slot, modes_ref, levels_ref, link2_ref, got_ref, *rest):
    if len(rest) > 2:
        had_ref, left_ref, local_ref, both_ref = rest
        count = had_ref.shape[0]
        both_ref[0:count] = had_ref[...]
        both_ref[count:] = got_ref[...]
    else:
        left_ref, local_ref = rest
    make_rows(
        got_ref.shape[2],
        hop,
        overall,
        share,
        modes_ref,
        levels_ref,
        got_ref.at[slot],
        link2_ref,
        left_ref,
        local_ref,
        None,
    )


spare = 16


def places(extent, width):
    row = lax.broadcasted_iota(jnp.int32, (extent, width), 0)
    lane = lax.broadcasted_iota(jnp.int32, (extent, width), 1)
    return row, jnp.where(lane < extent, lane, lane - extent), lane < extent


def pack_lesser(first, second):
    _, _, low = places(*first.shape)
    return jnp.where(low, first + swap_halves(first), second + swap_halves(second))


def with_turned(x):
    square = jnp.concatenate([x, swap_halves(x)], axis=0)
    return square, square.T


def unpack_lesser(packed):
    packed = packed.astype(f32)
    extent, width = packed.shape
    _, _, low = places(extent, width)
    square, turned = with_turned(packed)
    total, change = 0.5 * (square + turned), 0.5 * (square - turned)
    return (
        jnp.where(low, total[:extent], change[extent:]),
        jnp.where(low, total[extent:], change[:extent]),
    )


def pack_retarded(first, second):
    row, column, _ = places(*first.shape)
    diagonal = jnp.sum(jnp.where(row == column, second, 0.0), axis=0, keepdims=True)
    return jnp.where(row <= column, first, second), jnp.broadcast_to(diagonal, (spare, first.shape[1]))


def unpack_retarded(packed, diagonal):
    packed, diagonal = packed.astype(f32), diagonal.astype(f32)
    extent, width = packed.shape
    row, column, _ = places(extent, width)
    turned = with_turned(packed)[1][:extent]
    return (
        jnp.where(row <= column, packed, turned),
        jnp.where(row > column, packed, jnp.where(row == column, diagonal, turned)),
    )


def write_message(ref, maps):
    extent = maps[0][-1].shape[0]
    for pair in range(ref.shape[0]):
        first, second = maps[2 * pair], maps[2 * pair + 1]
        shared, diagonal = pack_retarded(first[-2], second[-2])
        ref[pair, 0:extent] = shared.astype(bf16)
        ref[pair, extent : 2 * extent] = pack_lesser(first[-1], second[-1]).astype(bf16)
        ref[pair, 2 * extent : 2 * extent + spare] = diagonal.astype(bf16)
        if ref.shape[1] > 2 * extent + spare:
            ref[pair, 2 * extent + spare : 3 * extent + spare] = first[0].astype(bf16)
            ref[pair, 3 * extent + spare :] = second[0].astype(bf16)


def read_message(ref):
    extent = ref.shape[2] // 2
    maps = []
    for pair in range(ref.shape[0]):
        retarded = unpack_retarded(ref[pair, 0:extent], ref[pair, 2 * extent : 2 * extent + 1])
        lesser = unpack_lesser(ref[pair, extent : 2 * extent])
        for which in range(2):
            start = (2 + which) * extent + spare
            front = (ref[pair, start : start + extent],) if ref.shape[1] > 2 * extent + spare else ()
            maps.append(front + (retarded[which].astype(bf16), lesser[which].astype(bf16)))
    return maps


def pushed(step, state):
    first = dot_mat(step[0], jnp.concatenate([full(state[0]), full(state[1])], axis=1)).astype(bf16)
    width = step[0].shape[1]
    return (
        dot_last(first[:, :width], full_conj(step[0])),
        dot_last(first[:, width:], full(step[0])),
    )


def compose(earlier, latter):
    retarded, lesser = pushed(latter, earlier[1:])
    return (
        dot_mat(latter[0], full(earlier[0])),
        latter[1].astype(f32) + retarded,
        latter[2].astype(f32) + lesser,
    )


def pick(flag, yes, no):
    return tuple(jnp.where(flag, a, b) for a, b in zip(yes, no))


def neutral(extent, width):
    row = lax.broadcasted_iota(jnp.int32, (extent, width), 0)
    lane = lax.broadcasted_iota(jnp.int32, (extent, width), 1)
    zero = jnp.zeros((extent, width), f32)
    return (jnp.where(row == lane, 1.0, 0.0).astype(bf16), zero.astype(bf16), zero.astype(bf16))


def read(ref, e):
    return tuple(ref[e, part] for part in range(ref.shape[1]))


def upper_half(level):
    return jnp.bitwise_and(jnp.right_shift(lax.axis_index("cell"), level), 1) == 1


def join_kernel(level, total_ref, other_ref, message_ref, *new_total_ref):
    upper = upper_half(level)
    others = read_message(other_ref)
    joined = []
    for e in range(total_ref.shape[0]):
        total, other = read(total_ref, e), others[e]
        pair = pick(upper, other, total), pick(upper, total, other)
        joined.append(compose(*pair) if new_total_ref else moved(pair[1], pair[0][1:]))
        for ref in new_total_ref:
            for part in range(3):
                ref[e, part] = joined[e][part].astype(bf16)
    write_message(message_ref, joined)


def enter_kernel(level, other_ref, *refs):
    upper = upper_half(level)
    others = read_message(other_ref)
    out_ref = refs[-1]
    for e in range(out_ref.shape[0]):
        if level:
            old = read(refs[0], e)
            new = pick(upper, tuple(x.astype(bf16) for x in compose(others[e], old)), old)
        else:
            new = pick(upper, others[e], neutral(*out_ref.shape[2:]))
        for part in range(3):
            out_ref[e, part] = new[part]


def moved(step, state):
    retarded, lesser = pushed(step, state)
    return step[1].astype(f32) + retarded, step[2].astype(f32) + lesser


def arrive_kernel(level, enter_ref, state_ref, retarded_ref, lesser_ref):
    upper = jnp.right_shift(lax.axis_index("cell"), level) == 1
    states = read_message(state_ref)
    lessers = []
    for e in range(enter_ref.shape[0]):
        enter = read(enter_ref, e)
        state = pick(upper, states[e], (jnp.zeros_like(enter[1]), jnp.zeros_like(enter[2])))
        retarded, lesser = pushed(enter, state)
        retarded_ref[e] = (enter[1].astype(f32) + retarded).astype(bf16)
        lessers.append(enter[2].astype(f32) + lesser)
    for pair in range(lesser_ref.shape[0]):
        lesser_ref[pair] = pack_lesser(lessers[2 * pair], lessers[2 * pair + 1]).astype(bf16)


def row_sums(x):
    return dot_last(jnp.ones((8, x.shape[1]), bf16), x.astype(bf16))[0:1]


def diagonal_kernel(overall, modes_ref, levels_ref, params_ref, out_ref, sums_ref):
    energies = params_ref.shape[2]
    first = lax.axis_index("energy") * energies
    modes = modes_ref[0].astype(f32)
    for e in range(energies):
        _, di = resolvents(overall, first, e, levels_ref, params_ref.at[0])
        out_ref[0, e : e + 1, :] = row_sums(modes * (modes * di).astype(bf16).astype(f32))
    blank = jnp.zeros(sums_ref.shape[2:], f32)
    for part in range(sums_ref.shape[0]):
        for e in range(sums_ref.shape[1]):
            sums_ref[part, e] = blank


def density_of(diagonal_ref, left_ref, retarded_ref, out_ref):
    for e in range(left_ref.shape[0]):
        left = left_ref[e]
        pz = dot_mat(left, full(retarded_ref[e])).astype(bf16).astype(f32)
        total = diagonal_ref[0, e : e + 1, :] + row_sums(pz * swap_halves(left.astype(f32)))
        out_ref[0, e : e + 1, :] = -total / math.pi


def convolve_kernel(reach, hop, last, offsets_ref, screen_ref, lesser_ref, left_ref, local_ref, _, *refs):
    if hop == 0:
        diagonal_ref, retarded_ref, *refs = refs
    sums_ref, *refs = refs
    if hop == 0:
        density_of(diagonal_ref, left_ref, retarded_ref, refs.pop(0))
    if last:
        out_hbm, *refs = refs
    g_ref, picked_ref, sem, *refs = refs
    copy = pltpu.make_async_copy(offsets_ref, picked_ref, sem)
    copy.start()
    energies = left_ref.shape[0]
    points, share, _ = screen_ref.shape[2:]
    overall = sums_ref.shape[1] - 2 * reach
    group = lax.axis_index("energy")
    mine = pl.multiple_of(group * share, share)
    base = jnp.bitwise_xor(group, hop) * energies + reach
    for pair in range(energies // 2):
        states = unpack_lesser(lesser_ref[pair])
        for e in (2 * pair, 2 * pair + 1):
            own = left_ref[e, pl.ds(mine, share), :]
            pl_hat = dot_mat(own, full(states[e - 2 * pair]))
            turned = swap_halves(pl_hat) * signs(pl_hat.shape[1], 1.0)
            chain = dot_last(jnp.concatenate([pl_hat, turned], axis=0).astype(bf16), left_ref[e])
            re = chain[:share] + local_ref[e, 0].astype(f32)
            im = chain[share:] + local_ref[e, 1].astype(f32)
            g_ref[0, e] = re + im
            g_ref[1, e] = im
            g_ref[2, e] = re
    copy.wait()
    height = 16

    def out_copy(step):
        rows = pl.ds(pl.multiple_of(step * height, height), height)
        return pltpu.make_async_copy(
            refs[0].at[:, :, :, rows, :], out_hbm.at[:, :, :, rows, :], refs[1].at[step]
        )

    def rows_of(step, _):
        rows = pl.ds(pl.multiple_of(step * height, height), height)
        for k in range(points):
            w_re = screen_ref[0, 0, k, rows, :].astype(f32)
            w_im = screen_ref[0, 1, k, rows, :].astype(f32)
            factors = (w_re, w_re + w_im, w_im - w_re)
            for e in range(energies):
                target = base + e + picked_ref[k]
                for part in range(3):
                    sums_ref[part, target, rows, :] += factors[part] * g_ref[part, e, rows, :]
        if last:
            for e in range(overall):
                common = sums_ref[0, reach + e, rows, :]
                refs[0][0, 0, e, rows, :] = (-(common + sums_ref[2, reach + e, rows, :])).astype(bf16)
                refs[0][0, 1, e, rows, :] = (common - sums_ref[1, reach + e, rows, :]).astype(bf16)
            out_copy(step).start()
        return 0

    steps = share // height
    lax.fori_loop(0, steps, rows_of, 0)
    if last:
        for step in range(steps):
            out_copy(step).wait()


def in_hbm(x):
    return pltpu.with_memory_space_constraint(x, pltpu.HBM)


def call(kernel, out_shape, in_specs, scratch=(), flops=1_000_000, size=1_000_000, out_specs=None, aliases={}):
    outs = out_specs or jax.tree.map(lambda _: VMEM, out_shape)
    return pl.pallas_call(
        kernel,
        out_shape=out_shape,
        in_specs=in_specs,
        out_specs=outs,
        scratch_shapes=list(scratch),
        input_output_aliases=aliases,
        compiler_params=pltpu.CompilerParams(vmem_limit_bytes=16 << 20),
        cost_estimate=pl.CostEstimate(flops=flops, bytes_accessed=size, transcendentals=0),
    )


def body(
    modes,
    levels,
    level_shift,
    broadening,
    injection,
    coupling,
    row_mask,
    interface,
    screened,
    offsets,
):
    cells = lax.axis_size("cell")
    groups = lax.axis_size("energy")
    rounds = cells.bit_length() - 1
    assert cells == 1 << rounds and groups & (groups - 1) == 0
    energies = level_shift.shape[1]
    overall = energies * groups
    orbitals, extent = coupling.shape[1:]
    width = 2 * extent
    share = orbitals // groups
    sds = jax.ShapeDtypeStruct

    def swapped(x, axis, distance):
        return lax.ppermute(x, axis, [(i, i ^ distance) for i in range(lax.axis_size(axis))])

    assert energies % 2 == 0
    pairs = energies // 2
    maps_shape = sds((energies, 3, extent, width), bf16)
    message = sds((pairs, 4 * extent + spare, width), bf16)
    state_message = sds((pairs, 2 * extent + spare, width), bf16)
    coupling = jnp.swapaxes(coupling, 1, 2)
    block = call(tile_kernel, sds((8, width), f32), [SMEM])(interface)
    one = swapped(block, "cell", 1)
    mate = [i + 1 if i % 2 else i - 1 for i in range(cells)]
    mate[0], mate[-1] = 0, cells - 1
    route = [(i * groups + g, mate[i] * groups + (g ^ int(mate[i] == i))) for i in range(cells) for g in range(groups)]
    two = lax.ppermute(block, ("cell", "energy"), route)

    link2, modes, levels, params, offsets = call(
        front_kernel,
        (
            sds((width, 2 * orbitals), bf16),
            sds(modes.shape, bf16),
            sds(levels.shape, f32),
            sds((1, 3, energies, orbitals), f32),
            sds(offsets.shape, jnp.int32),
        ),
        [HBM] * 8,
        [
            pltpu.SMEM(row_mask.shape, jnp.int32),
            pltpu.VMEM(coupling.shape, bf16),
            pltpu.SemaphoreType.DMA((8,)),
        ],
    )(*map(in_hbm, (row_mask, modes, levels, coupling, level_shift, broadening, injection, offsets)))
    left_shape = sds((energies, orbitals, width), bf16)
    local_shape = sds((energies, 2, share, orbitals), bf16)
    params_shape = (3, energies, orbitals)
    left, local, free = call(
        partial(own_rows_kernel, overall, share),
        (left_shape, local_shape, sds((energies, orbitals, 2 * orbitals), bf16)),
        [VMEM] * 4,
    )(modes, levels, link2, params)
    lefts, locals_ = [left], [local]

    total, sent = call(
        partial(maps_kernel, overall),
        (maps_shape, message),
        [VMEM] * 7,
    )(one, two, modes, levels, params, left, free)
    reach = overall // 4
    sums_shape = sds((3, overall + 2 * reach, share, orbitals), f32)
    sigma_shape = sds((1, 2, overall, share, orbitals), bf16)
    density_shape = sds((1, energies, orbitals), f32)
    diagonal, sums = call(
        partial(diagonal_kernel, overall), (density_shape, sums_shape), [VMEM] * 3
    )(modes, levels, params)

    known = params
    while known.shape[0] < groups:
        count = known.shape[0]
        got = swapped(known, "energy", count)
        more = 2 * count < groups
        for slot in range(count):
            outs, given = (left_shape, local_shape), (modes, levels, link2, got)
            if slot == 0 and more:
                outs, given = outs + (sds((2 * count,) + params_shape, f32),), given + (known,)
            left, local, *rest = call(
                partial(rows_kernel, overall, share, count + slot, slot), outs, [VMEM] * len(given)
            )(*given)
            lefts.append(left)
            locals_.append(local)
            if rest:
                both = rest[0]
        if not more:
            break
        known = both

    enter = None
    for level in range(rounds - 1):
        other = swapped(sent, "cell", 1 << level)
        outs = (message, maps_shape) if level < rounds - 2 else (state_message,)
        sent, *rest = call(partial(join_kernel, level), outs, [VMEM] * 2)(total, other)
        total = rest[0] if rest else None
        given = (other, enter) if level else (other,)
        enter = call(partial(enter_kernel, level), maps_shape, [VMEM] * len(given))(*given)
    state = swapped(sent, "cell", cells // 2)
    retarded, lesser = call(
        partial(arrive_kernel, rounds - 1),
        (sds((energies, extent, width), bf16), sds((pairs, extent, width), bf16)),
        [VMEM, VMEM],
    )(enter, state)

    lessers = [lesser]
    for hop in range(1, groups):
        lessers.append(swapped(lesser, "energy", hop))
    scratch = [
        pltpu.VMEM((3, energies, share, orbitals), f32),
        pltpu.SMEM(offsets.shape, jnp.int32),
        pltpu.SemaphoreType.DMA,
    ]
    for hop in range(groups):
        last = hop == groups - 1
        given = (offsets, screened, lessers[hop], lefts[hop], locals_[hop], sums)
        outs, specs, extra = (sums_shape,), (VMEM,), []
        if hop == 0:
            given += (diagonal, retarded)
            outs, specs = outs + (density_shape,), specs + (VMEM,)
        if last:
            outs, specs = outs + (sigma_shape,), specs + (HBM,)
            extra = [pltpu.VMEM(sigma_shape.shape, bf16), pltpu.SemaphoreType.DMA((share // 16,))]
        sums, *rest = call(
            partial(convolve_kernel, reach, hop, last),
            outs,
            [VMEM] * len(given),
            scratch + extra,
            out_specs=specs,
            aliases={5: 0},
        )(*given)
        if hop == 0:
            density = rest[0]
    sigma = rest[-1]
    return (density, sigma)


def solution(mesh):
    placed = (
        P("cell", None, None),
        P("cell", None),
        P("cell", "energy", None),
        P("cell", "energy", None),
        P("cell", "energy", None),
        P("cell", None, None),
        P("cell", None),
        P("cell"),
        P("cell", None, None, "energy", None),
        P(),
    )
    return jax.shard_map(
        body,
        mesh=mesh,
        in_specs=placed,
        out_specs=(P("cell", "energy", None), P("cell", None, None, "energy", None)),
        check_vma=False,
    )
```

```python
from functools import partial
import math

import jax
import jax.numpy as jnp
from jax import lax
from jax.experimental import pallas as pl
from jax.experimental.pallas import tpu as pltpu
from jax.sharding import PartitionSpec as P


broaden_base = 1.0
energy_low = -0.25
energy_span = 0.5
f32 = jnp.float32
bf16 = jnp.bfloat16

VMEM = pl.BlockSpec(memory_space=pltpu.VMEM)
SMEM = pl.BlockSpec(memory_space=pltpu.SMEM)
HBM = pl.BlockSpec(memory_space=pltpu.HBM)


def dot_last(a, b, precision=None):
    return lax.dot_general(
        a, b, (((1,), (1,)), ((), ())), precision=precision, preferred_element_type=f32
    )


def dot_mat(a, b):
    return lax.dot_general(a, b, (((1,), (0,)), ((), ())), preferred_element_type=f32)


def signs(width, left_sign):
    lane = lax.broadcasted_iota(jnp.int32, (1, width), 1)
    return jnp.where(lane < width // 2, left_sign, -left_sign).astype(f32)


def swap_halves(x):
    return pltpu.roll(x, x.shape[1] // 2, 1)


def full(x):
    x = x.astype(f32)
    return jnp.concatenate([x, swap_halves(x) * signs(x.shape[1], -1.0)], axis=0).astype(bf16)


def full_conj(x):
    x = x.astype(f32)
    return jnp.concatenate([x * signs(x.shape[1], 1.0), swap_halves(x)], axis=0).astype(bf16)


def resolvent(levels, shift, broad, index, overall):
    eps = energy_low + energy_span * (index.astype(f32) + 0.5) / overall
    detune = eps - levels - shift
    damping = broaden_base + broad
    inverse = 1.0 / (detune * detune + damping * damping)
    return detune * inverse, -damping * inverse


def masked_link(link2_ref, coupling_ref, mask_ref):
    extent, rows = coupling_ref.shape[1:]
    count = mask_ref.shape[1]
    block = lax.broadcasted_iota(jnp.int32, (1, rows), 1) // (rows // count)
    keep = jnp.zeros((1, rows), f32)
    for index in range(count):
        keep = jnp.where(block == index, mask_ref[0, index].astype(f32), keep)
    link = (coupling_ref[0].astype(f32) * keep).astype(bf16)
    none = jnp.zeros_like(link)
    link2_ref[0:extent, 0:rows] = link
    link2_ref[0:extent, rows:] = none
    link2_ref[extent:, 0:rows] = none
    link2_ref[extent:, rows:] = link


def resolvents(overall, first, e, levels_ref, params_ref):
    return resolvent(levels_ref[...], params_ref[0, e : e + 1, :], params_ref[1, e : e + 1, :], first + e, overall)


def maps_kernel(
    overall,
    one_ref,
    two_ref,
    modes_ref,
    levels_ref,
    params_ref,
    left_ref,
    free_ref,
    out_ref,
    message_ref,
):
    energies = params_ref.shape[2]
    extent = out_ref.shape[2]
    first = lax.axis_index("energy") * energies
    odd = jnp.bitwise_and(lax.axis_index("cell"), 1) == 1
    block = jnp.max(jnp.where(odd, two_ref[...], one_ref[...])).astype(jnp.int32)
    chosen = pl.multiple_of(block * extent, extent)
    rows = modes_ref[0, pl.ds(chosen, extent), :]
    width = rows.shape[1]
    rows_f = rows.astype(f32)
    none = jnp.zeros_like(rows)
    rows2 = jnp.concatenate(
        [jnp.concatenate([rows, none], axis=1), jnp.concatenate([none, rows], axis=1)], axis=0
    )
    maps = []
    for e in range(energies):
        dr, di = resolvents(overall, first, e, levels_ref, params_ref.at[0])
        scaled = jnp.concatenate([(rows_f * dr).astype(bf16), (rows_f * di).astype(bf16)], axis=1)
        free = free_ref[e, pl.ds(chosen, extent), :]
        free_f = free.astype(f32)
        weight = params_ref[0, 2, e : e + 1, :]
        weighted = jnp.concatenate([free_f[:, :width] * weight, free_f[:, width:] * weight], axis=1)
        turned = jnp.concatenate([-free_f[:, width:], free_f[:, :width]], axis=1)
        maps.append(
            (
                left_ref[e, pl.ds(chosen, extent), :],
                dot_last(scaled, rows2),
                dot_last(weighted.astype(bf16), jnp.concatenate([free, turned.astype(bf16)], axis=0)),
            )
        )
        for part in range(3):
            out_ref[e, part] = maps[e][part].astype(bf16)
    write_message(message_ref, maps)


def make_rows(energies, hop, overall, share, modes_ref, levels_ref, params_ref, link2_ref, left_ref, local_ref, free_ref):
    group = lax.axis_index("energy")
    first = jnp.bitwise_xor(group, hop) * energies
    link2 = link2_ref[...]
    modes = modes_ref[0]
    modes_f = modes.astype(f32)
    mine = pl.multiple_of(group * share, share)
    rows_f = modes_ref[0, pl.ds(mine, share), :].astype(f32)
    for e in range(energies):
        dr, di = resolvents(overall, first, e, levels_ref, params_ref)
        free_re = dot_last((modes_f * dr).astype(bf16), modes)
        free_im = dot_last((modes_f * di).astype(bf16), modes)
        free = jnp.concatenate([free_re.astype(bf16), free_im.astype(bf16)], axis=1)
        if free_ref is not None:
            free_ref[e] = free
        left_ref[e] = dot_last(free, link2).astype(bf16)
        weight = params_ref[2, e : e + 1, :]
        own = dot_last(jnp.concatenate([rows_f * dr, rows_f * di], axis=0).astype(bf16), modes) * weight
        own_re, own_im = own[:share], own[share:]
        own = jnp.concatenate(
            [jnp.concatenate([own_re, own_im], axis=1), jnp.concatenate([own_im, -own_re], axis=1)], axis=0
        )
        local = dot_last(own.astype(bf16), free)
        local_ref[e, 0] = local[:share].astype(bf16)
        local_ref[e, 1] = local[share:].astype(bf16)


def tile_kernel(interface_ref, block_ref):
    block_ref[...] = jnp.full(block_ref.shape, interface_ref[0].astype(f32))


def front_kernel(
    mask_hbm,
    modes_hbm,
    levels_hbm,
    coupling_hbm,
    shift_hbm,
    broad_hbm,
    inject_hbm,
    offsets_hbm,
    link2_ref,
    modes_ref,
    levels_ref,
    params_ref,
    offsets_ref,
    mask_ref,
    coupling_ref,
    sems,
):
    copies = [
        pltpu.make_async_copy(source, target, sems.at[index])
        for index, (source, target) in enumerate(
            (
                (mask_hbm, mask_ref),
                (offsets_hbm, offsets_ref),
                (coupling_hbm, coupling_ref),
                (shift_hbm, params_ref.at[0, 0:1]),
                (broad_hbm, params_ref.at[0, 1:2]),
                (inject_hbm, params_ref.at[0, 2:3]),
                (levels_hbm, levels_ref),
                (modes_hbm, modes_ref),
            )
        )
    ]
    for copy in copies:
        copy.start()
    for copy in copies:
        copy.wait()
    masked_link(link2_ref, coupling_ref, mask_ref)


def own_rows_kernel(overall, share, modes_ref, levels_ref, link2_ref, params_ref, left_ref, local_ref, free_ref):
    make_rows(
        params_ref.shape[2],
        0,
        overall,
        share,
        modes_ref,
        levels_ref,
        params_ref.at[0],
        link2_ref,
        left_ref,
        local_ref,
        free_ref,
    )


def both_kernel(had_ref, got_ref, both_ref):
    count = had_ref.shape[0]
    both_ref[0:count] = had_ref[...]
    both_ref[count:] = got_ref[...]


def rows_kernel(overall, share, hop, slot, modes_ref, levels_ref, link2_ref, got_ref, left_ref, local_ref):
    make_rows(
        got_ref.shape[2],
        hop,
        overall,
        share,
        modes_ref,
        levels_ref,
        got_ref.at[slot],
        link2_ref,
        left_ref,
        local_ref,
        None,
    )


spare = 16


def places(extent, width):
    row = lax.broadcasted_iota(jnp.int32, (extent, width), 0)
    lane = lax.broadcasted_iota(jnp.int32, (extent, width), 1)
    return row, jnp.where(lane < extent, lane, lane - extent), lane < extent


def pack_lesser(first, second):
    _, _, low = places(*first.shape)
    return jnp.where(low, first + swap_halves(first), second + swap_halves(second))


def with_turned(x):
    square = jnp.concatenate([x, swap_halves(x)], axis=0)
    return square, square.T


def unpack_lesser(packed):
    packed = packed.astype(f32)
    extent, width = packed.shape
    _, _, low = places(extent, width)
    square, turned = with_turned(packed)
    total, change = 0.5 * (square + turned), 0.5 * (square - turned)
    return (
        jnp.where(low, total[:extent], change[extent:]),
        jnp.where(low, total[extent:], change[:extent]),
    )


def pack_retarded(first, second):
    row, column, _ = places(*first.shape)
    diagonal = jnp.sum(jnp.where(row == column, second, 0.0), axis=0, keepdims=True)
    return jnp.where(row <= column, first, second), jnp.broadcast_to(diagonal, (spare, first.shape[1]))


def unpack_retarded(packed, diagonal):
    packed, diagonal = packed.astype(f32), diagonal.astype(f32)
    extent, width = packed.shape
    row, column, _ = places(extent, width)
    turned = with_turned(packed)[1][:extent]
    return (
        jnp.where(row <= column, packed, turned),
        jnp.where(row > column, packed, jnp.where(row == column, diagonal, turned)),
    )


def write_message(ref, maps):
    extent = maps[0][-1].shape[0]
    for pair in range(ref.shape[0]):
        first, second = maps[2 * pair], maps[2 * pair + 1]
        shared, diagonal = pack_retarded(first[-2], second[-2])
        ref[pair, 0:extent] = shared.astype(bf16)
        ref[pair, extent : 2 * extent] = pack_lesser(first[-1], second[-1]).astype(bf16)
        ref[pair, 2 * extent : 2 * extent + spare] = diagonal.astype(bf16)
        if ref.shape[1] > 2 * extent + spare:
            ref[pair, 2 * extent + spare : 3 * extent + spare] = first[0].astype(bf16)
            ref[pair, 3 * extent + spare :] = second[0].astype(bf16)


def read_message(ref):
    extent = ref.shape[2] // 2
    maps = []
    for pair in range(ref.shape[0]):
        retarded = unpack_retarded(ref[pair, 0:extent], ref[pair, 2 * extent : 2 * extent + 1])
        lesser = unpack_lesser(ref[pair, extent : 2 * extent])
        for which in range(2):
            start = (2 + which) * extent + spare
            front = (ref[pair, start : start + extent],) if ref.shape[1] > 2 * extent + spare else ()
            maps.append(front + (retarded[which].astype(bf16), lesser[which].astype(bf16)))
    return maps


def pushed(step, state):
    first = dot_mat(step[0], jnp.concatenate([full(state[0]), full(state[1])], axis=1)).astype(bf16)
    width = step[0].shape[1]
    return (
        dot_last(first[:, :width], full_conj(step[0])),
        dot_last(first[:, width:], full(step[0])),
    )


def compose(earlier, latter):
    retarded, lesser = pushed(latter, earlier[1:])
    return (
        dot_mat(latter[0], full(earlier[0])),
        latter[1].astype(f32) + retarded,
        latter[2].astype(f32) + lesser,
    )


def pick(flag, yes, no):
    return tuple(jnp.where(flag, a, b) for a, b in zip(yes, no))


def neutral(extent, width):
    row = lax.broadcasted_iota(jnp.int32, (extent, width), 0)
    lane = lax.broadcasted_iota(jnp.int32, (extent, width), 1)
    zero = jnp.zeros((extent, width), f32)
    return (jnp.where(row == lane, 1.0, 0.0).astype(bf16), zero.astype(bf16), zero.astype(bf16))


def read(ref, e):
    return tuple(ref[e, part] for part in range(ref.shape[1]))


def upper_half(level):
    return jnp.bitwise_and(jnp.right_shift(lax.axis_index("cell"), level), 1) == 1


def join_kernel(level, total_ref, other_ref, message_ref, *new_total_ref):
    upper = upper_half(level)
    others = read_message(other_ref)
    joined = []
    for e in range(total_ref.shape[0]):
        total, other = read(total_ref, e), others[e]
        pair = pick(upper, other, total), pick(upper, total, other)
        joined.append(compose(*pair) if new_total_ref else moved(pair[1], pair[0][1:]))
        for ref in new_total_ref:
            for part in range(3):
                ref[e, part] = joined[e][part].astype(bf16)
    write_message(message_ref, joined)


def enter_kernel(level, other_ref, *refs):
    upper = upper_half(level)
    others = read_message(other_ref)
    out_ref = refs[-1]
    for e in range(out_ref.shape[0]):
        if level:
            old = read(refs[0], e)
            new = pick(upper, tuple(x.astype(bf16) for x in compose(others[e], old)), old)
        else:
            new = pick(upper, others[e], neutral(*out_ref.shape[2:]))
        for part in range(3):
            out_ref[e, part] = new[part]


def moved(step, state):
    retarded, lesser = pushed(step, state)
    return step[1].astype(f32) + retarded, step[2].astype(f32) + lesser


def arrive_kernel(level, enter_ref, state_ref, retarded_ref, lesser_ref):
    upper = jnp.right_shift(lax.axis_index("cell"), level) == 1
    states = read_message(state_ref)
    lessers = []
    for e in range(enter_ref.shape[0]):
        enter = read(enter_ref, e)
        state = pick(upper, states[e], (jnp.zeros_like(enter[1]), jnp.zeros_like(enter[2])))
        retarded, lesser = pushed(enter, state)
        retarded_ref[e] = (enter[1].astype(f32) + retarded).astype(bf16)
        lessers.append(enter[2].astype(f32) + lesser)
    for pair in range(lesser_ref.shape[0]):
        lesser_ref[pair] = pack_lesser(lessers[2 * pair], lessers[2 * pair + 1]).astype(bf16)


def row_sums(x):
    return dot_last(jnp.ones((8, x.shape[1]), bf16), x.astype(bf16))[0:1]


def diagonal_kernel(overall, modes_ref, levels_ref, params_ref, out_ref, sums_ref):
    energies = params_ref.shape[2]
    first = lax.axis_index("energy") * energies
    modes = modes_ref[0].astype(f32)
    for e in range(energies):
        _, di = resolvents(overall, first, e, levels_ref, params_ref.at[0])
        out_ref[0, e : e + 1, :] = row_sums(modes * (modes * di).astype(bf16).astype(f32))
    blank = jnp.zeros(sums_ref.shape[2:], f32)
    for part in range(sums_ref.shape[0]):
        for e in range(sums_ref.shape[1]):
            sums_ref[part, e] = blank


def density_of(diagonal_ref, left_ref, retarded_ref, out_ref):
    for e in range(left_ref.shape[0]):
        left = left_ref[e]
        pz = dot_mat(left, full(retarded_ref[e])).astype(bf16).astype(f32)
        total = diagonal_ref[0, e : e + 1, :] + row_sums(pz * swap_halves(left.astype(f32)))
        out_ref[0, e : e + 1, :] = -total / math.pi


def convolve_kernel(reach, hop, last, offsets_ref, screen_ref, lesser_ref, left_ref, local_ref, _, *refs):
    if hop == 0:
        diagonal_ref, retarded_ref, *refs = refs
    sums_ref, *refs = refs
    if hop == 0:
        density_of(diagonal_ref, left_ref, retarded_ref, refs.pop(0))
    if last:
        out_hbm, *refs = refs
    g_ref, picked_ref, sem, *refs = refs
    copy = pltpu.make_async_copy(offsets_ref, picked_ref, sem)
    copy.start()
    energies = left_ref.shape[0]
    points, share, _ = screen_ref.shape[2:]
    overall = sums_ref.shape[1] - 2 * reach
    group = lax.axis_index("energy")
    mine = pl.multiple_of(group * share, share)
    base = jnp.bitwise_xor(group, hop) * energies + reach
    for pair in range(energies // 2):
        states = unpack_lesser(lesser_ref[pair])
        for e in (2 * pair, 2 * pair + 1):
            own = left_ref[e, pl.ds(mine, share), :]
            pl_hat = dot_mat(own, full(states[e - 2 * pair]))
            turned = swap_halves(pl_hat) * signs(pl_hat.shape[1], 1.0)
            chain = dot_last(jnp.concatenate([pl_hat, turned], axis=0).astype(bf16), left_ref[e])
            re = chain[:share] + local_ref[e, 0].astype(f32)
            im = chain[share:] + local_ref[e, 1].astype(f32)
            g_ref[0, e] = re + im
            g_ref[1, e] = im
            g_ref[2, e] = re
    copy.wait()
    height = 16

    def out_copy(step):
        rows = pl.ds(pl.multiple_of(step * height, height), height)
        return pltpu.make_async_copy(
            refs[0].at[:, :, :, rows, :], out_hbm.at[:, :, :, rows, :], refs[1].at[step]
        )

    def rows_of(step, _):
        rows = pl.ds(pl.multiple_of(step * height, height), height)
        held = [[g_ref[part, e, rows, :] for part in range(3)] for e in range(energies)]
        for k in range(points):
            w_re = screen_ref[0, 0, k, rows, :].astype(f32)
            w_im = screen_ref[0, 1, k, rows, :].astype(f32)
            factors = (w_re, w_re + w_im, w_im - w_re)
            for e in range(energies):
                target = base + e + picked_ref[k]
                for part in range(3):
                    sums_ref[part, target, rows, :] += factors[part] * held[e][part]
        if last:
            for e in range(overall):
                common = sums_ref[0, reach + e, rows, :]
                refs[0][0, 0, e, rows, :] = (-(common + sums_ref[2, reach + e, rows, :])).astype(bf16)
                refs[0][0, 1, e, rows, :] = (common - sums_ref[1, reach + e, rows, :]).astype(bf16)
            out_copy(step).start()
        return 0

    steps = share // height
    lax.fori_loop(0, steps, rows_of, 0)
    if last:
        for step in range(steps):
            out_copy(step).wait()


def in_hbm(x):
    return pltpu.with_memory_space_constraint(x, pltpu.HBM)


def call(kernel, out_shape, in_specs, scratch=(), flops=1_000_000, size=1_000_000, out_specs=None, aliases={}):
    outs = out_specs or jax.tree.map(lambda _: VMEM, out_shape)
    return pl.pallas_call(
        kernel,
        out_shape=out_shape,
        in_specs=in_specs,
        out_specs=outs,
        scratch_shapes=list(scratch),
        input_output_aliases=aliases,
        compiler_params=pltpu.CompilerParams(vmem_limit_bytes=16 << 20),
        cost_estimate=pl.CostEstimate(flops=flops, bytes_accessed=size, transcendentals=0),
    )


def body(
    modes,
    levels,
    level_shift,
    broadening,
    injection,
    coupling,
    row_mask,
    interface,
    screened,
    offsets,
):
    cells = lax.axis_size("cell")
    groups = lax.axis_size("energy")
    rounds = cells.bit_length() - 1
    assert cells == 1 << rounds and groups & (groups - 1) == 0
    energies = level_shift.shape[1]
    overall = energies * groups
    orbitals, extent = coupling.shape[1:]
    width = 2 * extent
    share = orbitals // groups
    sds = jax.ShapeDtypeStruct

    def swapped(x, axis, distance):
        return lax.ppermute(x, axis, [(i, i ^ distance) for i in range(lax.axis_size(axis))])

    assert energies % 2 == 0
    pairs = energies // 2
    maps_shape = sds((energies, 3, extent, width), bf16)
    message = sds((pairs, 4 * extent + spare, width), bf16)
    state_message = sds((pairs, 2 * extent + spare, width), bf16)
    coupling = jnp.swapaxes(coupling, 1, 2)
    block = call(tile_kernel, sds((8, width), f32), [SMEM])(interface)
    one = swapped(block, "cell", 1)
    mate = [i + 1 if i % 2 else i - 1 for i in range(cells)]
    mate[0], mate[-1] = 0, cells - 1
    route = [(i * groups + g, mate[i] * groups + (g ^ int(mate[i] == i))) for i in range(cells) for g in range(groups)]
    two = lax.ppermute(block, ("cell", "energy"), route)

    link2, modes, levels, params, offsets = call(
        front_kernel,
        (
            sds((width, 2 * orbitals), bf16),
            sds(modes.shape, bf16),
            sds(levels.shape, f32),
            sds((1, 3, energies, orbitals), f32),
            sds(offsets.shape, jnp.int32),
        ),
        [HBM] * 8,
        [
            pltpu.SMEM(row_mask.shape, jnp.int32),
            pltpu.VMEM(coupling.shape, bf16),
            pltpu.SemaphoreType.DMA((8,)),
        ],
    )(*map(in_hbm, (row_mask, modes, levels, coupling, level_shift, broadening, injection, offsets)))
    left_shape = sds((energies, orbitals, width), bf16)
    local_shape = sds((energies, 2, share, orbitals), bf16)
    params_shape = (3, energies, orbitals)
    left, local, free = call(
        partial(own_rows_kernel, overall, share),
        (left_shape, local_shape, sds((energies, orbitals, 2 * orbitals), bf16)),
        [VMEM] * 4,
    )(modes, levels, link2, params)
    lefts, locals_ = [left], [local]

    total, sent = call(
        partial(maps_kernel, overall),
        (maps_shape, message),
        [VMEM] * 7,
    )(one, two, modes, levels, params, left, free)
    reach = overall // 4
    sums_shape = sds((3, overall + 2 * reach, share, orbitals), f32)
    sigma_shape = sds((1, 2, overall, share, orbitals), bf16)
    density_shape = sds((1, energies, orbitals), f32)
    diagonal, sums = call(
        partial(diagonal_kernel, overall), (density_shape, sums_shape), [VMEM] * 3
    )(modes, levels, params)

    known = params
    while known.shape[0] < groups:
        count = known.shape[0]
        got = swapped(known, "energy", count)
        if 2 * count < groups:
            known = call(both_kernel, sds((2 * count,) + params_shape, f32), [VMEM] * 2)(known, got)
        for slot in range(count):
            left, local = call(
                partial(rows_kernel, overall, share, count + slot, slot), (left_shape, local_shape), [VMEM] * 4
            )(modes, levels, link2, got)
            lefts.append(left)
            locals_.append(local)
        if 2 * count >= groups:
            break

    enter = None
    for level in range(rounds - 1):
        other = swapped(sent, "cell", 1 << level)
        outs = (message, maps_shape) if level < rounds - 2 else (state_message,)
        sent, *rest = call(partial(join_kernel, level), outs, [VMEM] * 2)(total, other)
        total = rest[0] if rest else None
        given = (other, enter) if level else (other,)
        enter = call(partial(enter_kernel, level), maps_shape, [VMEM] * len(given))(*given)
    state = swapped(sent, "cell", cells // 2)
    retarded, lesser = call(
        partial(arrive_kernel, rounds - 1),
        (sds((energies, extent, width), bf16), sds((pairs, extent, width), bf16)),
        [VMEM, VMEM],
    )(enter, state)

    lessers = [lesser]
    for hop in range(1, groups):
        lessers.append(swapped(lesser, "energy", hop))
    scratch = [
        pltpu.VMEM((3, energies, share, orbitals), f32),
        pltpu.SMEM(offsets.shape, jnp.int32),
        pltpu.SemaphoreType.DMA,
    ]
    for hop in range(groups):
        last = hop == groups - 1
        given = (offsets, screened, lessers[hop], lefts[hop], locals_[hop], sums)
        outs, specs, extra = (sums_shape,), (VMEM,), []
        if hop == 0:
            given += (diagonal, retarded)
            outs, specs = outs + (density_shape,), specs + (VMEM,)
        if last:
            outs, specs = outs + (sigma_shape,), specs + (HBM,)
            extra = [pltpu.VMEM(sigma_shape.shape, bf16), pltpu.SemaphoreType.DMA((share // 16,))]
        sums, *rest = call(
            partial(convolve_kernel, reach, hop, last),
            outs,
            [VMEM] * len(given),
            scratch + extra,
            out_specs=specs,
            aliases={5: 0},
        )(*given)
        if hop == 0:
            density = rest[0]
    sigma = rest[-1]
    return (density, sigma)


def solution(mesh):
    placed = (
        P("cell", None, None),
        P("cell", None),
        P("cell", "energy", None),
        P("cell", "energy", None),
        P("cell", "energy", None),
        P("cell", None, None),
        P("cell", None),
        P("cell"),
        P("cell", None, None, "energy", None),
        P(),
    )
    return jax.shard_map(
        body,
        mesh=mesh,
        in_specs=placed,
        out_specs=(P("cell", "energy", None), P("cell", None, None, "energy", None)),
        check_vma=False,
    )
```

```python
from functools import partial
import math

import jax
import jax.numpy as jnp
from jax import lax
from jax.experimental import pallas as pl
from jax.experimental.pallas import tpu as pltpu
from jax.sharding import PartitionSpec as P


broaden_base = 1.0
energy_low = -0.25
energy_span = 0.5
f32 = jnp.float32
bf16 = jnp.bfloat16

VMEM = pl.BlockSpec(memory_space=pltpu.VMEM)
SMEM = pl.BlockSpec(memory_space=pltpu.SMEM)
HBM = pl.BlockSpec(memory_space=pltpu.HBM)


def dot_last(a, b, precision=None):
    return lax.dot_general(
        a, b, (((1,), (1,)), ((), ())), precision=precision, preferred_element_type=f32
    )


def dot_mat(a, b):
    return lax.dot_general(a, b, (((1,), (0,)), ((), ())), preferred_element_type=f32)


def signs(width, left_sign):
    lane = lax.broadcasted_iota(jnp.int32, (1, width), 1)
    return jnp.where(lane < width // 2, left_sign, -left_sign).astype(f32)


def swap_halves(x):
    return pltpu.roll(x, x.shape[1] // 2, 1)


def full(x):
    x = x.astype(f32)
    return jnp.concatenate([x, swap_halves(x) * signs(x.shape[1], -1.0)], axis=0).astype(bf16)


def full_conj(x):
    x = x.astype(f32)
    return jnp.concatenate([x * signs(x.shape[1], 1.0), swap_halves(x)], axis=0).astype(bf16)


def resolvent(levels, shift, broad, index, overall):
    eps = energy_low + energy_span * (index.astype(f32) + 0.5) / overall
    detune = eps - levels - shift
    damping = broaden_base + broad
    inverse = 1.0 / (detune * detune + damping * damping)
    return detune * inverse, -damping * inverse


def masked_link(coupling_ref, mask_ref):
    _, rows = coupling_ref.shape[1:]
    count = mask_ref.shape[1]
    block = lax.broadcasted_iota(jnp.int32, (1, rows), 1) // (rows // count)
    keep = jnp.zeros((1, rows), f32)
    for index in range(count):
        keep = jnp.where(block == index, mask_ref[0, index].astype(f32), keep)
    return (coupling_ref[0].astype(f32) * keep).astype(bf16)


def resolvents(overall, first, e, levels_ref, params_ref):
    return resolvent(levels_ref[...], params_ref[0, e : e + 1, :], params_ref[1, e : e + 1, :], first + e, overall)


def both_scaled(x, dr, di, axis):
    return jnp.concatenate([x * dr, x * di], axis=axis).astype(bf16)


def maps_kernel(
    overall, one_ref, two_ref, modes_ref, levels_ref, params_ref, mixed_ref, out_ref
):
    energies = params_ref.shape[2]
    extent = out_ref.shape[2]
    first = lax.axis_index("energy") * energies
    odd = jnp.bitwise_and(lax.axis_index("cell"), 1) == 1
    block = jnp.max(jnp.where(odd, two_ref[...], one_ref[...])).astype(jnp.int32)
    chosen = pl.multiple_of(block * extent, extent)
    modes = modes_ref[0]
    rows = modes_ref[0, pl.ds(chosen, extent), :]
    rows_f = rows.astype(f32)
    none = jnp.zeros_like(rows)
    rows2 = jnp.concatenate(
        [jnp.concatenate([rows, none], axis=1), jnp.concatenate([none, rows], axis=1)], axis=0
    )
    mixed = mixed_ref[...]
    for e in range(energies):
        dr, di = resolvents(overall, first, e, levels_ref, params_ref.at[0])
        free = dot_last(both_scaled(rows_f, dr, di, 0), modes)
        re, im = free[:extent], free[extent:]
        weight = params_ref[0, 2, e : e + 1, :]
        weighted = jnp.concatenate([re * weight, im * weight], axis=1).astype(bf16)
        straight = jnp.concatenate([re, im], axis=1)
        turned = jnp.concatenate([-im, re], axis=1)
        out_ref[e, 0] = dot_last(rows, both_scaled(mixed, dr, di, 0)).astype(bf16)
        out_ref[e, 1] = dot_last(both_scaled(rows_f, dr, di, 1), rows2).astype(bf16)
        out_ref[e, 2] = dot_last(weighted, jnp.concatenate([straight, turned], axis=0).astype(bf16)).astype(bf16)


def rows_kernel(overall, share, hop, slot, modes_ref, levels_ref, mixed_ref, params_ref, left_ref, local_ref):
    energies = params_ref.shape[2]
    group = lax.axis_index("energy")
    first = jnp.bitwise_xor(group, hop) * energies
    modes = modes_ref[0]
    mixed = mixed_ref[...]
    mine = pl.multiple_of(group * share, share)
    rows_f = modes_ref[0, pl.ds(mine, share), :].astype(f32)
    given = [resolvents(overall, first, e, levels_ref, params_ref.at[slot]) for e in range(energies)]
    own = dot_last(jnp.concatenate([both_scaled(rows_f, dr, di, 0) for dr, di in given], axis=0), modes)
    weighted = [
        own[2 * share * e : 2 * share * (e + 1)] * params_ref[slot, 2, e : e + 1, :] for e in range(energies)
    ]
    back = dot_mat(jnp.concatenate(weighted, axis=0).astype(bf16), modes)
    parts = []
    for e, (dr, di) in enumerate(given):
        re = back[2 * share * e : 2 * share * e + share]
        im = back[2 * share * e + share : 2 * share * (e + 1)]
        parts += [re * dr + im * di, im * dr - re * di]
    local = dot_last(jnp.concatenate(parts, axis=0).astype(bf16), modes)
    for e, (dr, di) in enumerate(given):
        left_ref[e] = dot_last(modes, both_scaled(mixed, dr, di, 0)).astype(bf16)
        for part in range(2):
            start = (2 * e + part) * share
            local_ref[e, part] = local[start : start + share].astype(bf16)


def tile_kernel(interface_ref, block_ref):
    block_ref[...] = jnp.full(block_ref.shape, interface_ref[0].astype(f32))


def front_kernel(
    mask_hbm,
    modes_hbm,
    levels_hbm,
    coupling_hbm,
    shift_hbm,
    broad_hbm,
    inject_hbm,
    offsets_hbm,
    mixed_ref,
    modes_ref,
    levels_ref,
    params_ref,
    offsets_ref,
    mask_ref,
    coupling_ref,
    sems,
):
    copies = [
        pltpu.make_async_copy(source, target, sems.at[index])
        for index, (source, target) in enumerate(
            (
                (mask_hbm, mask_ref),
                (offsets_hbm, offsets_ref),
                (coupling_hbm, coupling_ref),
                (shift_hbm, params_ref.at[0, 0:1]),
                (broad_hbm, params_ref.at[0, 1:2]),
                (inject_hbm, params_ref.at[0, 2:3]),
                (levels_hbm, levels_ref),
                (modes_hbm, modes_ref),
            )
        )
    ]
    for copy in copies:
        copy.start()
    for copy in copies:
        copy.wait()
    mixed_ref[...] = dot_mat(masked_link(coupling_ref, mask_ref), modes_ref[0])


def both_kernel(had_ref, got_ref, both_ref):
    count = had_ref.shape[0]
    both_ref[0:count] = had_ref[...]
    both_ref[count:] = got_ref[...]


spare = 16


def places(extent, width):
    row = lax.broadcasted_iota(jnp.int32, (extent, width), 0)
    lane = lax.broadcasted_iota(jnp.int32, (extent, width), 1)
    return row, jnp.where(lane < extent, lane, lane - extent), lane < extent


def pack_lesser(first, second):
    _, _, low = places(*first.shape)
    return jnp.where(low, first + swap_halves(first), second + swap_halves(second))


def with_turned(x):
    square = jnp.concatenate([x, swap_halves(x)], axis=0)
    return square, square.T


def unpack_lesser(packed):
    packed = packed.astype(f32)
    extent, width = packed.shape
    _, _, low = places(extent, width)
    square, turned = with_turned(packed)
    total, change = 0.5 * (square + turned), 0.5 * (square - turned)
    return (
        jnp.where(low, total[:extent], change[extent:]),
        jnp.where(low, total[extent:], change[:extent]),
    )


def pack_retarded(first, second):
    row, column, _ = places(*first.shape)
    diagonal = jnp.sum(jnp.where(row == column, second, 0.0), axis=0, keepdims=True)
    return jnp.where(row <= column, first, second), jnp.broadcast_to(diagonal, (spare, first.shape[1]))


def unpack_retarded(packed, diagonal):
    packed, diagonal = packed.astype(f32), diagonal.astype(f32)
    extent, width = packed.shape
    row, column, _ = places(extent, width)
    turned = with_turned(packed)[1][:extent]
    return (
        jnp.where(row <= column, packed, turned),
        jnp.where(row > column, packed, jnp.where(row == column, diagonal, turned)),
    )


def write_message(ref, maps):
    extent = maps[0][-1].shape[0]
    for pair in range(ref.shape[0]):
        first, second = maps[2 * pair], maps[2 * pair + 1]
        shared, diagonal = pack_retarded(first[-2], second[-2])
        ref[pair, 0:extent] = shared.astype(bf16)
        ref[pair, extent : 2 * extent] = pack_lesser(first[-1], second[-1]).astype(bf16)
        ref[pair, 2 * extent : 2 * extent + spare] = diagonal.astype(bf16)
        if ref.shape[1] > 2 * extent + spare:
            ref[pair, 2 * extent + spare : 3 * extent + spare] = first[0].astype(bf16)
            ref[pair, 3 * extent + spare :] = second[0].astype(bf16)


def read_maps(ref):
    if len(ref.shape) == 4:
        return [read(ref, e) for e in range(ref.shape[0])]
    return read_message(ref)


def read_message(ref):
    extent = ref.shape[2] // 2
    maps = []
    for pair in range(ref.shape[0]):
        retarded = unpack_retarded(ref[pair, 0:extent], ref[pair, 2 * extent : 2 * extent + 1])
        lesser = unpack_lesser(ref[pair, extent : 2 * extent])
        for which in range(2):
            start = (2 + which) * extent + spare
            front = (ref[pair, start : start + extent],) if ref.shape[1] > 2 * extent + spare else ()
            maps.append(front + (retarded[which].astype(bf16), lesser[which].astype(bf16)))
    return maps


def pushed(step, state):
    first = dot_mat(step[0], jnp.concatenate([full(state[0]), full(state[1])], axis=1)).astype(bf16)
    width = step[0].shape[1]
    return (
        dot_last(first[:, :width], full_conj(step[0])),
        dot_last(first[:, width:], full(step[0])),
    )


def compose(earlier, latter):
    retarded, lesser = pushed(latter, earlier[1:])
    return (
        dot_mat(latter[0], full(earlier[0])),
        latter[1].astype(f32) + retarded,
        latter[2].astype(f32) + lesser,
    )


def pick(flag, yes, no):
    return tuple(jnp.where(flag, a, b) for a, b in zip(yes, no))


def neutral(extent, width):
    row = lax.broadcasted_iota(jnp.int32, (extent, width), 0)
    lane = lax.broadcasted_iota(jnp.int32, (extent, width), 1)
    zero = jnp.zeros((extent, width), f32)
    return (jnp.where(row == lane, 1.0, 0.0).astype(bf16), zero.astype(bf16), zero.astype(bf16))


def read(ref, e):
    return tuple(ref[e, part] for part in range(ref.shape[1]))


def upper_half(level):
    return jnp.bitwise_and(jnp.right_shift(lax.axis_index("cell"), level), 1) == 1


def join_kernel(level, total_ref, other_ref, message_ref, *new_total_ref):
    upper = upper_half(level)
    others = read_maps(other_ref)
    joined = []
    for e in range(total_ref.shape[0]):
        total, other = read(total_ref, e), others[e]
        pair = pick(upper, other, total), pick(upper, total, other)
        joined.append(compose(*pair) if new_total_ref else moved(pair[1], pair[0][1:]))
        for ref in new_total_ref:
            for part in range(3):
                ref[e, part] = joined[e][part].astype(bf16)
    write_message(message_ref, joined)


def enter_kernel(level, other_ref, *refs):
    upper = upper_half(level)
    others = read_maps(other_ref)
    out_ref = refs[-1]
    for e in range(out_ref.shape[0]):
        if level:
            old = read(refs[0], e)
            new = pick(upper, tuple(x.astype(bf16) for x in compose(others[e], old)), old)
        else:
            new = pick(upper, others[e], neutral(*out_ref.shape[2:]))
        for part in range(3):
            out_ref[e, part] = new[part]


def moved(step, state):
    retarded, lesser = pushed(step, state)
    return step[1].astype(f32) + retarded, step[2].astype(f32) + lesser


def arrive_kernel(level, enter_ref, state_ref, retarded_ref, lesser_ref):
    upper = jnp.right_shift(lax.axis_index("cell"), level) == 1
    states = read_message(state_ref)
    lessers = []
    for e in range(enter_ref.shape[0]):
        enter = read(enter_ref, e)
        state = pick(upper, states[e], (jnp.zeros_like(enter[1]), jnp.zeros_like(enter[2])))
        retarded, lesser = pushed(enter, state)
        retarded_ref[e] = (enter[1].astype(f32) + retarded).astype(bf16)
        lessers.append(enter[2].astype(f32) + lesser)
    for pair in range(lesser_ref.shape[0]):
        lesser_ref[pair] = pack_lesser(lessers[2 * pair], lessers[2 * pair + 1]).astype(bf16)


def row_sums(x):
    return dot_last(jnp.ones((8, x.shape[1]), bf16), x.astype(bf16))[0:1]


def diagonal_kernel(overall, modes_ref, levels_ref, params_ref, out_ref, sums_ref):
    energies = params_ref.shape[2]
    first = lax.axis_index("energy") * energies
    modes = modes_ref[0].astype(f32)
    for e in range(energies):
        _, di = resolvents(overall, first, e, levels_ref, params_ref.at[0])
        out_ref[0, e : e + 1, :] = row_sums(modes * (modes * di).astype(bf16).astype(f32))
    blank = jnp.zeros(sums_ref.shape[2:], f32)
    for part in range(sums_ref.shape[0]):
        for e in range(sums_ref.shape[1]):
            sums_ref[part, e] = blank


def density_of(diagonal_ref, left_ref, retarded_ref, out_ref):
    for e in range(left_ref.shape[0]):
        left = left_ref[e]
        pz = dot_mat(left, full(retarded_ref[e])).astype(bf16).astype(f32)
        total = diagonal_ref[0, e : e + 1, :] + row_sums(pz * swap_halves(left.astype(f32)))
        out_ref[0, e : e + 1, :] = -total / math.pi


def convolve_kernel(reach, hop, last, offsets_ref, screen_ref, lesser_ref, left_ref, local_ref, _, *refs):
    if hop == 0:
        diagonal_ref, retarded_ref, *refs = refs
    sums_ref, *refs = refs
    if hop == 0:
        density_of(diagonal_ref, left_ref, retarded_ref, refs.pop(0))
    if last:
        out_hbm, *refs = refs
    g_ref, picked_ref, sem, *refs = refs
    copy = pltpu.make_async_copy(offsets_ref, picked_ref, sem)
    copy.start()
    energies = left_ref.shape[0]
    points, share, _ = screen_ref.shape[2:]
    overall = sums_ref.shape[1] - 2 * reach
    group = lax.axis_index("energy")
    mine = pl.multiple_of(group * share, share)
    base = jnp.bitwise_xor(group, hop) * energies + reach
    for pair in range(energies // 2):
        states = unpack_lesser(lesser_ref[pair])
        for e in (2 * pair, 2 * pair + 1):
            own = left_ref[e, pl.ds(mine, share), :]
            pl_hat = dot_mat(own, full(states[e - 2 * pair]))
            turned = swap_halves(pl_hat) * signs(pl_hat.shape[1], 1.0)
            chain = dot_last(jnp.concatenate([pl_hat, turned], axis=0).astype(bf16), left_ref[e])
            re = chain[:share] + local_ref[e, 0].astype(f32)
            im = chain[share:] + local_ref[e, 1].astype(f32)
            g_ref[0, e] = re + im
            g_ref[1, e] = im
            g_ref[2, e] = re
    copy.wait()
    height = 16

    def out_copy(step):
        rows = pl.ds(pl.multiple_of(step * height, height), height)
        return pltpu.make_async_copy(
            refs[0].at[:, :, :, rows, :], out_hbm.at[:, :, :, rows, :], refs[1].at[step]
        )

    def rows_of(step, _):
        rows = pl.ds(pl.multiple_of(step * height, height), height)
        held = [[g_ref[part, e, rows, :] for part in range(3)] for e in range(energies)]
        for k in range(points):
            w_re = screen_ref[0, 0, k, rows, :].astype(f32)
            w_im = screen_ref[0, 1, k, rows, :].astype(f32)
            factors = (w_re, w_re + w_im, w_im - w_re)
            for e in range(energies):
                target = base + e + picked_ref[k]
                for part in range(3):
                    sums_ref[part, target, rows, :] += factors[part] * held[e][part]
        if last:
            for e in range(overall):
                common = sums_ref[0, reach + e, rows, :]
                refs[0][0, 0, e, rows, :] = (-(common + sums_ref[2, reach + e, rows, :])).astype(bf16)
                refs[0][0, 1, e, rows, :] = (common - sums_ref[1, reach + e, rows, :]).astype(bf16)
            out_copy(step).start()
        return 0

    steps = share // height
    lax.fori_loop(0, steps, rows_of, 0)
    if last:
        for step in range(steps):
            out_copy(step).wait()


def in_hbm(x):
    return pltpu.with_memory_space_constraint(x, pltpu.HBM)


def call(kernel, out_shape, in_specs, scratch=(), flops=1_000_000, size=1_000_000, out_specs=None, aliases={}):
    outs = out_specs or jax.tree.map(lambda _: VMEM, out_shape)
    return pl.pallas_call(
        kernel,
        out_shape=out_shape,
        in_specs=in_specs,
        out_specs=outs,
        scratch_shapes=list(scratch),
        input_output_aliases=aliases,
        compiler_params=pltpu.CompilerParams(vmem_limit_bytes=16 << 20),
        cost_estimate=pl.CostEstimate(flops=flops, bytes_accessed=size, transcendentals=0),
    )


def body(
    modes,
    levels,
    level_shift,
    broadening,
    injection,
    coupling,
    row_mask,
    interface,
    screened,
    offsets,
):
    cells = lax.axis_size("cell")
    groups = lax.axis_size("energy")
    rounds = cells.bit_length() - 1
    assert cells == 1 << rounds and groups & (groups - 1) == 0
    energies = level_shift.shape[1]
    overall = energies * groups
    orbitals, extent = coupling.shape[1:]
    width = 2 * extent
    share = orbitals // groups
    sds = jax.ShapeDtypeStruct

    def swapped(x, axis, distance):
        return lax.ppermute(x, axis, [(i, i ^ distance) for i in range(lax.axis_size(axis))])

    assert energies % 2 == 0
    pairs = energies // 2
    maps_shape = sds((energies, 3, extent, width), bf16)
    message = sds((pairs, 4 * extent + spare, width), bf16)
    state_message = sds((pairs, 2 * extent + spare, width), bf16)
    coupling = jnp.swapaxes(coupling, 1, 2)
    block = call(tile_kernel, sds((8, width), f32), [SMEM])(interface)
    one = swapped(block, "cell", 1)
    mate = [i + 1 if i % 2 else i - 1 for i in range(cells)]
    mate[0], mate[-1] = 0, cells - 1
    route = [(i * groups + g, mate[i] * groups + (g ^ int(mate[i] == i))) for i in range(cells) for g in range(groups)]
    two = lax.ppermute(block, ("cell", "energy"), route)

    mixed, modes, levels, params, offsets = call(
        front_kernel,
        (
            sds((extent, orbitals), f32),
            sds(modes.shape, bf16),
            sds(levels.shape, f32),
            sds((1, 3, energies, orbitals), f32),
            sds(offsets.shape, jnp.int32),
        ),
        [HBM] * 8,
        [
            pltpu.SMEM(row_mask.shape, jnp.int32),
            pltpu.VMEM(coupling.shape, bf16),
            pltpu.SemaphoreType.DMA((8,)),
        ],
    )(*map(in_hbm, (row_mask, modes, levels, coupling, level_shift, broadening, injection, offsets)))
    left_shape = sds((energies, orbitals, width), bf16)
    local_shape = sds((energies, 2, share, orbitals), bf16)
    params_shape = (3, energies, orbitals)
    left, local = call(partial(rows_kernel, overall, share, 0, 0), (left_shape, local_shape), [VMEM] * 4)(
        modes, levels, mixed, params
    )
    lefts, locals_ = [left], [local]

    total = call(partial(maps_kernel, overall), maps_shape, [VMEM] * 6)(one, two, modes, levels, params, mixed)
    sent = total
    reach = overall // 4
    sums_shape = sds((3, overall + 2 * reach, share, orbitals), f32)
    sigma_shape = sds((1, 2, overall, share, orbitals), bf16)
    density_shape = sds((1, energies, orbitals), f32)
    diagonal, sums = call(
        partial(diagonal_kernel, overall), (density_shape, sums_shape), [VMEM] * 3
    )(modes, levels, params)

    known = params
    while known.shape[0] < groups:
        count = known.shape[0]
        got = swapped(known, "energy", count)
        if 2 * count < groups:
            known = call(both_kernel, sds((2 * count,) + params_shape, f32), [VMEM] * 2)(known, got)
        for slot in range(count):
            left, local = call(
                partial(rows_kernel, overall, share, count + slot, slot), (left_shape, local_shape), [VMEM] * 4
            )(modes, levels, mixed, got)
            lefts.append(left)
            locals_.append(local)
        if 2 * count >= groups:
            break

    enter = None
    for level in range(rounds - 1):
        other = swapped(sent, "cell", 1 << level)
        outs = (message, maps_shape) if level < rounds - 2 else (state_message,)
        sent, *rest = call(partial(join_kernel, level), outs, [VMEM] * 2)(total, other)
        total = rest[0] if rest else None
        given = (other, enter) if level else (other,)
        enter = call(partial(enter_kernel, level), maps_shape, [VMEM] * len(given))(*given)
    state = swapped(sent, "cell", cells // 2)
    retarded, lesser = call(
        partial(arrive_kernel, rounds - 1),
        (sds((energies, extent, width), bf16), sds((pairs, extent, width), bf16)),
        [VMEM, VMEM],
    )(enter, state)

    lessers = [lesser]
    for hop in range(1, groups):
        lessers.append(swapped(lesser, "energy", hop))
    scratch = [
        pltpu.VMEM((3, energies, share, orbitals), f32),
        pltpu.SMEM(offsets.shape, jnp.int32),
        pltpu.SemaphoreType.DMA,
    ]
    for hop in range(groups):
        last = hop == groups - 1
        given = (offsets, screened, lessers[hop], lefts[hop], locals_[hop], sums)
        outs, specs, extra = (sums_shape,), (VMEM,), []
        if hop == 0:
            given += (diagonal, retarded)
            outs, specs = outs + (density_shape,), specs + (VMEM,)
        if last:
            outs, specs = outs + (sigma_shape,), specs + (HBM,)
            extra = [pltpu.VMEM(sigma_shape.shape, bf16), pltpu.SemaphoreType.DMA((share // 16,))]
        sums, *rest = call(
            partial(convolve_kernel, reach, hop, last),
            outs,
            [VMEM] * len(given),
            scratch + extra,
            out_specs=specs,
            aliases={5: 0},
        )(*given)
        if hop == 0:
            density = rest[0]
    sigma = rest[-1]
    return (density, sigma)


def solution(mesh):
    placed = (
        P("cell", None, None),
        P("cell", None),
        P("cell", "energy", None),
        P("cell", "energy", None),
        P("cell", "energy", None),
        P("cell", None, None),
        P("cell", None),
        P("cell"),
        P("cell", None, None, "energy", None),
        P(),
    )
    return jax.shard_map(
        body,
        mesh=mesh,
        in_specs=placed,
        out_specs=(P("cell", "energy", None), P("cell", None, None, "energy", None)),
        check_vma=False,
    )
```

```python
from functools import partial
import math

import jax
import jax.numpy as jnp
from jax import lax
from jax.experimental import pallas as pl
from jax.experimental.pallas import tpu as pltpu
from jax.sharding import PartitionSpec as P


broaden_base = 1.0
energy_low = -0.25
energy_span = 0.5
f32 = jnp.float32
bf16 = jnp.bfloat16

VMEM = pl.BlockSpec(memory_space=pltpu.VMEM)
SMEM = pl.BlockSpec(memory_space=pltpu.SMEM)
HBM = pl.BlockSpec(memory_space=pltpu.HBM)


def dot_last(a, b, precision=None):
    return lax.dot_general(
        a, b, (((1,), (1,)), ((), ())), precision=precision, preferred_element_type=f32
    )


def dot_mat(a, b):
    return lax.dot_general(a, b, (((1,), (0,)), ((), ())), preferred_element_type=f32)


def signs(width, left_sign):
    lane = lax.broadcasted_iota(jnp.int32, (1, width), 1)
    return jnp.where(lane < width // 2, left_sign, -left_sign).astype(f32)


def swap_halves(x):
    return pltpu.roll(x, x.shape[1] // 2, 1)


def full(x):
    x = x.astype(f32)
    return jnp.concatenate([x, swap_halves(x) * signs(x.shape[1], -1.0)], axis=0).astype(bf16)


def full_conj(x):
    x = x.astype(f32)
    return jnp.concatenate([x * signs(x.shape[1], 1.0), swap_halves(x)], axis=0).astype(bf16)


def resolvent(levels, shift, broad, index, overall):
    eps = energy_low + energy_span * (index.astype(f32) + 0.5) / overall
    detune = eps - levels - shift
    damping = broaden_base + broad
    inverse = 1.0 / (detune * detune + damping * damping)
    return detune * inverse, -damping * inverse


def masked_link(coupling_ref, mask_ref):
    _, rows = coupling_ref.shape[1:]
    count = mask_ref.shape[1]
    block = lax.broadcasted_iota(jnp.int32, (1, rows), 1) // (rows // count)
    keep = jnp.zeros((1, rows), f32)
    for index in range(count):
        keep = jnp.where(block == index, mask_ref[0, index].astype(f32), keep)
    return (coupling_ref[0].astype(f32) * keep).astype(bf16)


def resolvents(overall, first, e, levels_ref, params_ref):
    return resolvent(levels_ref[...], params_ref[0, e : e + 1, :], params_ref[1, e : e + 1, :], first + e, overall)


def both_scaled(x, dr, di, axis):
    return jnp.concatenate([x * dr, x * di], axis=axis).astype(bf16)


def maps_kernel(
    overall, one_ref, two_ref, modes_ref, levels_ref, params_ref, mixed_ref, out_ref
):
    energies = params_ref.shape[2]
    extent = out_ref.shape[2]
    first = lax.axis_index("energy") * energies
    odd = jnp.bitwise_and(lax.axis_index("cell"), 1) == 1
    block = jnp.max(jnp.where(odd, two_ref[...], one_ref[...])).astype(jnp.int32)
    chosen = pl.multiple_of(block * extent, extent)
    modes = modes_ref[0]
    rows = modes_ref[0, pl.ds(chosen, extent), :]
    rows_f = rows.astype(f32)
    none = jnp.zeros_like(rows)
    rows2 = jnp.concatenate(
        [jnp.concatenate([rows, none], axis=1), jnp.concatenate([none, rows], axis=1)], axis=0
    )
    mixed = mixed_ref[...]
    for e in range(energies):
        dr, di = resolvents(overall, first, e, levels_ref, params_ref.at[0])
        free = dot_last(both_scaled(rows_f, dr, di, 0), modes)
        re, im = free[:extent], free[extent:]
        weight = params_ref[0, 2, e : e + 1, :]
        weighted = jnp.concatenate([re * weight, im * weight], axis=1).astype(bf16)
        straight = jnp.concatenate([re, im], axis=1)
        turned = jnp.concatenate([-im, re], axis=1)
        out_ref[e, 0] = dot_last(rows, both_scaled(mixed, dr, di, 0)).astype(bf16)
        out_ref[e, 1] = dot_last(both_scaled(rows_f, dr, di, 1), rows2).astype(bf16)
        out_ref[e, 2] = dot_last(weighted, jnp.concatenate([straight, turned], axis=0).astype(bf16)).astype(bf16)


def rows_kernel(overall, share, hop, slot, modes_ref, levels_ref, mixed_ref, params_ref, left_ref, local_ref):
    energies = params_ref.shape[2]
    group = lax.axis_index("energy")
    first = jnp.bitwise_xor(group, hop) * energies
    modes = modes_ref[0]
    mixed = mixed_ref[...]
    mine = pl.multiple_of(group * share, share)
    rows_f = modes_ref[0, pl.ds(mine, share), :].astype(f32)
    given = [resolvents(overall, first, e, levels_ref, params_ref.at[slot]) for e in range(energies)]
    own = dot_last(jnp.concatenate([both_scaled(rows_f, dr, di, 0) for dr, di in given], axis=0), modes)
    weighted = [
        own[2 * share * e : 2 * share * (e + 1)] * params_ref[slot, 2, e : e + 1, :] for e in range(energies)
    ]
    back = dot_mat(jnp.concatenate(weighted, axis=0).astype(bf16), modes)
    parts = []
    for e, (dr, di) in enumerate(given):
        re = back[2 * share * e : 2 * share * e + share]
        im = back[2 * share * e + share : 2 * share * (e + 1)]
        parts += [re * dr + im * di, im * dr - re * di]
    local = dot_last(jnp.concatenate(parts, axis=0).astype(bf16), modes)
    for e, (dr, di) in enumerate(given):
        left_ref[e] = dot_last(modes, both_scaled(mixed, dr, di, 0)).astype(bf16)
        for part in range(2):
            start = (2 * e + part) * share
            local_ref[e, part] = local[start : start + share].astype(bf16)


def tile_kernel(interface_ref, block_ref):
    block_ref[...] = jnp.full(block_ref.shape, interface_ref[0].astype(f32))


def front_kernel(
    mask_hbm,
    modes_hbm,
    levels_hbm,
    coupling_hbm,
    shift_hbm,
    broad_hbm,
    inject_hbm,
    offsets_hbm,
    mixed_ref,
    modes_ref,
    levels_ref,
    params_ref,
    offsets_ref,
    mask_ref,
    coupling_ref,
    sems,
):
    copies = [
        pltpu.make_async_copy(source, target, sems.at[index])
        for index, (source, target) in enumerate(
            (
                (mask_hbm, mask_ref),
                (offsets_hbm, offsets_ref),
                (coupling_hbm, coupling_ref),
                (shift_hbm, params_ref.at[0, 0:1]),
                (broad_hbm, params_ref.at[0, 1:2]),
                (inject_hbm, params_ref.at[0, 2:3]),
                (levels_hbm, levels_ref),
                (modes_hbm, modes_ref),
            )
        )
    ]
    for copy in copies:
        copy.start()
    for copy in copies:
        copy.wait()
    mixed_ref[...] = dot_mat(masked_link(coupling_ref, mask_ref), modes_ref[0])


def both_kernel(had_ref, got_ref, both_ref):
    count = had_ref.shape[0]
    both_ref[0:count] = had_ref[...]
    both_ref[count:] = got_ref[...]


spare = 16


def places(extent, width):
    row = lax.broadcasted_iota(jnp.int32, (extent, width), 0)
    lane = lax.broadcasted_iota(jnp.int32, (extent, width), 1)
    return row, jnp.where(lane < extent, lane, lane - extent), lane < extent


def pack_lesser(first, second):
    _, _, low = places(*first.shape)
    return jnp.where(low, first + swap_halves(first), second + swap_halves(second))


def with_turned(x):
    square = jnp.concatenate([x, swap_halves(x)], axis=0)
    return square, square.T


def unpack_lesser(packed):
    packed = packed.astype(f32)
    extent, width = packed.shape
    _, _, low = places(extent, width)
    square, turned = with_turned(packed)
    total, change = 0.5 * (square + turned), 0.5 * (square - turned)
    return (
        jnp.where(low, total[:extent], change[extent:]),
        jnp.where(low, total[extent:], change[:extent]),
    )


def unpack_full_lesser(packed):
    packed = packed.astype(f32)
    extent, width = packed.shape
    _, _, low = places(extent, width)
    square, turned = with_turned(packed)
    total, change = 0.5 * (square + turned), 0.5 * (square - turned)
    upper, lower = (total[:extent], change[:extent]), (total[extent:], change[extent:])
    return tuple(
        jnp.concatenate([jnp.where(low, a[0], b[1]), jnp.where(low, -a[1], b[0])], axis=0).astype(bf16)
        for a, b in ((upper, lower), (lower, upper))
    )


def pack_retarded(first, second):
    row, column, _ = places(*first.shape)
    diagonal = jnp.sum(jnp.where(row == column, second, 0.0), axis=0, keepdims=True)
    return jnp.where(row <= column, first, second), jnp.broadcast_to(diagonal, (spare, first.shape[1]))


def unpack_retarded(packed, diagonal):
    packed, diagonal = packed.astype(f32), diagonal.astype(f32)
    extent, width = packed.shape
    row, column, _ = places(extent, width)
    turned = with_turned(packed)[1][:extent]
    return (
        jnp.where(row <= column, packed, turned),
        jnp.where(row > column, packed, jnp.where(row == column, diagonal, turned)),
    )


def write_message(ref, maps):
    extent = maps[0][-1].shape[0]
    for pair in range(ref.shape[0]):
        first, second = maps[2 * pair], maps[2 * pair + 1]
        shared, diagonal = pack_retarded(first[-2], second[-2])
        ref[pair, 0:extent] = shared.astype(bf16)
        ref[pair, extent : 2 * extent] = pack_lesser(first[-1], second[-1]).astype(bf16)
        ref[pair, 2 * extent : 2 * extent + spare] = diagonal.astype(bf16)
        if ref.shape[1] > 2 * extent + spare:
            ref[pair, 2 * extent + spare : 3 * extent + spare] = first[0].astype(bf16)
            ref[pair, 3 * extent + spare :] = second[0].astype(bf16)


def read_maps(ref):
    if len(ref.shape) == 4:
        return [read(ref, e) for e in range(ref.shape[0])]
    return read_message(ref)


def read_message(ref):
    extent = ref.shape[2] // 2
    maps = []
    for pair in range(ref.shape[0]):
        retarded = unpack_retarded(ref[pair, 0:extent], ref[pair, 2 * extent : 2 * extent + 1])
        lesser = unpack_lesser(ref[pair, extent : 2 * extent])
        for which in range(2):
            start = (2 + which) * extent + spare
            front = (ref[pair, start : start + extent],) if ref.shape[1] > 2 * extent + spare else ()
            maps.append(front + (retarded[which].astype(bf16), lesser[which].astype(bf16)))
    return maps


def pushed(step, state):
    first = dot_mat(step[0], jnp.concatenate([full(state[0]), full(state[1])], axis=1)).astype(bf16)
    width = step[0].shape[1]
    return (
        dot_last(first[:, :width], full_conj(step[0])),
        dot_last(first[:, width:], full(step[0])),
    )


def compose(earlier, latter):
    retarded, lesser = pushed(latter, earlier[1:])
    return (
        dot_mat(latter[0], full(earlier[0])),
        latter[1].astype(f32) + retarded,
        latter[2].astype(f32) + lesser,
    )


def pick(flag, yes, no):
    return tuple(jnp.where(flag, a, b) for a, b in zip(yes, no))


def neutral(extent, width):
    row = lax.broadcasted_iota(jnp.int32, (extent, width), 0)
    lane = lax.broadcasted_iota(jnp.int32, (extent, width), 1)
    zero = jnp.zeros((extent, width), f32)
    return (jnp.where(row == lane, 1.0, 0.0).astype(bf16), zero.astype(bf16), zero.astype(bf16))


def read(ref, e):
    return tuple(ref[e, part] for part in range(ref.shape[1]))


def upper_half(level):
    return jnp.bitwise_and(jnp.right_shift(lax.axis_index("cell"), level), 1) == 1


def join_kernel(level, total_ref, other_ref, message_ref, new_total_ref):
    upper = upper_half(level)
    others = read_maps(other_ref)
    joined = []
    for e in range(total_ref.shape[0]):
        total, other = read(total_ref, e), others[e]
        joined.append(compose(pick(upper, other, total), pick(upper, total, other)))
        for part in range(3):
            new_total_ref[e, part] = joined[e][part].astype(bf16)
    write_message(message_ref, joined)


def last_join_kernel(level, total_ref, other_ref, message_ref):
    upper = upper_half(level)
    extent = total_ref.shape[2]
    joined = []
    for pair in range(message_ref.shape[0]):
        fulls = (
            unpack_full_retarded(
                other_ref[pair, 0:extent], other_ref[pair, 2 * extent : 2 * extent + 1]
            ),
            unpack_full_lesser(other_ref[pair, extent : 2 * extent]),
        )
        for which in range(2):
            e = 2 * pair + which
            start = (2 + which) * extent + spare
            step = jnp.where(upper, total_ref[e, 0], other_ref[pair, start : start + extent])
            sums = []
            for part, turn in ((1, full_conj), (2, full)):
                other = fulls[part - 1][which]
                own = total_ref[e, part]
                before = jnp.where(upper, other, full(own))
                after = jnp.where(upper, own, other[:extent]).astype(f32)
                sums.append(after + dot_last(dot_mat(step, before).astype(bf16), turn(step)))
            joined.append(sums)
    write_message(message_ref, joined)


def enter_kernel(level, other_ref, *refs):
    upper = upper_half(level)
    others = read_maps(other_ref)
    out_ref = refs[-1]
    for e in range(out_ref.shape[0]):
        if level:
            old = read(refs[0], e)
            new = pick(upper, tuple(x.astype(bf16) for x in compose(others[e], old)), old)
        else:
            new = pick(upper, others[e], neutral(*out_ref.shape[2:]))
        for part in range(3):
            out_ref[e, part] = new[part]


def unpack_full_retarded(packed, diagonal):
    packed, diagonal = packed.astype(f32), diagonal.astype(f32)
    extent, width = packed.shape
    row, column, low = places(extent, width)
    square, turned = with_turned(packed)
    swapped_diagonal = swap_halves(jnp.broadcast_to(diagonal, (8, width)))[0:1]
    first = [jnp.where(row <= column, square[k : k + extent], turned[:extent] if k == 0 else turned[extent:]) for k in (0, extent)]
    second = [
        jnp.where(
            row > column,
            square[k : k + extent],
            jnp.where(row == column, diagonal if k == 0 else swapped_diagonal, turned[:extent] if k == 0 else turned[extent:]),
        )
        for k in (0, extent)
    ]
    return tuple(
        jnp.concatenate([top, jnp.where(low, -bottom, bottom)], axis=0).astype(bf16) for top, bottom in (first, second)
    )


def arrive_kernel(level, enter_ref, state_ref, retarded_ref, lesser_ref):
    upper = jnp.right_shift(lax.axis_index("cell"), level) == 1
    extent = enter_ref.shape[2]
    for pair in range(lesser_ref.shape[0]):
        both = unpack_full_lesser(state_ref[pair, extent : 2 * extent])
        lessers = []
        for e in (2 * pair, 2 * pair + 1):
            step = enter_ref[e, 0]
            state = jnp.where(upper, both[e % 2], jnp.zeros_like(both[0]))
            middle = dot_mat(step, state).astype(bf16)
            lessers.append(enter_ref[e, 2].astype(f32) + dot_last(middle, full(step)))
        lesser_ref[pair] = pack_lesser(*lessers).astype(bf16)
        both = unpack_full_retarded(state_ref[pair, 0:extent], state_ref[pair, 2 * extent : 2 * extent + 1])
        for e in (2 * pair, 2 * pair + 1):
            step = enter_ref[e, 0]
            state = jnp.where(upper, both[e % 2], jnp.zeros_like(both[0]))
            middle = dot_mat(step, state).astype(bf16)
            retarded_ref[e] = (enter_ref[e, 1].astype(f32) + dot_last(middle, full_conj(step))).astype(bf16)


def row_sums(x):
    return dot_last(jnp.ones((8, x.shape[1]), bf16), x.astype(bf16))[0:1]


def diagonal_kernel(overall, modes_ref, levels_ref, params_ref, out_ref, sums_ref):
    energies = params_ref.shape[2]
    first = lax.axis_index("energy") * energies
    modes = modes_ref[0].astype(f32)
    for e in range(energies):
        _, di = resolvents(overall, first, e, levels_ref, params_ref.at[0])
        out_ref[0, e : e + 1, :] = row_sums(modes * (modes * di).astype(bf16).astype(f32))
    blank = jnp.zeros(sums_ref.shape[2:], f32)
    for part in range(sums_ref.shape[0]):
        for e in range(sums_ref.shape[1]):
            sums_ref[part, e] = blank


def density_of(diagonal_ref, left_ref, retarded_ref, out_ref):
    for e in range(left_ref.shape[0]):
        left = left_ref[e]
        pz = dot_mat(left, full(retarded_ref[e])).astype(bf16).astype(f32)
        total = diagonal_ref[0, e : e + 1, :] + row_sums(pz * swap_halves(left.astype(f32)))
        out_ref[0, e : e + 1, :] = -total / math.pi


def convolve_kernel(reach, hop, last, offsets_ref, screen_ref, lesser_ref, left_ref, local_ref, _, *refs):
    if hop == 0:
        diagonal_ref, retarded_ref, *refs = refs
    sums_ref, *refs = refs
    if hop == 0:
        density_of(diagonal_ref, left_ref, retarded_ref, refs.pop(0))
    if last:
        out_hbm, *refs = refs
    g_ref, picked_ref, sem, *refs = refs
    copy = pltpu.make_async_copy(offsets_ref, picked_ref, sem)
    copy.start()
    energies = left_ref.shape[0]
    points, share, _ = screen_ref.shape[2:]
    overall = sums_ref.shape[1] - 2 * reach
    group = lax.axis_index("energy")
    mine = pl.multiple_of(group * share, share)
    base = jnp.bitwise_xor(group, hop) * energies + reach
    for pair in range(energies // 2):
        states = unpack_full_lesser(lesser_ref[pair])
        for e in (2 * pair, 2 * pair + 1):
            own = left_ref[e, pl.ds(mine, share), :]
            pl_hat = dot_mat(own, states[e - 2 * pair])
            turned = swap_halves(pl_hat) * signs(pl_hat.shape[1], 1.0)
            chain = dot_last(jnp.concatenate([pl_hat, turned], axis=0).astype(bf16), left_ref[e])
            re = chain[:share] + local_ref[e, 0].astype(f32)
            im = chain[share:] + local_ref[e, 1].astype(f32)
            g_ref[0, e] = re + im
            g_ref[1, e] = im
            g_ref[2, e] = re
    copy.wait()
    height = 16

    def out_copy(step):
        rows = pl.ds(pl.multiple_of(step * height, height), height)
        return pltpu.make_async_copy(
            refs[0].at[:, :, :, rows, :], out_hbm.at[:, :, :, rows, :], refs[1].at[step]
        )

    def rows_of(step, _):
        rows = pl.ds(pl.multiple_of(step * height, height), height)
        held = [[g_ref[part, e, rows, :] for part in range(3)] for e in range(energies)]
        for k in range(points):
            w_re = screen_ref[0, 0, k, rows, :].astype(f32)
            w_im = screen_ref[0, 1, k, rows, :].astype(f32)
            factors = (w_re, w_re + w_im, w_im - w_re)
            for e in range(energies):
                target = base + e + picked_ref[k]
                for part in range(3):
                    sums_ref[part, target, rows, :] += factors[part] * held[e][part]
        if last:
            for e in range(overall):
                common = sums_ref[0, reach + e, rows, :]
                refs[0][0, 0, e, rows, :] = (-(common + sums_ref[2, reach + e, rows, :])).astype(bf16)
                refs[0][0, 1, e, rows, :] = (common - sums_ref[1, reach + e, rows, :]).astype(bf16)
            out_copy(step).start()
        return 0

    steps = share // height
    lax.fori_loop(0, steps, rows_of, 0)
    if last:
        for step in range(steps):
            out_copy(step).wait()


def in_hbm(x):
    return pltpu.with_memory_space_constraint(x, pltpu.HBM)


def call(kernel, out_shape, in_specs, scratch=(), flops=1_000_000, size=1_000_000, out_specs=None, aliases={}):
    outs = out_specs or jax.tree.map(lambda _: VMEM, out_shape)
    return pl.pallas_call(
        kernel,
        out_shape=out_shape,
        in_specs=in_specs,
        out_specs=outs,
        scratch_shapes=list(scratch),
        input_output_aliases=aliases,
        compiler_params=pltpu.CompilerParams(vmem_limit_bytes=16 << 20),
        cost_estimate=pl.CostEstimate(flops=flops, bytes_accessed=size, transcendentals=0),
    )


def body(
    modes,
    levels,
    level_shift,
    broadening,
    injection,
    coupling,
    row_mask,
    interface,
    screened,
    offsets,
):
    cells = lax.axis_size("cell")
    groups = lax.axis_size("energy")
    rounds = cells.bit_length() - 1
    assert cells == 1 << rounds and rounds > 2 and groups & (groups - 1) == 0
    energies = level_shift.shape[1]
    overall = energies * groups
    orbitals, extent = coupling.shape[1:]
    width = 2 * extent
    share = orbitals // groups
    sds = jax.ShapeDtypeStruct

    def swapped(x, axis, distance):
        return lax.ppermute(x, axis, [(i, i ^ distance) for i in range(lax.axis_size(axis))])

    assert energies % 2 == 0
    pairs = energies // 2
    maps_shape = sds((energies, 3, extent, width), bf16)
    message = sds((pairs, 4 * extent + spare, width), bf16)
    state_message = sds((pairs, 2 * extent + spare, width), bf16)
    coupling = jnp.swapaxes(coupling, 1, 2)
    block = call(tile_kernel, sds((8, width), f32), [SMEM])(interface)
    one = swapped(block, "cell", 1)
    mate = [i + 1 if i % 2 else i - 1 for i in range(cells)]
    mate[0], mate[-1] = 0, cells - 1
    route = [(i * groups + g, mate[i] * groups + (g ^ int(mate[i] == i))) for i in range(cells) for g in range(groups)]
    two = lax.ppermute(block, ("cell", "energy"), route)

    mixed, modes, levels, params, offsets = call(
        front_kernel,
        (
            sds((extent, orbitals), f32),
            sds(modes.shape, bf16),
            sds(levels.shape, f32),
            sds((1, 3, energies, orbitals), f32),
            sds(offsets.shape, jnp.int32),
        ),
        [HBM] * 8,
        [
            pltpu.SMEM(row_mask.shape, jnp.int32),
            pltpu.VMEM(coupling.shape, bf16),
            pltpu.SemaphoreType.DMA((8,)),
        ],
    )(*map(in_hbm, (row_mask, modes, levels, coupling, level_shift, broadening, injection, offsets)))
    left_shape = sds((energies, orbitals, width), bf16)
    local_shape = sds((energies, 2, share, orbitals), bf16)
    params_shape = (3, energies, orbitals)
    left, local = call(partial(rows_kernel, overall, share, 0, 0), (left_shape, local_shape), [VMEM] * 4)(
        modes, levels, mixed, params
    )
    lefts, locals_ = [left], [local]

    total = call(partial(maps_kernel, overall), maps_shape, [VMEM] * 6)(one, two, modes, levels, params, mixed)
    sent = total
    reach = overall // 4
    sums_shape = sds((3, overall + 2 * reach, share, orbitals), f32)
    sigma_shape = sds((1, 2, overall, share, orbitals), bf16)
    density_shape = sds((1, energies, orbitals), f32)
    diagonal, sums = call(
        partial(diagonal_kernel, overall), (density_shape, sums_shape), [VMEM] * 3
    )(modes, levels, params)

    known = params
    while known.shape[0] < groups:
        count = known.shape[0]
        got = swapped(known, "energy", count)
        if 2 * count < groups:
            known = call(both_kernel, sds((2 * count,) + params_shape, f32), [VMEM] * 2)(known, got)
        for slot in range(count):
            left, local = call(
                partial(rows_kernel, overall, share, count + slot, slot), (left_shape, local_shape), [VMEM] * 4
            )(modes, levels, mixed, got)
            lefts.append(left)
            locals_.append(local)
        if 2 * count >= groups:
            break

    enter = None
    for level in range(rounds - 1):
        other = swapped(sent, "cell", 1 << level)
        if level < rounds - 2:
            kernel, outs = join_kernel, (message, maps_shape)
        else:
            kernel, outs = last_join_kernel, (state_message,)
        sent, *rest = call(partial(kernel, level), outs, [VMEM] * 2)(total, other)
        total = rest[0] if rest else None
        given = (other, enter) if level else (other,)
        enter = call(partial(enter_kernel, level), maps_shape, [VMEM] * len(given))(*given)
    state = swapped(sent, "cell", cells // 2)
    retarded, lesser = call(
        partial(arrive_kernel, rounds - 1),
        (sds((energies, extent, width), bf16), sds((pairs, extent, width), bf16)),
        [VMEM, VMEM],
    )(enter, state)

    lessers = [lesser]
    for hop in range(1, groups):
        lessers.append(swapped(lesser, "energy", hop))
    scratch = [
        pltpu.VMEM((3, energies, share, orbitals), f32),
        pltpu.SMEM(offsets.shape, jnp.int32),
        pltpu.SemaphoreType.DMA,
    ]
    order = [h ^ (h >> 1) for h in range(groups)]
    for hop in order:
        last = hop == order[-1]
        given = (offsets, screened, lessers[hop], lefts[hop], locals_[hop], sums)
        outs, specs, extra = (sums_shape,), (VMEM,), []
        if hop == 0:
            given += (diagonal, retarded)
            outs, specs = outs + (density_shape,), specs + (VMEM,)
        if last:
            outs, specs = outs + (sigma_shape,), specs + (HBM,)
            extra = [pltpu.VMEM(sigma_shape.shape, bf16), pltpu.SemaphoreType.DMA((share // 16,))]
        sums, *rest = call(
            partial(convolve_kernel, reach, hop, last),
            outs,
            [VMEM] * len(given),
            scratch + extra,
            out_specs=specs,
            aliases={5: 0},
        )(*given)
        if hop == 0:
            density = rest[0]
    sigma = rest[-1]
    return (density, sigma)


def solution(mesh):
    placed = (
        P("cell", None, None),
        P("cell", None),
        P("cell", "energy", None),
        P("cell", "energy", None),
        P("cell", "energy", None),
        P("cell", None, None),
        P("cell", None),
        P("cell"),
        P("cell", None, None, "energy", None),
        P(),
    )
    return jax.shard_map(
        body,
        mesh=mesh,
        in_specs=placed,
        out_specs=(P("cell", "energy", None), P("cell", None, None, "energy", None)),
        check_vma=False,
    )
```

```python
from functools import partial
import math

import jax
import jax.numpy as jnp
from jax import lax
from jax.experimental import pallas as pl
from jax.experimental.pallas import tpu as pltpu
from jax.sharding import PartitionSpec as P


broaden_base = 1.0
energy_low = -0.25
energy_span = 0.5
f32 = jnp.float32
bf16 = jnp.bfloat16

VMEM = pl.BlockSpec(memory_space=pltpu.VMEM)
SMEM = pl.BlockSpec(memory_space=pltpu.SMEM)
HBM = pl.BlockSpec(memory_space=pltpu.HBM)


def dot_last(a, b, precision=None):
    return lax.dot_general(
        a, b, (((1,), (1,)), ((), ())), precision=precision, preferred_element_type=f32
    )


def dot_mat(a, b):
    return lax.dot_general(a, b, (((1,), (0,)), ((), ())), preferred_element_type=f32)


def signs(width, left_sign):
    lane = lax.broadcasted_iota(jnp.int32, (1, width), 1)
    return jnp.where(lane < width // 2, left_sign, -left_sign).astype(f32)


def swap_halves(x):
    return pltpu.roll(x, x.shape[1] // 2, 1)


def full(x):
    x = x.astype(f32)
    return jnp.concatenate([x, swap_halves(x) * signs(x.shape[1], -1.0)], axis=0).astype(bf16)


def full_conj(x):
    x = x.astype(f32)
    return jnp.concatenate([x * signs(x.shape[1], 1.0), swap_halves(x)], axis=0).astype(bf16)


def resolvent(levels, shift, broad, index, overall):
    eps = energy_low + energy_span * (index.astype(f32) + 0.5) / overall
    detune = eps - levels - shift
    damping = broaden_base + broad
    inverse = 1.0 / (detune * detune + damping * damping)
    return detune * inverse, -damping * inverse


def masked_link(coupling_ref, mask_ref):
    _, rows = coupling_ref.shape[1:]
    count = mask_ref.shape[1]
    block = lax.broadcasted_iota(jnp.int32, (1, rows), 1) // (rows // count)
    keep = jnp.zeros((1, rows), f32)
    for index in range(count):
        keep = jnp.where(block == index, mask_ref[0, index].astype(f32), keep)
    return (coupling_ref[0].astype(f32) * keep).astype(bf16)


def resolvents(overall, first, e, levels_ref, params_ref):
    return resolvent(levels_ref[...], params_ref[0, e : e + 1, :], params_ref[1, e : e + 1, :], first + e, overall)


def both_scaled(x, dr, di, axis):
    return jnp.concatenate([x * dr, x * di], axis=axis).astype(bf16)


def maps_kernel(
    overall, one_ref, two_ref, modes_ref, levels_ref, params_ref, mixed_ref, out_ref
):
    energies = params_ref.shape[2]
    extent = out_ref.shape[2]
    first = lax.axis_index("energy") * energies
    odd = jnp.bitwise_and(lax.axis_index("cell"), 1) == 1
    block = jnp.max(jnp.where(odd, two_ref[...], one_ref[...])).astype(jnp.int32)
    chosen = pl.multiple_of(block * extent, extent)
    modes = modes_ref[0]
    rows = modes_ref[0, pl.ds(chosen, extent), :]
    rows_f = rows.astype(f32)
    none = jnp.zeros_like(rows)
    rows2 = jnp.concatenate(
        [jnp.concatenate([rows, none], axis=1), jnp.concatenate([none, rows], axis=1)], axis=0
    )
    mixed = mixed_ref[...]
    for e in range(energies):
        dr, di = resolvents(overall, first, e, levels_ref, params_ref.at[0])
        free = dot_last(both_scaled(rows_f, dr, di, 0), modes)
        re, im = free[:extent], free[extent:]
        weight = params_ref[0, 2, e : e + 1, :]
        weighted = jnp.concatenate([re * weight, im * weight], axis=1).astype(bf16)
        straight = jnp.concatenate([re, im], axis=1)
        turned = jnp.concatenate([-im, re], axis=1)
        out_ref[e, 0] = dot_last(rows, both_scaled(mixed, dr, di, 0)).astype(bf16)
        out_ref[e, 1] = dot_last(both_scaled(rows_f, dr, di, 1), rows2).astype(bf16)
        out_ref[e, 2] = dot_last(weighted, jnp.concatenate([straight, turned], axis=0).astype(bf16)).astype(bf16)


def rows_kernel(overall, share, hop, slot, modes_ref, levels_ref, mixed_ref, params_ref, left_ref, local_ref):
    energies = params_ref.shape[2]
    group = lax.axis_index("energy")
    first = jnp.bitwise_xor(group, hop) * energies
    modes = modes_ref[0]
    mixed = mixed_ref[...]
    mine = pl.multiple_of(group * share, share)
    rows_f = modes_ref[0, pl.ds(mine, share), :].astype(f32)
    given = [resolvents(overall, first, e, levels_ref, params_ref.at[slot]) for e in range(energies)]
    own = dot_last(jnp.concatenate([both_scaled(rows_f, dr, di, 0) for dr, di in given], axis=0), modes)
    weighted = [
        own[2 * share * e : 2 * share * (e + 1)] * params_ref[slot, 2, e : e + 1, :] for e in range(energies)
    ]
    back = dot_mat(jnp.concatenate(weighted, axis=0).astype(bf16), modes)
    parts = []
    for e, (dr, di) in enumerate(given):
        re = back[2 * share * e : 2 * share * e + share]
        im = back[2 * share * e + share : 2 * share * (e + 1)]
        parts += [re * dr + im * di, im * dr - re * di]
    local = dot_last(jnp.concatenate(parts, axis=0).astype(bf16), modes)
    for e, (dr, di) in enumerate(given):
        left_ref[e] = dot_last(modes, both_scaled(mixed, dr, di, 0)).astype(bf16)
        for part in range(2):
            start = (2 * e + part) * share
            local_ref[e, part] = local[start : start + share].astype(bf16)


def tile_kernel(interface_ref, block_ref):
    block_ref[...] = jnp.full(block_ref.shape, interface_ref[0].astype(f32))


def front_kernel(
    mask_hbm,
    modes_hbm,
    levels_hbm,
    coupling_hbm,
    shift_hbm,
    broad_hbm,
    inject_hbm,
    offsets_hbm,
    mixed_ref,
    modes_ref,
    levels_ref,
    params_ref,
    offsets_ref,
    mask_ref,
    coupling_ref,
    sems,
):
    copies = [
        pltpu.make_async_copy(source, target, sems.at[index])
        for index, (source, target) in enumerate(
            (
                (mask_hbm, mask_ref),
                (offsets_hbm, offsets_ref),
                (coupling_hbm, coupling_ref),
                (shift_hbm, params_ref.at[0, 0:1]),
                (broad_hbm, params_ref.at[0, 1:2]),
                (inject_hbm, params_ref.at[0, 2:3]),
                (levels_hbm, levels_ref),
                (modes_hbm, modes_ref),
            )
        )
    ]
    for copy in copies:
        copy.start()
    for copy in copies:
        copy.wait()
    mixed_ref[...] = dot_mat(masked_link(coupling_ref, mask_ref), modes_ref[0])


def both_kernel(had_ref, got_ref, both_ref):
    count = had_ref.shape[0]
    both_ref[0:count] = had_ref[...]
    both_ref[count:] = got_ref[...]


spare = 16


def places(extent, width):
    row = lax.broadcasted_iota(jnp.int32, (extent, width), 0)
    lane = lax.broadcasted_iota(jnp.int32, (extent, width), 1)
    return row, jnp.where(lane < extent, lane, lane - extent), lane < extent


def pack_lesser(first, second):
    _, _, low = places(*first.shape)
    return jnp.where(low, first + swap_halves(first), second + swap_halves(second))


def with_turned(x):
    square = jnp.concatenate([x, swap_halves(x)], axis=0)
    return square, square.T


def unpack_lesser(packed):
    packed = packed.astype(f32)
    extent, width = packed.shape
    _, _, low = places(extent, width)
    square, turned = with_turned(packed)
    total, change = 0.5 * (square + turned), 0.5 * (square - turned)
    return (
        jnp.where(low, total[:extent], change[extent:]),
        jnp.where(low, total[extent:], change[:extent]),
    )


def unpack_full_lesser(packed):
    packed = packed.astype(f32)
    extent, width = packed.shape
    _, _, low = places(extent, width)
    square, turned = with_turned(packed)
    total, change = 0.5 * (square + turned), 0.5 * (square - turned)
    upper, lower = (total[:extent], change[:extent]), (total[extent:], change[extent:])
    return tuple(
        jnp.concatenate([jnp.where(low, a[0], b[1]), jnp.where(low, -a[1], b[0])], axis=0).astype(bf16)
        for a, b in ((upper, lower), (lower, upper))
    )


def pack_retarded(first, second):
    row, column, _ = places(*first.shape)
    diagonal = jnp.sum(jnp.where(row == column, second, 0.0), axis=0, keepdims=True)
    return jnp.where(row <= column, first, second), jnp.broadcast_to(diagonal, (spare, first.shape[1]))


def unpack_retarded(packed, diagonal):
    packed, diagonal = packed.astype(f32), diagonal.astype(f32)
    extent, width = packed.shape
    row, column, _ = places(extent, width)
    turned = with_turned(packed)[1][:extent]
    return (
        jnp.where(row <= column, packed, turned),
        jnp.where(row > column, packed, jnp.where(row == column, diagonal, turned)),
    )


def write_message(ref, maps):
    extent = maps[0][-1].shape[0]
    for pair in range(ref.shape[0]):
        first, second = maps[2 * pair], maps[2 * pair + 1]
        shared, diagonal = pack_retarded(first[-2], second[-2])
        ref[pair, 0:extent] = shared.astype(bf16)
        ref[pair, extent : 2 * extent] = pack_lesser(first[-1], second[-1]).astype(bf16)
        ref[pair, 2 * extent : 2 * extent + spare] = diagonal.astype(bf16)
        if ref.shape[1] > 2 * extent + spare:
            ref[pair, 2 * extent + spare : 3 * extent + spare] = first[0].astype(bf16)
            ref[pair, 3 * extent + spare :] = second[0].astype(bf16)


def read_maps(ref):
    if len(ref.shape) == 4:
        return [read(ref, e) for e in range(ref.shape[0])]
    return read_message(ref)


def read_message(ref):
    extent = ref.shape[2] // 2
    maps = []
    for pair in range(ref.shape[0]):
        retarded = unpack_retarded(ref[pair, 0:extent], ref[pair, 2 * extent : 2 * extent + 1])
        lesser = unpack_lesser(ref[pair, extent : 2 * extent])
        for which in range(2):
            start = (2 + which) * extent + spare
            front = (ref[pair, start : start + extent],) if ref.shape[1] > 2 * extent + spare else ()
            maps.append(front + (retarded[which].astype(bf16), lesser[which].astype(bf16)))
    return maps


def pushed(step, state):
    first = dot_mat(step[0], jnp.concatenate([full(state[0]), full(state[1])], axis=1)).astype(bf16)
    width = step[0].shape[1]
    return (
        dot_last(first[:, :width], full_conj(step[0])),
        dot_last(first[:, width:], full(step[0])),
    )


def compose(earlier, latter):
    retarded, lesser = pushed(latter, earlier[1:])
    return (
        dot_mat(latter[0], full(earlier[0])),
        latter[1].astype(f32) + retarded,
        latter[2].astype(f32) + lesser,
    )


def pick(flag, yes, no):
    return tuple(jnp.where(flag, a, b) for a, b in zip(yes, no))


def neutral(extent, width):
    row = lax.broadcasted_iota(jnp.int32, (extent, width), 0)
    lane = lax.broadcasted_iota(jnp.int32, (extent, width), 1)
    zero = jnp.zeros((extent, width), f32)
    return (jnp.where(row == lane, 1.0, 0.0).astype(bf16), zero.astype(bf16), zero.astype(bf16))


def read(ref, e):
    return tuple(ref[e, part] for part in range(ref.shape[1]))


def upper_half(level):
    return jnp.bitwise_and(jnp.right_shift(lax.axis_index("cell"), level), 1) == 1


def join_kernel(level, total_ref, other_ref, message_ref, new_total_ref):
    upper = upper_half(level)
    others = read_maps(other_ref)
    joined = []
    for e in range(total_ref.shape[0]):
        total, other = read(total_ref, e), others[e]
        joined.append(compose(pick(upper, other, total), pick(upper, total, other)))
        for part in range(3):
            new_total_ref[e, part] = joined[e][part].astype(bf16)
    write_message(message_ref, joined)


def last_join_kernel(level, total_ref, other_ref, message_ref):
    upper = upper_half(level)
    extent = total_ref.shape[2]
    joined = []
    for pair in range(message_ref.shape[0]):
        fulls = (
            unpack_full_retarded(
                other_ref[pair, 0:extent], other_ref[pair, 2 * extent : 2 * extent + 1]
            ),
            unpack_full_lesser(other_ref[pair, extent : 2 * extent]),
        )
        for which in range(2):
            e = 2 * pair + which
            start = (2 + which) * extent + spare
            step = jnp.where(upper, total_ref[e, 0], other_ref[pair, start : start + extent])
            sums = []
            for part, turn in ((1, full_conj), (2, full)):
                other = fulls[part - 1][which]
                own = total_ref[e, part]
                before = jnp.where(upper, other, full(own))
                after = jnp.where(upper, own, other[:extent]).astype(f32)
                sums.append(after + dot_last(dot_mat(step, before).astype(bf16), turn(step)))
            joined.append(sums)
    write_message(message_ref, joined)


def enter_kernel(level, other_ref, *refs):
    upper = upper_half(level)
    others = read_maps(other_ref)
    out_ref = refs[-1]
    for e in range(out_ref.shape[0]):
        if level:
            old = read(refs[0], e)
            new = pick(upper, tuple(x.astype(bf16) for x in compose(others[e], old)), old)
        else:
            new = pick(upper, others[e], neutral(*out_ref.shape[2:]))
        for part in range(3):
            out_ref[e, part] = new[part]


def unpack_full_retarded(packed, diagonal):
    packed, diagonal = packed.astype(f32), diagonal.astype(f32)
    extent, width = packed.shape
    row, column, low = places(extent, width)
    square, turned = with_turned(packed)
    swapped_diagonal = swap_halves(jnp.broadcast_to(diagonal, (8, width)))[0:1]
    first = [jnp.where(row <= column, square[k : k + extent], turned[:extent] if k == 0 else turned[extent:]) for k in (0, extent)]
    second = [
        jnp.where(
            row > column,
            square[k : k + extent],
            jnp.where(row == column, diagonal if k == 0 else swapped_diagonal, turned[:extent] if k == 0 else turned[extent:]),
        )
        for k in (0, extent)
    ]
    return tuple(
        jnp.concatenate([top, jnp.where(low, -bottom, bottom)], axis=0).astype(bf16) for top, bottom in (first, second)
    )


def arrive_kernel(level, enter_ref, state_ref, retarded_ref, lesser_ref):
    upper = jnp.right_shift(lax.axis_index("cell"), level) == 1
    extent = enter_ref.shape[2]
    for pair in range(lesser_ref.shape[0]):
        both = unpack_full_lesser(state_ref[pair, extent : 2 * extent])
        lessers = []
        for e in (2 * pair, 2 * pair + 1):
            step = enter_ref[e, 0]
            state = jnp.where(upper, both[e % 2], jnp.zeros_like(both[0]))
            middle = dot_mat(step, state).astype(bf16)
            lessers.append(enter_ref[e, 2].astype(f32) + dot_last(middle, full(step)))
        lesser_ref[pair] = pack_lesser(*lessers).astype(bf16)
        both = unpack_full_retarded(state_ref[pair, 0:extent], state_ref[pair, 2 * extent : 2 * extent + 1])
        for e in (2 * pair, 2 * pair + 1):
            step = enter_ref[e, 0]
            state = jnp.where(upper, both[e % 2], jnp.zeros_like(both[0]))
            middle = dot_mat(step, state).astype(bf16)
            retarded_ref[e] = (enter_ref[e, 1].astype(f32) + dot_last(middle, full_conj(step))).astype(bf16)


def row_sums(x):
    return dot_last(jnp.ones((8, x.shape[1]), bf16), x.astype(bf16))[0:1]


def diagonal_kernel(overall, modes_ref, levels_ref, params_ref, out_ref, sums_ref):
    energies = params_ref.shape[2]
    first = lax.axis_index("energy") * energies
    modes = modes_ref[0].astype(f32)
    for e in range(energies):
        _, di = resolvents(overall, first, e, levels_ref, params_ref.at[0])
        out_ref[0, e : e + 1, :] = row_sums(modes * (modes * di).astype(bf16).astype(f32))
    blank = jnp.zeros(sums_ref.shape[2:], f32)
    for part in range(sums_ref.shape[0]):
        for e in range(sums_ref.shape[1]):
            sums_ref[part, e] = blank


def density_of(diagonal_ref, left_ref, retarded_ref, out_ref):
    for e in range(left_ref.shape[0]):
        left = left_ref[e]
        pz = dot_mat(left, full(retarded_ref[e])).astype(bf16).astype(f32)
        total = diagonal_ref[0, e : e + 1, :] + row_sums(pz * swap_halves(left.astype(f32)))
        out_ref[0, e : e + 1, :] = -total / math.pi


def convolve_kernel(reach, hop, last, offsets_ref, screen_ref, lesser_ref, left_ref, local_ref, _, *refs):
    if hop == 0:
        diagonal_ref, retarded_ref, *refs = refs
    sums_ref, *refs = refs
    if hop == 0:
        density_of(diagonal_ref, left_ref, retarded_ref, refs.pop(0))
    if last:
        out_hbm, *refs = refs
    g_ref, picked_ref, sem, *refs = refs
    copy = pltpu.make_async_copy(offsets_ref, picked_ref, sem)
    copy.start()
    energies = left_ref.shape[0]
    points, share, _ = screen_ref.shape[2:]
    overall = sums_ref.shape[1] - 2 * reach
    group = lax.axis_index("energy")
    mine = pl.multiple_of(group * share, share)
    base = jnp.bitwise_xor(group, hop) * energies + reach
    for pair in range(energies // 2):
        states = unpack_full_lesser(lesser_ref[pair])
        for e in (2 * pair, 2 * pair + 1):
            own = left_ref[e, pl.ds(mine, share), :]
            pl_hat = dot_mat(own, states[e - 2 * pair])
            turned = swap_halves(pl_hat) * signs(pl_hat.shape[1], 1.0)
            chain = dot_last(jnp.concatenate([pl_hat, turned], axis=0).astype(bf16), left_ref[e])
            re = chain[:share] + local_ref[e, 0].astype(f32)
            im = chain[share:] + local_ref[e, 1].astype(f32)
            g_ref[0, e] = re + im
            g_ref[1, e] = im
            g_ref[2, e] = re
    copy.wait()
    height = 16

    def out_copy(step, part):
        rows = pl.ds(pl.multiple_of(step * height, height), height)
        return pltpu.make_async_copy(
            refs[0].at[0, part, :, rows, :], out_hbm.at[0, part, :, rows, :], refs[1].at[step, part]
        )

    def rows_of(step, _):
        rows = pl.ds(pl.multiple_of(step * height, height), height)
        held = [[g_ref[part, e, rows, :] for part in range(3)] for e in range(energies)]
        for k in range(points):
            w_re = screen_ref[0, 0, k, rows, :].astype(f32)
            w_im = screen_ref[0, 1, k, rows, :].astype(f32)
            factors = (w_re, w_re + w_im, w_im - w_re)
            for e in range(energies):
                target = base + e + picked_ref[k]
                for part in range(3):
                    sums_ref[part, target, rows, :] += factors[part] * held[e][part]
        if last:
            for part, turned in ((0, 2), (1, 1)):
                for e in range(overall):
                    common, other = sums_ref[0, reach + e, rows, :], sums_ref[turned, reach + e, rows, :]
                    value = common - other if part else -(common + other)
                    refs[0][0, part, e, rows, :] = value.astype(bf16)
                out_copy(step, part).start()
        return 0

    steps = share // height
    lax.fori_loop(0, steps, rows_of, 0)
    if last:
        for step in range(steps):
            for part in range(2):
                out_copy(step, part).wait()


def in_hbm(x):
    return pltpu.with_memory_space_constraint(x, pltpu.HBM)


def call(kernel, out_shape, in_specs, scratch=(), flops=1_000_000, size=1_000_000, out_specs=None, aliases={}):
    outs = out_specs or jax.tree.map(lambda _: VMEM, out_shape)
    return pl.pallas_call(
        kernel,
        out_shape=out_shape,
        in_specs=in_specs,
        out_specs=outs,
        scratch_shapes=list(scratch),
        input_output_aliases=aliases,
        compiler_params=pltpu.CompilerParams(vmem_limit_bytes=16 << 20),
        cost_estimate=pl.CostEstimate(flops=flops, bytes_accessed=size, transcendentals=0),
    )


def body(
    modes,
    levels,
    level_shift,
    broadening,
    injection,
    coupling,
    row_mask,
    interface,
    screened,
    offsets,
):
    cells = lax.axis_size("cell")
    groups = lax.axis_size("energy")
    rounds = cells.bit_length() - 1
    assert cells == 1 << rounds and rounds > 2 and groups & (groups - 1) == 0
    energies = level_shift.shape[1]
    overall = energies * groups
    orbitals, extent = coupling.shape[1:]
    width = 2 * extent
    share = orbitals // groups
    sds = jax.ShapeDtypeStruct

    def swapped(x, axis, distance):
        return lax.ppermute(x, axis, [(i, i ^ distance) for i in range(lax.axis_size(axis))])

    assert energies % 2 == 0
    pairs = energies // 2
    maps_shape = sds((energies, 3, extent, width), bf16)
    message = sds((pairs, 4 * extent + spare, width), bf16)
    state_message = sds((pairs, 2 * extent + spare, width), bf16)
    coupling = jnp.swapaxes(coupling, 1, 2)
    block = call(tile_kernel, sds((8, width), f32), [SMEM])(interface)
    one = swapped(block, "cell", 1)
    mate = [i + 1 if i % 2 else i - 1 for i in range(cells)]
    mate[0], mate[-1] = 0, cells - 1
    route = [(i * groups + g, mate[i] * groups + (g ^ int(mate[i] == i))) for i in range(cells) for g in range(groups)]
    two = lax.ppermute(block, ("cell", "energy"), route)

    mixed, modes, levels, params, offsets = call(
        front_kernel,
        (
            sds((extent, orbitals), f32),
            sds(modes.shape, bf16),
            sds(levels.shape, f32),
            sds((1, 3, energies, orbitals), f32),
            sds(offsets.shape, jnp.int32),
        ),
        [HBM] * 8,
        [
            pltpu.SMEM(row_mask.shape, jnp.int32),
            pltpu.VMEM(coupling.shape, bf16),
            pltpu.SemaphoreType.DMA((8,)),
        ],
    )(*map(in_hbm, (row_mask, modes, levels, coupling, level_shift, broadening, injection, offsets)))
    left_shape = sds((energies, orbitals, width), bf16)
    local_shape = sds((energies, 2, share, orbitals), bf16)
    params_shape = (3, energies, orbitals)
    left, local = call(partial(rows_kernel, overall, share, 0, 0), (left_shape, local_shape), [VMEM] * 4)(
        modes, levels, mixed, params
    )
    lefts, locals_ = [left], [local]

    total = call(partial(maps_kernel, overall), maps_shape, [VMEM] * 6)(one, two, modes, levels, params, mixed)
    sent = total
    reach = overall // 4
    sums_shape = sds((3, overall + 2 * reach, share, orbitals), f32)
    sigma_shape = sds((1, 2, overall, share, orbitals), bf16)
    density_shape = sds((1, energies, orbitals), f32)
    diagonal, sums = call(
        partial(diagonal_kernel, overall), (density_shape, sums_shape), [VMEM] * 3
    )(modes, levels, params)

    known = params
    while known.shape[0] < groups:
        count = known.shape[0]
        got = swapped(known, "energy", count)
        if 2 * count < groups:
            known = call(both_kernel, sds((2 * count,) + params_shape, f32), [VMEM] * 2)(known, got)
        for slot in range(count):
            left, local = call(
                partial(rows_kernel, overall, share, count + slot, slot), (left_shape, local_shape), [VMEM] * 4
            )(modes, levels, mixed, got)
            lefts.append(left)
            locals_.append(local)
        if 2 * count >= groups:
            break

    enter = None
    for level in range(rounds - 1):
        other = swapped(sent, "cell", 1 << level)
        if level < rounds - 2:
            kernel, outs = join_kernel, (message, maps_shape)
        else:
            kernel, outs = last_join_kernel, (state_message,)
        sent, *rest = call(partial(kernel, level), outs, [VMEM] * 2)(total, other)
        total = rest[0] if rest else None
        given = (other, enter) if level else (other,)
        enter = call(partial(enter_kernel, level), maps_shape, [VMEM] * len(given))(*given)
    state = swapped(sent, "cell", cells // 2)
    retarded, lesser = call(
        partial(arrive_kernel, rounds - 1),
        (sds((energies, extent, width), bf16), sds((pairs, extent, width), bf16)),
        [VMEM, VMEM],
    )(enter, state)

    lessers = [lesser]
    for hop in range(1, groups):
        lessers.append(swapped(lesser, "energy", hop))
    scratch = [
        pltpu.VMEM((3, energies, share, orbitals), f32),
        pltpu.SMEM(offsets.shape, jnp.int32),
        pltpu.SemaphoreType.DMA,
    ]
    order = [h ^ (h >> 1) for h in range(groups)]
    for hop in order:
        last = hop == order[-1]
        given = (offsets, screened, lessers[hop], lefts[hop], locals_[hop], sums)
        outs, specs, extra = (sums_shape,), (VMEM,), []
        if hop == 0:
            given += (diagonal, retarded)
            outs, specs = outs + (density_shape,), specs + (VMEM,)
        if last:
            outs, specs = outs + (sigma_shape,), specs + (HBM,)
            extra = [pltpu.VMEM(sigma_shape.shape, bf16), pltpu.SemaphoreType.DMA((share // 16, 2))]
        sums, *rest = call(
            partial(convolve_kernel, reach, hop, last),
            outs,
            [VMEM] * len(given),
            scratch + extra,
            out_specs=specs,
            aliases={5: 0},
        )(*given)
        if hop == 0:
            density = rest[0]
    sigma = rest[-1]
    return (density, sigma)


def solution(mesh):
    placed = (
        P("cell", None, None),
        P("cell", None),
        P("cell", "energy", None),
        P("cell", "energy", None),
        P("cell", "energy", None),
        P("cell", None, None),
        P("cell", None),
        P("cell"),
        P("cell", None, None, "energy", None),
        P(),
    )
    return jax.shard_map(
        body,
        mesh=mesh,
        in_specs=placed,
        out_specs=(P("cell", "energy", None), P("cell", None, None, "energy", None)),
        check_vma=False,
    )
```
